32 devices in a mesh: groups: 2 (over y), chan: 4 (over z), tm: 2 (over x), src: 2 (over core).
Axes of the slice: x: 2, y: 2, z: 4, core: 2. Of those that a mesh axis runs over, the one named last changes fastest.
Arguments:
- record: float32 [8192, 512], P(('groups', 'chan', 'src'), 'tm'), parts along dimension 0, may hold values from -6 to 6
- fir_taps: float32 [4, 128], replicated, may hold values from -0.5 to 0.5
- chan_table: int32 [4096], P(('chan', 'src')), may hold values from 0 to 3
- steering: bfloat16 [32, 256, 128], P(('chan', 'src')), may hold values from -0.375 to 0.375
- pair_block: int32 [64], P(('chan', 'src')), may hold values from 0 to 3
- pair_owner: int32 [64, 1], P(('chan', 'src')), may hold values from 0 to 7; in each aligned block of 8 rows (0 to 7, 8 to 15, ...) at most 2 rows name the same one
- pair_sub: int32 [64], P(('chan', 'src')), may hold values from 0 to 3
- pair_delay: int32 [64], P(('chan', 'src')), may hold values from 1 to 254
- pair_frac: int32 [64], P(('chan', 'src')), may hold values from 0 to 15
Outputs:
- beam: float32 [16384, 512], P(('groups', 'chan', 'src'), 'tm'), parts along dimension 0
The draws below stay inside these ranges and needn't reach their ends.
There are 2 independent parts, one for each index of `groups`. The reference program is written for one: setup_inputs(seed, part) draws one part's arguments, and reference() takes and returns one part's arrays. A program takes and returns all parts, laid end to end along the dimension named above; an argument that names none is the same for every part. Nothing has to cross between parts.
Inputs may be any that keep to these rules, and one draw needn't show every extreme that they name: `pair_owner`: in the rows of one device (aligned blocks of 8 rows) no owner is named more than 2 times, and in every draw some owner is named exactly 2 times in some such block; every owner is named somewhere.
All inputs are finite; a program needn't handle non-finite values.
Results may differ from the reference program's by a relative error of at most 0.0029.
Values may be sent and summed in bfloat16 or wider, within the bound.
A program may use at most 128 MiB of HBM per device.

```python
import math
import jax
import jax.numpy as jnp
import numpy as np
from jax import lax

CHANNEL_PER_BLK = 128
POINTS_PER_BLOCK = 256
TAPS = 128
WINDOW_SAMPLES = 512
NTAB = 4
NFRAC = 16
CB_DEV = 4
SOURCE_BLK_OWNED = 4
PAIR_LIMIT = 2
SEGMENT_SAMPLES = 256
PAIRS_DEV = 8
CHANNELS = 4096
SOURCE_BLOCKS = 32
PAIRS = 64
N_CHAN = 4
N_SRC = 2


def with_ends(entries, stream_key, low, high):
    dims = entries.shape
    spot = [jax.random.randint(jax.random.fold_in(stream_key, axis), (), 0, dims[axis]) for axis in range(len(dims))]
    entries = entries.at[tuple(spot)].set(low)
    longest = dims.index(max(dims))
    spot[longest] = (spot[longest] + 1) % dims[longest]
    return entries.at[tuple(spot)].set(high)


def block_scale(own_key, shape, shards, low, top_value):
    loudness, own = 1.0, jax.random.fold_in(own_key, 6)
    for dim, shards_of in shards:
        draws = jnp.exp(jax.random.uniform(jax.random.fold_in(own, dim), (shards_of,), jnp.float32, low / len(shards), top_value / len(shards)))
        loudness = loudness * jnp.repeat(draws, shape[dim] // shards_of).reshape([-1 if axis == dim else 1 for axis in range(len(shape))])
    return loudness


def assign_block(stream_key, own, number, rows, count, top, limit, skew):
    sequence = jax.random.permutation(stream_key, count)
    heavy_load, common = load_shares(count, rows * top, limit, skew, True), load_shares(count, rows * top, limit, skew, False)
    places = jnp.arange(count)

    def named(tallies, rotation):
        used = int((tallies > 0).sum())
        fixed = max(1, used // 4)
        moved = fixed + (places - fixed + rotation * (used - fixed)) % max(1, count - fixed)
        return jnp.zeros((count,), jnp.int32).at[sequence[jnp.where(places < fixed, places, moved)]].set(jnp.asarray(tallies, jnp.int32))

    tallies = jnp.where(number % 4 == 0, named(heavy_load, number // 4), named(common, number - number // 4 - 1))
    mixed = jax.random.permutation(jax.random.fold_in(own, 3), count)
    giver, taker = mixed[0:count // 2 * 2:2], mixed[1:count // 2 * 2:2]
    margin = jnp.minimum(tallies[giver] - 1, limit - tallies[taker]) // 2
    margin = jnp.where((giver == sequence[0]) | (taker == sequence[0]) | (tallies[taker] == 0), 0, jnp.maximum(margin, 0))
    moved = jax.random.randint(jax.random.fold_in(own, 4), (count // 2,), 0, 1 << 20) % (margin + 1)
    tallies = tallies.at[giver].add(-moved).at[taker].add(moved)
    members = jnp.searchsorted(jnp.cumsum(tallies), jnp.arange(rows * top), side="right").astype(jnp.int32)
    grid = members.reshape(top, rows).T
    grid = grid[jax.random.permutation(jax.random.fold_in(own, 1), rows)]
    rotation = jax.random.randint(jax.random.fold_in(own, 2), (rows, 1), 0, top)
    return jnp.take_along_axis(grid, (jnp.arange(top)[None, :] + rotation) % top, axis=1)


def load_shares(count, total, most, lean, full):
    loads = [(1 << 20) // math.isqrt(standing ** lean) + 1 for standing in range(1, count + 1)]
    largest = most if full else min(most, max(-(-total // count), total * loads[0] // sum(loads)))
    least = 1 if total - largest >= count - 1 else 0
    holding, surplus = [largest] + [least] * (count - 1), total - largest - least * (count - 1)
    while surplus > 0:
        movable = [i for i in range(1, count) if holding[i] < largest] or [i for i in range(1, count) if holding[i] < most]
        mass, remaining = sum([loads[i] for i in movable]), surplus
        for i in movable:
            more = min(most - holding[i], max(1, remaining * loads[i] // mass), surplus)
            holding[i] = holding[i] + more
            surplus = surplus - more
    return np.array(holding)


def bell_draw(own_key, dims, scale, bound, pieces=(), kind=jnp.bfloat16):
    entries = scale * jax.random.normal(own_key, dims, jnp.float32)
    if pieces:
        entries = entries * block_scale(own_key, dims, pieces, -0.22, 0.18)
    return jnp.clip(entries, -bound, bound).astype(kind)


def setup_inputs(seed: int = 0, part: int = 0) -> dict:
    seeds = jax.random.split(jax.random.key(seed), 10)
    part_keys = jax.random.split(jax.random.fold_in(seeds[9], part), 10)
    record = bell_draw(part_keys[0], (CHANNELS, WINDOW_SAMPLES), 1.0, 6.0, ((0, 8), (1, 2)), jnp.float32)
    fir_taps = bell_draw(seeds[1], (NTAB, TAPS), TAPS ** -0.5, 0.5, (), jnp.float32)
    chan_table = with_ends(jax.random.randint(seeds[2], (CHANNELS,), 0, NTAB), jax.random.fold_in(seeds[2], 1), 0, NTAB - 1).astype(jnp.int32)
    steering = bell_draw(seeds[3], (SOURCE_BLOCKS, POINTS_PER_BLOCK, CHANNEL_PER_BLK), (CHANNEL_PER_BLK * PAIR_LIMIT * N_CHAN * N_SRC // (2 * SOURCE_BLK_OWNED)) ** -0.5, 0.375, ((0, 8),))
    pair_block = with_ends(jax.random.randint(seeds[4], (PAIRS,), 0, CB_DEV), jax.random.fold_in(seeds[4], 1), 0, CB_DEV - 1).astype(jnp.int32)
    pair_owner_keys = jax.random.split(jax.random.fold_in(seeds[5], 1), PAIRS // PAIRS_DEV)
    pair_owner_turns = jax.random.permutation(jax.random.fold_in(seeds[5], 3), PAIRS // PAIRS_DEV)
    pair_owner = jax.vmap(lambda own, number: assign_block(jax.random.fold_in(seeds[5], 2), own, number, PAIRS_DEV, N_CHAN * N_SRC, 1, PAIR_LIMIT, 2))(pair_owner_keys, pair_owner_turns).reshape((PAIRS, 1))
    pair_sub = with_ends(jax.random.randint(seeds[6], (PAIRS,), 0, SOURCE_BLK_OWNED), jax.random.fold_in(seeds[6], 1), 0, SOURCE_BLK_OWNED - 1).astype(jnp.int32)
    pair_delay = with_ends(jax.random.randint(seeds[7], (PAIRS,), 1, SEGMENT_SAMPLES - 1), jax.random.fold_in(seeds[7], 1), 1, (SEGMENT_SAMPLES - 1) - 1).astype(jnp.int32)
    pair_frac = with_ends(jax.random.randint(seeds[8], (PAIRS,), 0, NFRAC), jax.random.fold_in(seeds[8], 1), 0, NFRAC - 1).astype(jnp.int32)
    return {"record": record, "fir_taps": fir_taps, "chan_table": chan_table, "steering": steering, "pair_block": pair_block, "pair_owner": pair_owner, "pair_sub": pair_sub, "pair_delay": pair_delay, "pair_frac": pair_frac}


def lagrange(position):
    first = -position * (position - 1.0) * (position - 2.0) / 6.0
    second = (position + 1.0) * (position - 1.0) * (position - 2.0) / 2.0
    third = -(position + 1.0) * position * (position - 2.0) / 2.0
    fourth = (position + 1.0) * position * (position - 1.0) / 6.0
    return jnp.stack([first, second, third, fourth], axis=-1)


def reference(record, fir_taps, chan_table, steering, pair_block, pair_owner, pair_sub, pair_delay, pair_frac):
    channel_list = record.shape[0]
    select = (chan_table[:, None] == jnp.arange(NTAB, dtype=jnp.int32)[None, :]).astype(jnp.float32)
    chan_taps = jnp.dot(select, fir_taps, precision=lax.Precision.HIGHEST)
    padded = jnp.pad(record, ((0, 0), (TAPS - 1, 0)))

    def add_tap(step, total):
        column = lax.dynamic_slice_in_dim(chan_taps, step, 1, 1)
        window = lax.dynamic_slice_in_dim(padded, TAPS - 1 - step, WINDOW_SAMPLES, 1)
        return total + column * window

    filtered_trace = lax.fori_loop(0, TAPS, add_tap, jnp.zeros((channel_list, WINDOW_SAMPLES), jnp.float32))
    extended_trace = jnp.pad(filtered_trace, ((0, 0), (0, SEGMENT_SAMPLES))).reshape(channel_list // CHANNEL_PER_BLK, CHANNEL_PER_BLK, WINDOW_SAMPLES + SEGMENT_SAMPLES)
    weights = lagrange(pair_frac.astype(jnp.float32) / NFRAC)
    pair_count = pair_block.shape[0]
    lister = jnp.arange(pair_count, dtype=jnp.int32) // PAIRS_DEV
    chan_block = (lister * CB_DEV + pair_block).astype(jnp.int32)
    source_block = (pair_owner[:, 0] * SOURCE_BLK_OWNED + pair_sub).astype(jnp.int32)

    def accumulate_pair(stacked_sums, index):
        rows = extended_trace[chan_block[index]]
        window = lax.dynamic_slice_in_dim(rows, (pair_delay[index] - 1).astype(jnp.int32), WINDOW_SAMPLES + 3, 1)
        weight = weights[index]
        mixed = weight[0] * window[:, 0:WINDOW_SAMPLES] + weight[1] * window[:, 1:WINDOW_SAMPLES + 1]
        mixed = mixed + weight[2] * window[:, 2:WINDOW_SAMPLES + 2] + weight[3] * window[:, 3:WINDOW_SAMPLES + 3]
        rounded = lax.optimization_barrier(mixed.astype(jnp.bfloat16)).astype(jnp.float32)
        return stacked_sums.at[source_block[index]].add(rounded), None

    block_count = steering.shape[0]
    stacked_sums, unused_value = lax.scan(accumulate_pair, jnp.zeros((block_count, CHANNEL_PER_BLK, WINDOW_SAMPLES), jnp.float32), jnp.arange(pair_count, dtype=jnp.int32))
    beam = jnp.einsum("bxc,bct->bxt", steering.astype(jnp.float32), stacked_sums, precision=lax.Precision.HIGHEST)
    return beam.reshape(block_count * POINTS_PER_BLOCK, WINDOW_SAMPLES)
```

```python
import functools

import jax
import jax.numpy as jnp
from jax import lax
from jax.experimental import pallas as pl
from jax.experimental.pallas import tpu as pltpu
from jax.sharding import PartitionSpec as P

NFRAC = 16
GROUPS = 4
PARTS = 8
LAG = 3
MESH = pl.DeviceIdType.MESH


def split(value):
    high = value.astype(jnp.bfloat16)
    return high, (value - high.astype(jnp.float32)).astype(jnp.bfloat16)


def mm(a, b):
    return jnp.dot(a, b, preferred_element_type=jnp.float32)


def kernel(
    dims,
    block_ref,
    owner_ref,
    sub_ref,
    delay_ref,
    frac_ref,
    record,
    taps_ref,
    table_ref,
    steer_ref,
    beam_ref,
    prev,
    after,
    band_hi,
    band_lo,
    tab,
    filt,
    shifted,
    out_slots,
    in_slots,
    out_label,
    in_label,
    sums,
    slot_pair,
    prev_send,
    prev_recv,
    after_send,
    after_recv,
    slot_send,
    slot_recv,
    label_send,
    label_recv,
):
    nchan, nsrc, ntm = dims
    owners = nchan * nsrc
    blocks, block_rows, seg = record.shape
    ntab, ntaps = taps_ref.shape
    pairs = block_ref.shape[0]
    cap = out_slots.shape[1]
    targets = steer_ref.shape[0]
    points = steer_ref.shape[1]
    step_rows = block_rows // GROUPS
    rows = blocks * step_rows
    me = lax.axis_index("chan") * nsrc + lax.axis_index("src")
    tm = lax.axis_index("tm")

    def place(owner):
        return {"chan": owner // nsrc, "src": owner % nsrc}

    barrier = pltpu.get_barrier_semaphore()

    @pl.when(tm > 0)
    def _():
        pl.semaphore_signal(barrier, inc=1, device_id={"tm": tm - 1}, device_id_type=MESH)

    @pl.when(tm < ntm - 1)
    def _():
        pl.semaphore_signal(barrier, inc=1, device_id={"tm": tm + 1}, device_id_type=MESH)

    def greet(i, carry):
        pl.semaphore_signal(
            barrier, inc=1, device_id=place((me + i) % owners), device_id_type=MESH
        )
        return carry

    lax.fori_loop(1, owners, greet, 0)

    build_band(taps_ref, band_hi, band_lo)

    @pl.when(tm == 0)
    def _():
        prev[...] = jnp.zeros_like(prev)

    @pl.when(tm == ntm - 1)
    def _():
        after[...] = jnp.zeros_like(after)

    pl.semaphore_wait(
        barrier,
        owners - 1 + jnp.where(tm > 0, 1, 0) + jnp.where(tm < ntm - 1, 1, 0),
    )

    def part(r):
        return pl.ds(pl.multiple_of(r * step_rows, step_rows), step_rows)

    def to_prev(r):
        return pltpu.make_async_remote_copy(
            src_ref=record.at[:, part(r), pl.ds(seg - ntaps, ntaps)],
            dst_ref=prev.at[:, part(r), :],
            send_sem=prev_send.at[r],
            recv_sem=prev_recv.at[r],
            device_id={"tm": tm + 1},
            device_id_type=MESH,
        )

    def to_after(r):
        return pltpu.make_async_remote_copy(
            src_ref=record.at[:, part(r), :],
            dst_ref=after.at[:, part(r), :],
            send_sem=after_send.at[r],
            recv_sem=after_recv.at[r],
            device_id={"tm": tm - 1},
            device_id_type=MESH,
        )

    def slots_to(r, other, landing):
        return pltpu.make_async_remote_copy(
            src_ref=out_slots.at[other, :, part(r), :],
            dst_ref=in_slots.at[landing, :, part(r), :],
            send_sem=slot_send.at[r, other],
            recv_sem=slot_recv.at[r, landing],
            device_id=place(other),
            device_id_type=MESH,
        )

    def label_to(other, landing):
        return pltpu.make_async_remote_copy(
            src_ref=out_label.at[other],
            dst_ref=in_label.at[landing],
            send_sem=label_send.at[other],
            recv_sem=label_recv.at[landing],
            device_id=place(other),
            device_id_type=MESH,
        )

    for r in range(GROUPS):

        @pl.when(tm > 0)
        def _():
            to_after(r).start()

        @pl.when(tm < ntm - 1)
        def _():
            to_prev(r).start()

    for g in range(blocks):
        tab[g] = jnp.broadcast_to(table_ref[g : g + 1, :], (block_rows, block_rows)).T

    def slots_of(owner, carry):
        def look(p, found):
            hit = owner_ref[p] == owner
            count = found[0]
            named = [
                jnp.where(jnp.logical_and(hit, count == k), p, found[1 + k]) for k in range(cap)
            ]
            return (count + jnp.where(hit, 1, 0), *named)

        found = lax.fori_loop(0, pairs, look, (0,) + (-1,) * cap, unroll=min(pairs, 8))
        line = lax.broadcasted_iota(jnp.int32, out_label.shape[1:], 0)
        labels = jnp.full(out_label.shape[1:], -1.0, jnp.float32)
        for k in range(cap):
            pair = jnp.maximum(found[1 + k], 0)
            slot_pair[owner * cap + k] = pair
            name = jnp.where(found[1 + k] >= 0, sub_ref[pair], -1).astype(jnp.float32)
            labels = jnp.where(line == k, name, labels)
        out_label[owner] = labels
        return carry

    lax.fori_loop(0, owners, slots_of, 0)

    def send_label(i, carry):
        label_to((me + i) % owners, me).start()
        return carry

    lax.fori_loop(1, owners, send_label, 0)

    def produce(r, carry):
        @pl.when(tm > 0)
        def _():
            to_prev(r).wait_recv()

        @pl.when(tm < ntm - 1)
        def _():
            to_after(r).wait_recv()

        window = jnp.concatenate(
            [
                prev[:, part(r), :].reshape(rows, ntaps),
                record[:, part(r), :].reshape(rows, seg),
                after[:, part(r), :].reshape(rows, seg),
            ],
            axis=1,
        )
        inside = jnp.where(tm < ntm - 1, 1.0, 0.0)
        which = tab[:, part(r), :].reshape(rows, block_rows)
        band_filter(window, band_hi, band_lo, which, inside, seg, ntab, filt)

        def one_pair(p, c):
            shifted[p] = shift_pair(filt[block_ref[p]], delay_ref[p], frac_ref[p], seg)
            return c

        lax.fori_loop(0, pairs, one_pair, 0, unroll=min(pairs, 4))

        def ship(i, c):
            other = (me + owners // 2 + i) % owners
            for k in range(cap):
                out_slots[other, k, part(r), :] = shifted[slot_pair[other * cap + k]]

            @pl.when(other != me)
            def _():
                slots_to(r, other, me).start()

            return c

        lax.fori_loop(0, owners, ship, 0)
        return carry

    lax.fori_loop(0, GROUPS, produce, 0)

    def wait_label(i, carry):
        source = (me + i) % owners
        label_to(source, source).wait_recv()
        return carry

    lax.fori_loop(1, owners, wait_label, 0)

    def add(total, values, labels):
        for k in range(cap):
            name = jnp.concatenate([labels[k : k + 1, :]] * (seg // labels.shape[1]), axis=1)
            value = values[k].astype(jnp.float32)
            total = [
                total[b] + value * jnp.where(name == float(b), 1.0, 0.0) for b in range(targets)
            ]
        return total

    def gather(r, carry):
        total = [jnp.zeros((step_rows, seg), jnp.float32)] * targets
        total = add(total, out_slots[me, :, part(r), :], out_label[me])

        def one_source(i, running):
            source = (me + i) % owners
            slots_to(r, source, source).wait_recv()
            return tuple(add(list(running), in_slots[source, :, part(r), :], in_label[source]))

        total = lax.fori_loop(1, owners, one_source, tuple(total))
        for b in range(targets):
            sums[b, part(r), :] = total[b]
        return carry

    lax.fori_loop(0, GROUPS, gather, 0)

    for b in range(targets):
        high, low = split(sums[b])
        beam_ref[b * points : (b + 1) * points, :] = mm(steer_ref[b], high) + mm(steer_ref[b], low)

    def finish(i, carry):
        other = (me + i) % owners
        label_to(other, me).wait_send()
        for r in range(GROUPS):
            slots_to(r, other, me).wait_send()
        return carry

    lax.fori_loop(1, owners, finish, 0)
    for r in range(GROUPS):

        @pl.when(tm > 0)
        def _():
            to_after(r).wait_send()

        @pl.when(tm < ntm - 1)
        def _():
            to_prev(r).wait_send()


def copy_to(source, target, send, receive, place):
    return pltpu.make_async_remote_copy(
        src_ref=source,
        dst_ref=target,
        send_sem=send,
        recv_sem=receive,
        device_id=place,
        device_id_type=MESH,
    )


def line_kernel(
    dims,
    block_ref,
    owner_ref,
    sub_ref,
    delay_ref,
    frac_ref,
    record,
    taps_ref,
    table_ref,
    sums,
    prev_out,
    prev_in,
    after_out,
    after_in,
    band_hi,
    band_lo,
    tab,
    weight,
    filt,
    shifted,
    out_pairs,
    in_pairs,
    out_slots,
    in_slots,
    out_name,
    in_name,
    out_label,
    in_label,
    pick,
    out_local,
    in_local,
    out_dense,
    in_dense,
    prev_send,
    prev_recv,
    after_send,
    after_recv,
    pair_send,
    pair_recv,
    slot_send,
    slot_recv,
    name_send,
    name_recv,
    label_send,
    label_recv,
    local_send,
    local_recv,
    dense_send,
    dense_recv,
):
    nchan, nsrc, ntm = dims
    blocks, block_rows, seg = record.shape
    ntab, ntaps = taps_ref.shape
    pairs = block_ref.shape[0]
    cap = out_slots.shape[2]
    targets = sums.shape[0]
    half = seg // nsrc
    step_rows = block_rows // PARTS
    rows = blocks * step_rows
    chip = lax.axis_index("chan")
    core = lax.axis_index("src")
    mate = 1 - core
    tm = lax.axis_index("tm")
    middle = jnp.logical_and(chip > 0, chip < nchan - 1)
    ending = jnp.logical_or(chip == 0, chip == nchan - 1)
    low_half = chip < nchan // 2
    outer = jnp.where(low_half, 0, nchan - 1)
    inner = jnp.where(low_half, 1, nchan - 2)
    other = nchan - 1 - inner
    far = nchan - 1 - outer

    barrier = pltpu.get_barrier_semaphore()

    def greet(place):
        pl.semaphore_signal(barrier, inc=1, device_id=place, device_id_type=MESH)

    @pl.when(tm > 0)
    def _():
        greet({"tm": tm - 1})

    @pl.when(tm < ntm - 1)
    def _():
        greet({"tm": tm + 1})

    greet({"src": mate})
    for k in range(nsrc):
        greet({"chan": other, "src": k})

    @pl.when(middle)
    def _():
        for k in range(nsrc):
            greet({"chan": outer, "src": k})

    @pl.when(ending)
    def _():
        for k in range(nsrc):
            greet({"chan": inner, "src": k})

    def part(r):
        return pl.ds(pl.multiple_of(r * step_rows, step_rows), step_rows)

    @pl.when(tm > 0)
    def _():
        for r in range(PARTS):
            after_out[r] = record[:, part(r), :].astype(jnp.bfloat16)

    @pl.when(tm < ntm - 1)
    def _():
        for r in range(PARTS):
            prev_out[r] = record[:, part(r), seg - ntaps :].astype(jnp.bfloat16)

    @pl.when(tm == 0)
    def _():
        prev_in[...] = jnp.zeros_like(prev_in)

    @pl.when(tm == ntm - 1)
    def _():
        after_in[...] = jnp.zeros_like(after_in)

    lanes = out_name.shape[1]
    lane = lax.broadcasted_iota(jnp.int32, out_name.shape, 1)
    own_name = jnp.zeros(out_name.shape, jnp.int32)
    for p in range(pairs):
        own_name = jnp.where(lane // step_rows == p, owner_ref[p] * targets + sub_ref[p], own_name)
    out_name[...] = own_name.astype(jnp.float32)
    slot_pair = []
    for k in range(nsrc):
        owner = outer * nsrc + k
        count = 0
        found = [-1] * cap
        for p in range(pairs):
            hit = owner_ref[p] == owner
            found = [jnp.where(jnp.logical_and(hit, count == j), p, found[j]) for j in range(cap)]
            count = count + jnp.where(hit, 1, 0)
        labels = jnp.full(out_name.shape, -1, jnp.int32)
        for j in range(cap):
            pair = jnp.maximum(found[j], 0)
            slot_pair.append(pair)
            name = jnp.where(found[j] >= 0, sub_ref[pair], -1)
            labels = jnp.where(lane // step_rows % cap == j, name, labels)
        out_label[k] = labels.astype(jnp.float32)

    build_band(taps_ref, band_hi, band_lo)

    pl.semaphore_wait(
        barrier,
        jnp.where(middle, 7, 3) + jnp.where(tm > 0, 1, 0) + jnp.where(tm < ntm - 1, 1, 0),
    )

    def to_prev(r):
        return copy_to(
            prev_out.at[r], prev_in.at[r], prev_send.at[r], prev_recv.at[r], {"tm": tm + 1}
        )

    def to_after(r):
        return copy_to(
            after_out.at[r], after_in.at[r], after_send.at[r], after_recv.at[r], {"tm": tm - 1}
        )

    def pairs_to(k, r, landing, place):
        return copy_to(
            out_pairs.at[r, k],
            in_pairs.at[landing, r],
            pair_send.at[k, r],
            pair_recv.at[landing, r],
            place,
        )

    def slots_to(k, r, landing, place):
        return copy_to(
            out_slots.at[r, k],
            in_slots.at[landing, r],
            slot_send.at[k, r],
            slot_recv.at[landing, r],
            place,
        )

    def name_to(k, landing, place):
        return copy_to(
            out_name, in_name.at[landing], name_send.at[k], name_recv.at[landing], place
        )

    def label_to(k, landing, place):
        return copy_to(
            out_label.at[k], in_label.at[landing], label_send.at[k], label_recv.at[landing], place
        )

    def local_to(r):
        return copy_to(
            out_local.at[r, mate], in_local.at[r], local_send.at[r], local_recv.at[r], {"src": mate}
        )

    def dense_to(k, r, landing):
        return copy_to(
            out_dense.at[r, k],
            in_dense.at[landing, r],
            dense_send.at[k, r],
            dense_recv.at[landing, r],
            {"chan": far if k < nsrc else other, "src": k % nsrc},
        )

    at_mate = {"src": mate}

    def at_inner(k):
        return {"chan": inner, "src": k}

    def at_outer(k):
        return {"chan": outer, "src": k}

    for r in range(PARTS):

        @pl.when(tm > 0)
        def _():
            to_after(r).start()

        @pl.when(tm < ntm - 1)
        def _():
            to_prev(r).start()

    @pl.when(middle)
    def _():
        name_to(0, 0, at_mate).start()
        for k in range(nsrc):
            label_to(k, 1 + core, at_outer(k)).start()

    @pl.when(ending)
    def _():
        for k in range(nsrc):
            name_to(k, 1 + core, at_inner(k)).start()
        label_to(mate, 0, at_mate).start()

    for g in range(blocks):
        tab[g] = jnp.broadcast_to(table_ref[g : g + 1, :], (block_rows, block_rows)).T
    for p in range(pairs):
        for k, value in enumerate(lagrange(frac_ref[p], lanes)):
            weight[p * 4 + k : p * 4 + k + 1, :] = value

    def produce(r):
        @pl.when(tm > 0)
        def _():
            to_prev(r).wait_recv()

        @pl.when(tm < ntm - 1)
        def _():
            to_after(r).wait_recv()

        inside = jnp.where(tm < ntm - 1, 1.0, 0.0)
        high, low = split(record[:, part(r), :].reshape(rows, seg))
        before = prev_in[r].reshape(rows, ntaps)
        behind = after_in[r].reshape(rows, seg)
        window = jnp.concatenate([before, high, behind], axis=1)
        rest = jnp.concatenate(
            [jnp.zeros_like(before), low, jnp.zeros((rows, ntaps), jnp.bfloat16)], axis=1
        )
        steps = 2 * seg // ntaps
        near = seg // ntaps + 1
        lhs_hi = jnp.concatenate(
            [window[:, j * ntaps : (j + 2) * ntaps] for j in range(steps)], axis=0
        )
        lhs_lo = jnp.concatenate(
            [rest[:, j * ntaps : (j + 2) * ntaps] for j in range(near)], axis=0
        )
        every = mm(lhs_hi, band_lo[...]) + mm(lhs_hi, band_hi[...])
        fine = mm(lhs_lo, band_hi[...])
        which = tab[:, part(r), :].reshape(rows, block_rows)
        pieces = []
        for j in range(steps):
            own = every[j * rows : (j + 1) * rows]
            if j < near:
                own = own + fine[j * rows : (j + 1) * rows]
            value = own[:, :ntaps]
            for m in range(1, ntab):
                value = jnp.where(which == m, own[:, m * ntaps : (m + 1) * ntaps], value)
            if j >= seg // ntaps:
                value = value * inside
            pieces.append(value)
        whole = jnp.concatenate(pieces, axis=1)
        for k in range(4):
            moved = whole if k == 0 else pltpu.roll(whole, 2 * seg - k, 1)
            filt[k] = moved.reshape(blocks, step_rows, 2 * seg)

        def one_pair(p, c):
            source = block_ref[p]
            mixed = []
            for j in range(2 * seg // lanes):
                cols = slice(j * lanes, (j + 1) * lanes)
                total = weight[pl.ds(p * 4, 1), :] * filt[0, source, :, cols]
                for k in range(1, 4):
                    total = total + weight[pl.ds(p * 4 + k, 1), :] * filt[k, source, :, cols]
                mixed.append(total)
            moved = pltpu.roll(
                jnp.concatenate(mixed, axis=1), 2 * seg - (delay_ref[p] - 1), 1
            )[:, :seg].astype(jnp.bfloat16)
            shifted[p] = moved
            for k in range(nsrc):
                out_pairs[r, k, p] = moved[:, k * half : (k + 1) * half]
            return c

        lax.fori_loop(0, pairs, one_pair, 0, unroll=min(pairs, 4))

        @pl.when(ending)
        def _():
            for k in range(nsrc):
                pairs_to(k, r, 1 + core, at_inner(k)).start()

        @pl.when(middle)
        def _():
            pairs_to(mate, r, 0, at_mate).start()

        for k in range(nsrc):
            for j in range(cap):
                out_slots[r, k, j] = shifted[slot_pair[k * cap + j]]

        @pl.when(ending)
        def _():
            slots_to(mate, r, 0, at_mate).start()

        @pl.when(middle)
        def _():
            for k in range(nsrc):
                slots_to(k, r, 1 + core, at_outer(k)).start()

    def dense(r):
        pairs_to(0, r, 0, at_mate).wait_recv()
        for k in range(nsrc):
            pairs_to(0, r, 1 + k, at_outer(k)).wait_recv()
        depth = pairs * step_rows
        values = jnp.concatenate(
            [out_pairs[r, core].reshape(depth, half)]
            + [in_pairs[k, r].reshape(depth, half) for k in range(1 + nsrc)],
            axis=0,
        )
        total = mm(pick[...], values).reshape(3 * nsrc, targets, step_rows, half)
        for k in range(2 * nsrc):
            out_dense[r, k] = total[k].astype(jnp.bfloat16)
            dense_to(k, r, core).start()
        for k in range(nsrc):
            out_local[r, k] = total[2 * nsrc + k]
        local_to(r).start()

    unit = pairs * step_rows
    spot = lax.broadcasted_iota(jnp.int32, (unit, unit), 0)
    line = lax.broadcasted_iota(jnp.int32, (unit, unit), 1)
    diagonal = spot % step_rows == line % step_rows

    @pl.when(middle)
    def _():
        name_to(0, 0, at_mate).wait_recv()
        for k in range(nsrc):
            name_to(0, 1 + k, at_outer(k)).wait_recv()
        for i, chan in enumerate((far, other, chip)):
            wanted = (chan * nsrc * targets + spot // step_rows).astype(jnp.float32)
            for kind in range(2 + nsrc):
                names = out_name[0:1, :] if kind == 0 else in_name[kind - 1, 0:1, :]
                hit = jnp.logical_and(wanted == names, diagonal)
                pick[i * unit : (i + 1) * unit, kind * unit : (kind + 1) * unit] = jnp.where(
                    hit, 1.0, 0.0
                ).astype(jnp.bfloat16)

    @pl.when(ending)
    def _():
        label_to(mate, 0, at_mate).wait_recv()
        for k in range(nsrc):
            label_to(k, 1 + k, at_inner(k)).wait_recv()
        names = out_label[core, 0:1, :]
        for kind in range(1, 2 + nsrc):
            names = jnp.where(
                lane[0:1, :] // (cap * step_rows) == kind, in_label[kind - 1, 0:1, :], names
            )
        wanted = (spot // step_rows).astype(jnp.float32)
        hit = jnp.logical_and(wanted == names, diagonal)
        pick[:unit, :unit] = jnp.where(hit, 1.0, 0.0).astype(jnp.bfloat16)

    def produce_step(i, carry):
        @pl.when(i < PARTS)
        def _():
            produce(i)

        @pl.when(jnp.logical_and(middle, i >= LAG))
        def _():
            dense(i - LAG)

        return carry

    lax.fori_loop(0, PARTS + LAG, produce_step, 0)

    def store(r, b, value):
        high, low = split(value)
        sums[b, part(r), :] = high
        sums[b, pl.ds(pl.multiple_of(block_rows + r * step_rows, step_rows), step_rows), :] = low

    def finish(r, carry):
        @pl.when(ending)
        def _():
            slots_to(mate, r, 0, at_mate).wait_recv()
            for k in range(nsrc):
                slots_to(k, r, 1 + k, at_inner(k)).wait_recv()
            depth = cap * step_rows
            values = jnp.concatenate(
                [out_slots[r, core].reshape(depth, seg)]
                + [in_slots[k, r].reshape(depth, seg) for k in range(1 + nsrc)],
                axis=0,
            )
            total = mm(pick[: targets * step_rows, :unit], values)
            for k in range(nsrc):
                dense_to(0, r, k).wait_recv()
            for b in range(targets):
                added = jnp.concatenate([in_dense[k, r, b] for k in range(nsrc)], axis=1)
                store(
                    r, b, total[b * step_rows : (b + 1) * step_rows] + added.astype(jnp.float32)
                )

        @pl.when(middle)
        def _():
            local_to(r).wait_recv()
            for k in range(nsrc):
                dense_to(0, r, k).wait_recv()
            for b in range(targets):
                mine, theirs = out_local[r, core, b], in_local[r, b]
                total = jnp.concatenate(
                    [jnp.where(core == k, mine, theirs) for k in range(nsrc)], axis=1
                )
                added = jnp.concatenate([in_dense[k, r, b] for k in range(nsrc)], axis=1)
                store(r, b, total + added.astype(jnp.float32))

        return carry

    lax.fori_loop(0, PARTS, finish, 0)

    @pl.when(middle)
    def _():
        name_to(0, 0, at_mate).wait_send()
        for k in range(nsrc):
            label_to(k, 1 + core, at_outer(k)).wait_send()

    @pl.when(ending)
    def _():
        for k in range(nsrc):
            name_to(k, 1 + core, at_inner(k)).wait_send()
        label_to(mate, 0, at_mate).wait_send()

    def leave(r, carry):
        @pl.when(tm > 0)
        def _():
            to_after(r).wait_send()

        @pl.when(tm < ntm - 1)
        def _():
            to_prev(r).wait_send()

        @pl.when(ending)
        def _():
            for k in range(nsrc):
                pairs_to(k, r, 1 + core, at_inner(k)).wait_send()
            slots_to(mate, r, 0, at_mate).wait_send()

        @pl.when(middle)
        def _():
            pairs_to(mate, r, 0, at_mate).wait_send()
            for k in range(nsrc):
                slots_to(k, r, 1 + core, at_outer(k)).wait_send()
            for k in range(2 * nsrc):
                dense_to(k, r, core).wait_send()
            local_to(r).wait_send()

        return carry

    lax.fori_loop(0, PARTS, leave, 0)


def lagrange(frac, width):
    mu = jnp.full((1, width), frac.astype(jnp.float32)) / NFRAC
    return (
        -mu * (mu - 1.0) * (mu - 2.0) / 6.0,
        (mu + 1.0) * (mu - 1.0) * (mu - 2.0) / 2.0,
        -(mu + 1.0) * mu * (mu - 2.0) / 2.0,
        (mu + 1.0) * mu * (mu - 1.0) / 6.0,
    )


def steer_kernel(steer_ref, sums, beam_ref):
    for b in range(sums.shape[0]):
        points = steer_ref.shape[1]
        twice = jnp.concatenate([steer_ref[b], steer_ref[b]], axis=1)
        beam_ref[b * points : (b + 1) * points, :] = mm(twice, sums[b])


def build_band(taps_ref, band_hi, band_lo):
    ntab, ntaps = taps_ref.shape
    for m in range(ntab):
        row = jnp.concatenate([taps_ref[m : m + 1, :], jnp.zeros((1, ntaps), jnp.float32)], axis=1)
        full = jnp.broadcast_to(row, (2 * ntaps, 2 * ntaps))
        rolled = pltpu.roll(full, ntaps, 1, stride=1, stride_axis=0)[:, :ntaps]
        high, low = split(rolled)
        band_hi[:, m * ntaps : (m + 1) * ntaps] = high
        band_lo[:, m * ntaps : (m + 1) * ntaps] = low


def band_filter(window, band_hi, band_lo, which, inside, seg, ntab, filt):
    blocks, step_rows, _ = filt.shape
    rows = blocks * step_rows
    ntaps = band_hi.shape[0] // 2
    high, low = split(window)
    steps = 2 * seg // ntaps
    lhs_hi = jnp.concatenate([high[:, j * ntaps : (j + 2) * ntaps] for j in range(steps)], axis=0)
    lhs_lo = jnp.concatenate([low[:, j * ntaps : (j + 2) * ntaps] for j in range(steps)], axis=0)
    every = mm(lhs_lo, band_hi[...]) + mm(lhs_hi, band_lo[...]) + mm(lhs_hi, band_hi[...])
    for j in range(steps):
        own = every[j * rows : (j + 1) * rows]
        value = own[:, :ntaps]
        for m in range(1, ntab):
            value = jnp.where(which == m, own[:, m * ntaps : (m + 1) * ntaps], value)
        if j >= seg // ntaps:
            value = value * inside
        filt[:, :, j * ntaps : (j + 1) * ntaps] = value.reshape(blocks, step_rows, ntaps)


def shift_pair(source, delay, frac, seg):
    mu = jnp.full((1, seg), frac.astype(jnp.float32)) / NFRAC
    first = -mu * (mu - 1.0) * (mu - 2.0) / 6.0
    second = (mu + 1.0) * (mu - 1.0) * (mu - 2.0) / 2.0
    third = -(mu + 1.0) * mu * (mu - 2.0) / 2.0
    fourth = (mu + 1.0) * mu * (mu - 1.0) / 6.0
    base = pltpu.roll(source, 2 * seg - (delay - 1), 1)
    mixed = first * base[:, :seg]
    mixed = mixed + second * pltpu.roll(base, 2 * seg - 1, 1)[:, :seg]
    mixed = mixed + third * pltpu.roll(base, 2 * seg - 2, 1)[:, :seg]
    mixed = mixed + fourth * pltpu.roll(base, 2 * seg - 3, 1)[:, :seg]
    return mixed.astype(jnp.bfloat16)


def solution(mesh):
    nchan, nsrc, ntm = mesh.shape["chan"], mesh.shape["src"], mesh.shape["tm"]
    owners = nchan * nsrc

    def local(
        record, fir_taps, chan_table, steering, pair_block, pair_owner, pair_sub, pair_delay, pair_frac
    ):
        channels, seg = record.shape
        ntab, ntaps = fir_taps.shape
        targets, points, block_rows = steering.shape
        blocks = channels // block_rows
        pairs = pair_block.shape[0]
        cap = 2 * pairs // owners
        step_rows = block_rows // GROUPS
        smem = pl.BlockSpec(memory_space=pltpu.SMEM)
        vmem = pl.BlockSpec(memory_space=pltpu.VMEM)
        dma = pltpu.SemaphoreType.DMA
        operands = (
            pair_block,
            pair_owner.reshape(pairs),
            pair_sub,
            pair_delay,
            pair_frac,
            record.reshape(blocks, block_rows, seg),
            fir_taps,
            chan_table.reshape(blocks, block_rows),
            steering,
        )
        unit = pairs * block_rows // PARTS
        square = unit == 128 and pairs == nsrc * targets and cap * (2 + nsrc) == pairs
        if nchan == 4 and nsrc == 2 and square:
            step_rows = block_rows // PARTS
            half = seg // nsrc
            kinds = 1 + nsrc
            bf16, f32 = jnp.bfloat16, jnp.float32
            sums = pl.pallas_call(
                functools.partial(line_kernel, (nchan, nsrc, ntm)),
                out_shape=jax.ShapeDtypeStruct((targets, 2 * block_rows, seg), bf16),
                in_specs=[smem] * 5 + [vmem] * 3,
                out_specs=vmem,
                scratch_shapes=[
                    pltpu.VMEM((PARTS, blocks, step_rows, ntaps), bf16),
                    pltpu.VMEM((PARTS, blocks, step_rows, ntaps), bf16),
                    pltpu.VMEM((PARTS, blocks, step_rows, seg), bf16),
                    pltpu.VMEM((PARTS, blocks, step_rows, seg), bf16),
                    pltpu.VMEM((2 * ntaps, ntab * ntaps), bf16),
                    pltpu.VMEM((2 * ntaps, ntab * ntaps), bf16),
                    pltpu.VMEM((blocks, block_rows, block_rows), jnp.int32),
                    pltpu.VMEM((pairs * 4, 128), f32),
                    pltpu.VMEM((4, blocks, step_rows, 2 * seg), f32),
                    pltpu.VMEM((pairs, step_rows, seg), bf16),
                    pltpu.VMEM((PARTS, nsrc, pairs, step_rows, half), bf16),
                    pltpu.VMEM((kinds, PARTS, pairs, step_rows, half), bf16),
                    pltpu.VMEM((PARTS, nsrc, cap, step_rows, seg), bf16),
                    pltpu.VMEM((kinds, PARTS, cap, step_rows, seg), bf16),
                    pltpu.VMEM((8, 128), f32),
                    pltpu.VMEM((kinds, 8, 128), f32),
                    pltpu.VMEM((nsrc, 8, 128), f32),
                    pltpu.VMEM((kinds, 8, 128), f32),
                    pltpu.VMEM((3 * unit, (1 + kinds) * unit), bf16),
                    pltpu.VMEM((PARTS, nsrc, targets, step_rows, half), f32),
                    pltpu.VMEM((PARTS, targets, step_rows, half), f32),
                    pltpu.VMEM((PARTS, 2 * nsrc, targets, step_rows, half), bf16),
                    pltpu.VMEM((nsrc, PARTS, targets, step_rows, half), bf16),
                    dma((PARTS,)),
                    dma((PARTS,)),
                    dma((PARTS,)),
                    dma((PARTS,)),
                    dma((nsrc, PARTS)),
                    dma((kinds, PARTS)),
                    dma((nsrc, PARTS)),
                    dma((kinds, PARTS)),
                    dma((nsrc,)),
                    dma((kinds,)),
                    dma((nsrc,)),
                    dma((kinds,)),
                    dma((PARTS,)),
                    dma((PARTS,)),
                    dma((2 * nsrc, PARTS)),
                    dma((nsrc, PARTS)),
                ],
                compiler_params=pltpu.CompilerParams(collective_id=0, has_side_effects=True),
            )(*operands[:-1])
            return pl.pallas_call(
                steer_kernel,
                out_shape=jax.ShapeDtypeStruct((targets * points, seg), f32),
                in_specs=[vmem] * 2,
                out_specs=vmem,
            )(steering, sums)
        return pl.pallas_call(
            functools.partial(kernel, (nchan, nsrc, ntm)),
            out_shape=jax.ShapeDtypeStruct((targets * points, seg), jnp.float32),
            in_specs=[smem] * 5 + [vmem] * 4,
            out_specs=vmem,
            scratch_shapes=[
                pltpu.VMEM((blocks, block_rows, ntaps), jnp.float32),
                pltpu.VMEM((blocks, block_rows, seg), jnp.float32),
                pltpu.VMEM((2 * ntaps, ntab * ntaps), jnp.bfloat16),
                pltpu.VMEM((2 * ntaps, ntab * ntaps), jnp.bfloat16),
                pltpu.VMEM((blocks, block_rows, block_rows), jnp.int32),
                pltpu.VMEM((blocks, step_rows, 2 * seg), jnp.float32),
                pltpu.VMEM((pairs, step_rows, seg), jnp.bfloat16),
                pltpu.VMEM((owners, cap, block_rows, seg), jnp.bfloat16),
                pltpu.VMEM((owners, cap, block_rows, seg), jnp.bfloat16),
                pltpu.VMEM((owners, 8, 128), jnp.float32),
                pltpu.VMEM((owners, 8, 128), jnp.float32),
                pltpu.VMEM((targets, block_rows, seg), jnp.float32),
                pltpu.SMEM((owners * cap,), jnp.int32),
                dma((GROUPS,)),
                dma((GROUPS,)),
                dma((GROUPS,)),
                dma((GROUPS,)),
                dma((GROUPS, owners)),
                dma((GROUPS, owners)),
                dma((owners,)),
                dma((owners,)),
            ],
            compiler_params=pltpu.CompilerParams(collective_id=0, has_side_effects=True),
        )(*operands)

    in_specs = (
        P(("groups", "chan", "src"), "tm"),
        P(),
        P(("chan", "src")),
        P(("chan", "src"), None, None),
        P(("chan", "src")),
        P(("chan", "src"), None),
        P(("chan", "src")),
        P(("chan", "src")),
        P(("chan", "src")),
    )
    out_specs = P(("groups", "chan", "src"), "tm")
    return jax.shard_map(local, mesh=mesh, in_specs=in_specs, out_specs=out_specs, check_vma=False)
```

```python
import functools

import jax
import jax.numpy as jnp
from jax import lax
from jax.experimental import pallas as pl
from jax.experimental.pallas import tpu as pltpu
from jax.sharding import PartitionSpec as P

NFRAC = 16
GROUPS = 4
PARTS = 8
LAG = 3
MESH = pl.DeviceIdType.MESH


def split(value):
    high = value.astype(jnp.bfloat16)
    return high, (value - high.astype(jnp.float32)).astype(jnp.bfloat16)


def mm(a, b):
    return jnp.dot(a, b, preferred_element_type=jnp.float32)


def kernel(
    dims,
    block_ref,
    owner_ref,
    sub_ref,
    delay_ref,
    frac_ref,
    record,
    taps_ref,
    table_ref,
    steer_ref,
    beam_ref,
    prev,
    after,
    band_hi,
    band_lo,
    tab,
    filt,
    shifted,
    out_slots,
    in_slots,
    out_label,
    in_label,
    sums,
    slot_pair,
    prev_send,
    prev_recv,
    after_send,
    after_recv,
    slot_send,
    slot_recv,
    label_send,
    label_recv,
):
    nchan, nsrc, ntm = dims
    owners = nchan * nsrc
    blocks, block_rows, seg = record.shape
    ntab, ntaps = taps_ref.shape
    pairs = block_ref.shape[0]
    cap = out_slots.shape[1]
    targets = steer_ref.shape[0]
    points = steer_ref.shape[1]
    step_rows = block_rows // GROUPS
    rows = blocks * step_rows
    me = lax.axis_index("chan") * nsrc + lax.axis_index("src")
    tm = lax.axis_index("tm")

    def place(owner):
        return {"chan": owner // nsrc, "src": owner % nsrc}

    barrier = pltpu.get_barrier_semaphore()

    @pl.when(tm > 0)
    def _():
        pl.semaphore_signal(barrier, inc=1, device_id={"tm": tm - 1}, device_id_type=MESH)

    @pl.when(tm < ntm - 1)
    def _():
        pl.semaphore_signal(barrier, inc=1, device_id={"tm": tm + 1}, device_id_type=MESH)

    def greet(i, carry):
        pl.semaphore_signal(
            barrier, inc=1, device_id=place((me + i) % owners), device_id_type=MESH
        )
        return carry

    lax.fori_loop(1, owners, greet, 0)

    build_band(taps_ref, band_hi, band_lo)

    @pl.when(tm == 0)
    def _():
        prev[...] = jnp.zeros_like(prev)

    @pl.when(tm == ntm - 1)
    def _():
        after[...] = jnp.zeros_like(after)

    pl.semaphore_wait(
        barrier,
        owners - 1 + jnp.where(tm > 0, 1, 0) + jnp.where(tm < ntm - 1, 1, 0),
    )

    def part(r):
        return pl.ds(pl.multiple_of(r * step_rows, step_rows), step_rows)

    def to_prev(r):
        return pltpu.make_async_remote_copy(
            src_ref=record.at[:, part(r), pl.ds(seg - ntaps, ntaps)],
            dst_ref=prev.at[:, part(r), :],
            send_sem=prev_send.at[r],
            recv_sem=prev_recv.at[r],
            device_id={"tm": tm + 1},
            device_id_type=MESH,
        )

    def to_after(r):
        return pltpu.make_async_remote_copy(
            src_ref=record.at[:, part(r), :],
            dst_ref=after.at[:, part(r), :],
            send_sem=after_send.at[r],
            recv_sem=after_recv.at[r],
            device_id={"tm": tm - 1},
            device_id_type=MESH,
        )

    def slots_to(r, other, landing):
        return pltpu.make_async_remote_copy(
            src_ref=out_slots.at[other, :, part(r), :],
            dst_ref=in_slots.at[landing, :, part(r), :],
            send_sem=slot_send.at[r, other],
            recv_sem=slot_recv.at[r, landing],
            device_id=place(other),
            device_id_type=MESH,
        )

    def label_to(other, landing):
        return pltpu.make_async_remote_copy(
            src_ref=out_label.at[other],
            dst_ref=in_label.at[landing],
            send_sem=label_send.at[other],
            recv_sem=label_recv.at[landing],
            device_id=place(other),
            device_id_type=MESH,
        )

    for r in range(GROUPS):

        @pl.when(tm > 0)
        def _():
            to_after(r).start()

        @pl.when(tm < ntm - 1)
        def _():
            to_prev(r).start()

    for g in range(blocks):
        tab[g] = jnp.broadcast_to(table_ref[g : g + 1, :], (block_rows, block_rows)).T

    def slots_of(owner, carry):
        def look(p, found):
            hit = owner_ref[p] == owner
            count = found[0]
            named = [
                jnp.where(jnp.logical_and(hit, count == k), p, found[1 + k]) for k in range(cap)
            ]
            return (count + jnp.where(hit, 1, 0), *named)

        found = lax.fori_loop(0, pairs, look, (0,) + (-1,) * cap, unroll=min(pairs, 8))
        line = lax.broadcasted_iota(jnp.int32, out_label.shape[1:], 0)
        labels = jnp.full(out_label.shape[1:], -1.0, jnp.float32)
        for k in range(cap):
            pair = jnp.maximum(found[1 + k], 0)
            slot_pair[owner * cap + k] = pair
            name = jnp.where(found[1 + k] >= 0, sub_ref[pair], -1).astype(jnp.float32)
            labels = jnp.where(line == k, name, labels)
        out_label[owner] = labels
        return carry

    lax.fori_loop(0, owners, slots_of, 0)

    def send_label(i, carry):
        label_to((me + i) % owners, me).start()
        return carry

    lax.fori_loop(1, owners, send_label, 0)

    def produce(r, carry):
        @pl.when(tm > 0)
        def _():
            to_prev(r).wait_recv()

        @pl.when(tm < ntm - 1)
        def _():
            to_after(r).wait_recv()

        window = jnp.concatenate(
            [
                prev[:, part(r), :].reshape(rows, ntaps),
                record[:, part(r), :].reshape(rows, seg),
                after[:, part(r), :].reshape(rows, seg),
            ],
            axis=1,
        )
        inside = jnp.where(tm < ntm - 1, 1.0, 0.0)
        which = tab[:, part(r), :].reshape(rows, block_rows)
        band_filter(window, band_hi, band_lo, which, inside, seg, ntab, filt)

        def one_pair(p, c):
            shifted[p] = shift_pair(filt[block_ref[p]], delay_ref[p], frac_ref[p], seg)
            return c

        lax.fori_loop(0, pairs, one_pair, 0, unroll=min(pairs, 4))

        def ship(i, c):
            other = (me + owners // 2 + i) % owners
            for k in range(cap):
                out_slots[other, k, part(r), :] = shifted[slot_pair[other * cap + k]]

            @pl.when(other != me)
            def _():
                slots_to(r, other, me).start()

            return c

        lax.fori_loop(0, owners, ship, 0)
        return carry

    lax.fori_loop(0, GROUPS, produce, 0)

    def wait_label(i, carry):
        source = (me + i) % owners
        label_to(source, source).wait_recv()
        return carry

    lax.fori_loop(1, owners, wait_label, 0)

    def add(total, values, labels):
        for k in range(cap):
            name = jnp.concatenate([labels[k : k + 1, :]] * (seg // labels.shape[1]), axis=1)
            value = values[k].astype(jnp.float32)
            total = [
                total[b] + value * jnp.where(name == float(b), 1.0, 0.0) for b in range(targets)
            ]
        return total

    def gather(r, carry):
        total = [jnp.zeros((step_rows, seg), jnp.float32)] * targets
        total = add(total, out_slots[me, :, part(r), :], out_label[me])

        def one_source(i, running):
            source = (me + i) % owners
            slots_to(r, source, source).wait_recv()
            return tuple(add(list(running), in_slots[source, :, part(r), :], in_label[source]))

        total = lax.fori_loop(1, owners, one_source, tuple(total))
        for b in range(targets):
            sums[b, part(r), :] = total[b]
        return carry

    lax.fori_loop(0, GROUPS, gather, 0)

    for b in range(targets):
        high, low = split(sums[b])
        beam_ref[b * points : (b + 1) * points, :] = mm(steer_ref[b], high) + mm(steer_ref[b], low)

    def finish(i, carry):
        other = (me + i) % owners
        label_to(other, me).wait_send()
        for r in range(GROUPS):
            slots_to(r, other, me).wait_send()
        return carry

    lax.fori_loop(1, owners, finish, 0)
    for r in range(GROUPS):

        @pl.when(tm > 0)
        def _():
            to_after(r).wait_send()

        @pl.when(tm < ntm - 1)
        def _():
            to_prev(r).wait_send()


def copy_to(source, target, send, receive, place):
    return pltpu.make_async_remote_copy(
        src_ref=source,
        dst_ref=target,
        send_sem=send,
        recv_sem=receive,
        device_id=place,
        device_id_type=MESH,
    )


def line_kernel(
    dims,
    block_ref,
    owner_ref,
    sub_ref,
    delay_ref,
    frac_ref,
    record,
    taps_ref,
    table_ref,
    sums,
    prev_out,
    prev_in,
    after_out,
    after_in,
    band_hi,
    band_lo,
    tab,
    weight,
    filt,
    shifted,
    out_pairs,
    in_pairs,
    out_slots,
    in_slots,
    out_name,
    in_name,
    out_label,
    in_label,
    pick,
    out_local,
    in_local,
    out_dense,
    in_dense,
    prev_send,
    prev_recv,
    after_send,
    after_recv,
    pair_send,
    pair_recv,
    slot_send,
    slot_recv,
    name_send,
    name_recv,
    label_send,
    label_recv,
    local_send,
    local_recv,
    dense_send,
    dense_recv,
):
    nchan, nsrc, ntm = dims
    blocks, block_rows, seg = record.shape
    ntab, ntaps = taps_ref.shape
    pairs = block_ref.shape[0]
    cap = out_slots.shape[2]
    targets = sums.shape[0]
    half = seg // nsrc
    step_rows = block_rows // PARTS
    rows = blocks * step_rows
    chip = lax.axis_index("chan")
    core = lax.axis_index("src")
    mate = 1 - core
    tm = lax.axis_index("tm")
    middle = jnp.logical_and(chip > 0, chip < nchan - 1)
    ending = jnp.logical_or(chip == 0, chip == nchan - 1)
    low_half = chip < nchan // 2
    outer = jnp.where(low_half, 0, nchan - 1)
    inner = jnp.where(low_half, 1, nchan - 2)
    other = nchan - 1 - inner
    far = nchan - 1 - outer

    barrier = pltpu.get_barrier_semaphore()

    def greet(place):
        pl.semaphore_signal(barrier, inc=1, device_id=place, device_id_type=MESH)

    @pl.when(tm > 0)
    def _():
        greet({"tm": tm - 1})

    @pl.when(tm < ntm - 1)
    def _():
        greet({"tm": tm + 1})

    greet({"src": mate})
    for k in range(nsrc):
        greet({"chan": other, "src": k})

    @pl.when(middle)
    def _():
        for k in range(nsrc):
            greet({"chan": outer, "src": k})

    @pl.when(ending)
    def _():
        for k in range(nsrc):
            greet({"chan": inner, "src": k})

    def part(r):
        return pl.ds(pl.multiple_of(r * step_rows, step_rows), step_rows)

    @pl.when(tm > 0)
    def _():
        for r in range(PARTS):
            after_out[r] = record[:, part(r), :].astype(jnp.bfloat16)

    @pl.when(tm < ntm - 1)
    def _():
        for r in range(PARTS):
            prev_out[r] = record[:, part(r), seg - ntaps :].astype(jnp.bfloat16)

    @pl.when(tm == 0)
    def _():
        prev_in[...] = jnp.zeros_like(prev_in)

    @pl.when(tm == ntm - 1)
    def _():
        after_in[...] = jnp.zeros_like(after_in)

    lanes = out_name.shape[1]
    lane = lax.broadcasted_iota(jnp.int32, out_name.shape, 1)
    own_name = jnp.zeros(out_name.shape, jnp.int32)
    for p in range(pairs):
        own_name = jnp.where(lane // step_rows == p, owner_ref[p] * targets + sub_ref[p], own_name)
    out_name[...] = own_name.astype(jnp.float32)
    slot_pair = []
    for k in range(nsrc):
        owner = outer * nsrc + k
        count = 0
        found = [-1] * cap
        for p in range(pairs):
            hit = owner_ref[p] == owner
            found = [jnp.where(jnp.logical_and(hit, count == j), p, found[j]) for j in range(cap)]
            count = count + jnp.where(hit, 1, 0)
        labels = jnp.full(out_name.shape, -1, jnp.int32)
        for j in range(cap):
            pair = jnp.maximum(found[j], 0)
            slot_pair.append(pair)
            name = jnp.where(found[j] >= 0, sub_ref[pair], -1)
            labels = jnp.where(lane // step_rows % cap == j, name, labels)
        out_label[k] = labels.astype(jnp.float32)

    build_band(taps_ref, band_hi, band_lo)

    pl.semaphore_wait(
        barrier,
        jnp.where(middle, 7, 3) + jnp.where(tm > 0, 1, 0) + jnp.where(tm < ntm - 1, 1, 0),
    )

    def to_prev(r):
        return copy_to(
            prev_out.at[r], prev_in.at[r], prev_send.at[r], prev_recv.at[r], {"tm": tm + 1}
        )

    def to_after(r):
        return copy_to(
            after_out.at[r], after_in.at[r], after_send.at[r], after_recv.at[r], {"tm": tm - 1}
        )

    def pairs_to(k, r, landing, place):
        return copy_to(
            out_pairs.at[r, k],
            in_pairs.at[landing, r],
            pair_send.at[k, r],
            pair_recv.at[landing, r],
            place,
        )

    def slots_to(k, r, landing, place):
        return copy_to(
            out_slots.at[r, k],
            in_slots.at[landing, r],
            slot_send.at[k, r],
            slot_recv.at[landing, r],
            place,
        )

    def name_to(k, landing, place):
        return copy_to(
            out_name, in_name.at[landing], name_send.at[k], name_recv.at[landing], place
        )

    def label_to(k, landing, place):
        return copy_to(
            out_label.at[k], in_label.at[landing], label_send.at[k], label_recv.at[landing], place
        )

    def local_to(r):
        return copy_to(
            out_local.at[r, mate], in_local.at[r], local_send.at[r], local_recv.at[r], {"src": mate}
        )

    def dense_to(k, r, landing):
        return copy_to(
            out_dense.at[r, k],
            in_dense.at[landing, r],
            dense_send.at[k, r],
            dense_recv.at[landing, r],
            {"chan": far if k < nsrc else other, "src": k % nsrc},
        )

    at_mate = {"src": mate}

    def at_inner(k):
        return {"chan": inner, "src": k}

    def at_outer(k):
        return {"chan": outer, "src": k}

    for r in range(PARTS):

        @pl.when(tm > 0)
        def _():
            to_after(r).start()

        @pl.when(tm < ntm - 1)
        def _():
            to_prev(r).start()

    @pl.when(middle)
    def _():
        name_to(0, 0, at_mate).start()
        for k in range(nsrc):
            label_to(k, 1 + core, at_outer(k)).start()

    @pl.when(ending)
    def _():
        for k in range(nsrc):
            name_to(k, 1 + core, at_inner(k)).start()
        label_to(mate, 0, at_mate).start()

    for g in range(blocks):
        tab[g] = jnp.broadcast_to(table_ref[g : g + 1, :], (block_rows, block_rows)).T
    for p in range(pairs):
        for k, value in enumerate(lagrange(frac_ref[p], lanes)):
            weight[p * 4 + k : p * 4 + k + 1, :] = value

    def produce(r):
        @pl.when(tm > 0)
        def _():
            to_prev(r).wait_recv()

        @pl.when(tm < ntm - 1)
        def _():
            to_after(r).wait_recv()

        inside = jnp.where(tm < ntm - 1, 1.0, 0.0)
        high, low = split(record[:, part(r), :].reshape(rows, seg))
        before = prev_in[r].reshape(rows, ntaps)
        behind = after_in[r].reshape(rows, seg)
        window = jnp.concatenate([before, high, behind], axis=1)
        rest = jnp.concatenate(
            [jnp.zeros_like(before), low, jnp.zeros((rows, ntaps), jnp.bfloat16)], axis=1
        )
        steps = 2 * seg // ntaps
        near = seg // ntaps + 1
        lhs_hi = jnp.concatenate(
            [window[:, j * ntaps : (j + 2) * ntaps] for j in range(steps)], axis=0
        )
        lhs_lo = jnp.concatenate(
            [rest[:, j * ntaps : (j + 2) * ntaps] for j in range(near)], axis=0
        )
        every = mm(lhs_hi, band_lo[...]) + mm(lhs_hi, band_hi[...])
        fine = mm(lhs_lo, band_hi[...])
        which = tab[:, part(r), :].reshape(rows, block_rows)
        pieces = []
        for j in range(steps):
            own = every[j * rows : (j + 1) * rows]
            if j < near:
                own = own + fine[j * rows : (j + 1) * rows]
            value = own[:, :ntaps]
            for m in range(1, ntab):
                value = jnp.where(which == m, own[:, m * ntaps : (m + 1) * ntaps], value)
            if j >= seg // ntaps:
                value = value * inside
            pieces.append(value)
        whole = jnp.concatenate(pieces, axis=1)
        for k in range(4):
            moved = whole if k == 0 else pltpu.roll(whole, 2 * seg - k, 1)
            filt[k] = moved.reshape(blocks, step_rows, 2 * seg)

        def one_pair(p, c):
            source = block_ref[p]
            mixed = []
            for j in range(2 * seg // lanes):
                cols = slice(j * lanes, (j + 1) * lanes)
                total = weight[pl.ds(p * 4, 1), :] * filt[0, source, :, cols]
                for k in range(1, 4):
                    total = total + weight[pl.ds(p * 4 + k, 1), :] * filt[k, source, :, cols]
                mixed.append(total)
            moved = pltpu.roll(
                jnp.concatenate(mixed, axis=1), 2 * seg - (delay_ref[p] - 1), 1
            )[:, :seg].astype(jnp.bfloat16)
            shifted[p] = moved
            for k in range(nsrc):
                out_pairs[r, k, p] = moved[:, k * half : (k + 1) * half]
            return c

        lax.fori_loop(0, pairs, one_pair, 0, unroll=min(pairs, 4))

        @pl.when(ending)
        def _():
            for k in range(nsrc):
                pairs_to(k, r, 1 + core, at_inner(k)).start()

        @pl.when(middle)
        def _():
            pairs_to(mate, r, 0, at_mate).start()

        for k in range(nsrc):
            for j in range(cap):
                out_slots[r, k, j] = shifted[slot_pair[k * cap + j]]

        @pl.when(ending)
        def _():
            slots_to(mate, r, 0, at_mate).start()

        @pl.when(middle)
        def _():
            for k in range(nsrc):
                slots_to(k, r, 1 + core, at_outer(k)).start()

    def dense(r):
        pairs_to(0, r, 0, at_mate).wait_recv()
        for k in range(nsrc):
            pairs_to(0, r, 1 + k, at_outer(k)).wait_recv()
        depth = pairs * step_rows
        values = jnp.concatenate(
            [out_pairs[r, core].reshape(depth, half)]
            + [in_pairs[k, r].reshape(depth, half) for k in range(1 + nsrc)],
            axis=0,
        )
        total = mm(pick[...], values).reshape(3 * nsrc, targets, step_rows, half)
        for k in range(2 * nsrc):
            out_dense[r, k] = total[k].astype(jnp.bfloat16)
            dense_to(k, r, core).start()
        for k in range(nsrc):
            out_local[r, k] = total[2 * nsrc + k]
        local_to(r).start()

    unit = pairs * step_rows
    spot = lax.broadcasted_iota(jnp.int32, (unit, unit), 0)
    line = lax.broadcasted_iota(jnp.int32, (unit, unit), 1)
    diagonal = spot % step_rows == line % step_rows

    @pl.when(middle)
    def _():
        name_to(0, 0, at_mate).wait_recv()
        for k in range(nsrc):
            name_to(0, 1 + k, at_outer(k)).wait_recv()
        for i, chan in enumerate((far, other, chip)):
            wanted = (chan * nsrc * targets + spot // step_rows).astype(jnp.float32)
            for kind in range(2 + nsrc):
                names = out_name[0:1, :] if kind == 0 else in_name[kind - 1, 0:1, :]
                hit = jnp.logical_and(wanted == names, diagonal)
                pick[i * unit : (i + 1) * unit, kind * unit : (kind + 1) * unit] = jnp.where(
                    hit, 1.0, 0.0
                ).astype(jnp.bfloat16)

    @pl.when(ending)
    def _():
        label_to(mate, 0, at_mate).wait_recv()
        for k in range(nsrc):
            label_to(k, 1 + k, at_inner(k)).wait_recv()
        names = out_label[core, 0:1, :]
        for kind in range(1, 2 + nsrc):
            names = jnp.where(
                lane[0:1, :] // (cap * step_rows) == kind, in_label[kind - 1, 0:1, :], names
            )
        wanted = (spot // step_rows).astype(jnp.float32)
        hit = jnp.logical_and(wanted == names, diagonal)
        pick[:unit, :unit] = jnp.where(hit, 1.0, 0.0).astype(jnp.bfloat16)

    def produce_step(i, carry):
        @pl.when(i < PARTS)
        def _():
            produce(i)

        @pl.when(jnp.logical_and(middle, i >= LAG))
        def _():
            dense(i - LAG)

        return carry

    lax.fori_loop(0, PARTS + LAG, produce_step, 0)

    def store(r, b, value):
        high, low = split(value)
        sums[b, part(r), :] = high
        sums[b, pl.ds(pl.multiple_of(block_rows + r * step_rows, step_rows), step_rows), :] = low

    def finish(r, carry):
        @pl.when(ending)
        def _():
            slots_to(mate, r, 0, at_mate).wait_recv()
            for k in range(nsrc):
                slots_to(k, r, 1 + k, at_inner(k)).wait_recv()
            depth = cap * step_rows
            values = jnp.concatenate(
                [out_slots[r, core].reshape(depth, seg)]
                + [in_slots[k, r].reshape(depth, seg) for k in range(1 + nsrc)],
                axis=0,
            )
            total = mm(pick[: targets * step_rows, :unit], values)
            for k in range(nsrc):
                dense_to(0, r, k).wait_recv()
            for b in range(targets):
                added = jnp.concatenate([in_dense[k, r, b] for k in range(nsrc)], axis=1)
                store(
                    r, b, total[b * step_rows : (b + 1) * step_rows] + added.astype(jnp.float32)
                )

        @pl.when(middle)
        def _():
            local_to(r).wait_recv()
            for k in range(nsrc):
                dense_to(0, r, k).wait_recv()
            for b in range(targets):
                mine, theirs = out_local[r, core, b], in_local[r, b]
                total = jnp.concatenate(
                    [jnp.where(core == k, mine, theirs) for k in range(nsrc)], axis=1
                )
                added = jnp.concatenate([in_dense[k, r, b] for k in range(nsrc)], axis=1)
                store(r, b, total + added.astype(jnp.float32))

        return carry

    lax.fori_loop(0, PARTS, finish, 0)

    @pl.when(middle)
    def _():
        name_to(0, 0, at_mate).wait_send()
        for k in range(nsrc):
            label_to(k, 1 + core, at_outer(k)).wait_send()

    @pl.when(ending)
    def _():
        for k in range(nsrc):
            name_to(k, 1 + core, at_inner(k)).wait_send()
        label_to(mate, 0, at_mate).wait_send()

    def leave(r, carry):
        @pl.when(tm > 0)
        def _():
            to_after(r).wait_send()

        @pl.when(tm < ntm - 1)
        def _():
            to_prev(r).wait_send()

        @pl.when(ending)
        def _():
            for k in range(nsrc):
                pairs_to(k, r, 1 + core, at_inner(k)).wait_send()
            slots_to(mate, r, 0, at_mate).wait_send()

        @pl.when(middle)
        def _():
            pairs_to(mate, r, 0, at_mate).wait_send()
            for k in range(nsrc):
                slots_to(k, r, 1 + core, at_outer(k)).wait_send()
            for k in range(2 * nsrc):
                dense_to(k, r, core).wait_send()
            local_to(r).wait_send()

        return carry

    lax.fori_loop(0, PARTS, leave, 0)


def lagrange(frac, width):
    mu = jnp.full((1, width), frac.astype(jnp.float32)) / NFRAC
    return (
        -mu * (mu - 1.0) * (mu - 2.0) / 6.0,
        (mu + 1.0) * (mu - 1.0) * (mu - 2.0) / 2.0,
        -(mu + 1.0) * mu * (mu - 2.0) / 2.0,
        (mu + 1.0) * mu * (mu - 1.0) / 6.0,
    )


def steer_kernel(steer_ref, sums, beam_ref, held, done):
    points = steer_ref.shape[1]
    sends = []
    for b in range(sums.shape[0]):
        rows = pl.ds(b * points, points)
        twice = jnp.concatenate([steer_ref[b], steer_ref[b]], axis=1)
        held[rows, :] = mm(twice, sums[b])
        send = pltpu.make_async_copy(held.at[rows, :], beam_ref.at[rows, :], done.at[b])
        send.start()
        sends.append(send)
    for send in sends:
        send.wait()


def build_band(taps_ref, band_hi, band_lo):
    ntab, ntaps = taps_ref.shape
    for m in range(ntab):
        row = jnp.concatenate([taps_ref[m : m + 1, :], jnp.zeros((1, ntaps), jnp.float32)], axis=1)
        full = jnp.broadcast_to(row, (2 * ntaps, 2 * ntaps))
        rolled = pltpu.roll(full, ntaps, 1, stride=1, stride_axis=0)[:, :ntaps]
        high, low = split(rolled)
        band_hi[:, m * ntaps : (m + 1) * ntaps] = high
        band_lo[:, m * ntaps : (m + 1) * ntaps] = low


def band_filter(window, band_hi, band_lo, which, inside, seg, ntab, filt):
    blocks, step_rows, _ = filt.shape
    rows = blocks * step_rows
    ntaps = band_hi.shape[0] // 2
    high, low = split(window)
    steps = 2 * seg // ntaps
    lhs_hi = jnp.concatenate([high[:, j * ntaps : (j + 2) * ntaps] for j in range(steps)], axis=0)
    lhs_lo = jnp.concatenate([low[:, j * ntaps : (j + 2) * ntaps] for j in range(steps)], axis=0)
    every = mm(lhs_lo, band_hi[...]) + mm(lhs_hi, band_lo[...]) + mm(lhs_hi, band_hi[...])
    for j in range(steps):
        own = every[j * rows : (j + 1) * rows]
        value = own[:, :ntaps]
        for m in range(1, ntab):
            value = jnp.where(which == m, own[:, m * ntaps : (m + 1) * ntaps], value)
        if j >= seg // ntaps:
            value = value * inside
        filt[:, :, j * ntaps : (j + 1) * ntaps] = value.reshape(blocks, step_rows, ntaps)


def shift_pair(source, delay, frac, seg):
    mu = jnp.full((1, seg), frac.astype(jnp.float32)) / NFRAC
    first = -mu * (mu - 1.0) * (mu - 2.0) / 6.0
    second = (mu + 1.0) * (mu - 1.0) * (mu - 2.0) / 2.0
    third = -(mu + 1.0) * mu * (mu - 2.0) / 2.0
    fourth = (mu + 1.0) * mu * (mu - 1.0) / 6.0
    base = pltpu.roll(source, 2 * seg - (delay - 1), 1)
    mixed = first * base[:, :seg]
    mixed = mixed + second * pltpu.roll(base, 2 * seg - 1, 1)[:, :seg]
    mixed = mixed + third * pltpu.roll(base, 2 * seg - 2, 1)[:, :seg]
    mixed = mixed + fourth * pltpu.roll(base, 2 * seg - 3, 1)[:, :seg]
    return mixed.astype(jnp.bfloat16)


def solution(mesh):
    nchan, nsrc, ntm = mesh.shape["chan"], mesh.shape["src"], mesh.shape["tm"]
    owners = nchan * nsrc

    def local(
        record, fir_taps, chan_table, steering, pair_block, pair_owner, pair_sub, pair_delay, pair_frac
    ):
        channels, seg = record.shape
        ntab, ntaps = fir_taps.shape
        targets, points, block_rows = steering.shape
        blocks = channels // block_rows
        pairs = pair_block.shape[0]
        cap = 2 * pairs // owners
        step_rows = block_rows // GROUPS
        smem = pl.BlockSpec(memory_space=pltpu.SMEM)
        vmem = pl.BlockSpec(memory_space=pltpu.VMEM)
        dma = pltpu.SemaphoreType.DMA
        operands = (
            pair_block,
            pair_owner.reshape(pairs),
            pair_sub,
            pair_delay,
            pair_frac,
            record.reshape(blocks, block_rows, seg),
            fir_taps,
            chan_table.reshape(blocks, block_rows),
            steering,
        )
        unit = pairs * block_rows // PARTS
        square = unit == 128 and pairs == nsrc * targets and cap * (2 + nsrc) == pairs
        if nchan == 4 and nsrc == 2 and square:
            step_rows = block_rows // PARTS
            half = seg // nsrc
            kinds = 1 + nsrc
            bf16, f32 = jnp.bfloat16, jnp.float32
            sums = pl.pallas_call(
                functools.partial(line_kernel, (nchan, nsrc, ntm)),
                out_shape=pltpu.VMEM((targets, 2 * block_rows, seg), bf16),
                in_specs=[smem] * 5 + [vmem] * 3,
                out_specs=vmem,
                scratch_shapes=[
                    pltpu.VMEM((PARTS, blocks, step_rows, ntaps), bf16),
                    pltpu.VMEM((PARTS, blocks, step_rows, ntaps), bf16),
                    pltpu.VMEM((PARTS, blocks, step_rows, seg), bf16),
                    pltpu.VMEM((PARTS, blocks, step_rows, seg), bf16),
                    pltpu.VMEM((2 * ntaps, ntab * ntaps), bf16),
                    pltpu.VMEM((2 * ntaps, ntab * ntaps), bf16),
                    pltpu.VMEM((blocks, block_rows, block_rows), jnp.int32),
                    pltpu.VMEM((pairs * 4, 128), f32),
                    pltpu.VMEM((4, blocks, step_rows, 2 * seg), f32),
                    pltpu.VMEM((pairs, step_rows, seg), bf16),
                    pltpu.VMEM((PARTS, nsrc, pairs, step_rows, half), bf16),
                    pltpu.VMEM((kinds, PARTS, pairs, step_rows, half), bf16),
                    pltpu.VMEM((PARTS, nsrc, cap, step_rows, seg), bf16),
                    pltpu.VMEM((kinds, PARTS, cap, step_rows, seg), bf16),
                    pltpu.VMEM((8, 128), f32),
                    pltpu.VMEM((kinds, 8, 128), f32),
                    pltpu.VMEM((nsrc, 8, 128), f32),
                    pltpu.VMEM((kinds, 8, 128), f32),
                    pltpu.VMEM((3 * unit, (1 + kinds) * unit), bf16),
                    pltpu.VMEM((PARTS, nsrc, targets, step_rows, half), f32),
                    pltpu.VMEM((PARTS, targets, step_rows, half), f32),
                    pltpu.VMEM((PARTS, 2 * nsrc, targets, step_rows, half), bf16),
                    pltpu.VMEM((nsrc, PARTS, targets, step_rows, half), bf16),
                    dma((PARTS,)),
                    dma((PARTS,)),
                    dma((PARTS,)),
                    dma((PARTS,)),
                    dma((nsrc, PARTS)),
                    dma((kinds, PARTS)),
                    dma((nsrc, PARTS)),
                    dma((kinds, PARTS)),
                    dma((nsrc,)),
                    dma((kinds,)),
                    dma((nsrc,)),
                    dma((kinds,)),
                    dma((PARTS,)),
                    dma((PARTS,)),
                    dma((2 * nsrc, PARTS)),
                    dma((nsrc, PARTS)),
                ],
                compiler_params=pltpu.CompilerParams(collective_id=0, has_side_effects=True),
            )(*operands[:-1])
            return pl.pallas_call(
                steer_kernel,
                out_shape=jax.ShapeDtypeStruct((targets * points, seg), f32),
                in_specs=[vmem] * 2,
                out_specs=pl.BlockSpec(memory_space=pl.ANY),
                scratch_shapes=[pltpu.VMEM((targets * points, seg), f32), dma((targets,))],
                compiler_params=pltpu.CompilerParams(vmem_limit_bytes=16 << 20),
            )(steering, sums)
        return pl.pallas_call(
            functools.partial(kernel, (nchan, nsrc, ntm)),
            out_shape=jax.ShapeDtypeStruct((targets * points, seg), jnp.float32),
            in_specs=[smem] * 5 + [vmem] * 4,
            out_specs=vmem,
            scratch_shapes=[
                pltpu.VMEM((blocks, block_rows, ntaps), jnp.float32),
                pltpu.VMEM((blocks, block_rows, seg), jnp.float32),
                pltpu.VMEM((2 * ntaps, ntab * ntaps), jnp.bfloat16),
                pltpu.VMEM((2 * ntaps, ntab * ntaps), jnp.bfloat16),
                pltpu.VMEM((blocks, block_rows, block_rows), jnp.int32),
                pltpu.VMEM((blocks, step_rows, 2 * seg), jnp.float32),
                pltpu.VMEM((pairs, step_rows, seg), jnp.bfloat16),
                pltpu.VMEM((owners, cap, block_rows, seg), jnp.bfloat16),
                pltpu.VMEM((owners, cap, block_rows, seg), jnp.bfloat16),
                pltpu.VMEM((owners, 8, 128), jnp.float32),
                pltpu.VMEM((owners, 8, 128), jnp.float32),
                pltpu.VMEM((targets, block_rows, seg), jnp.float32),
                pltpu.SMEM((owners * cap,), jnp.int32),
                dma((GROUPS,)),
                dma((GROUPS,)),
                dma((GROUPS,)),
                dma((GROUPS,)),
                dma((GROUPS, owners)),
                dma((GROUPS, owners)),
                dma((owners,)),
                dma((owners,)),
            ],
            compiler_params=pltpu.CompilerParams(collective_id=0, has_side_effects=True),
        )(*operands)

    in_specs = (
        P(("groups", "chan", "src"), "tm"),
        P(),
        P(("chan", "src")),
        P(("chan", "src"), None, None),
        P(("chan", "src")),
        P(("chan", "src"), None),
        P(("chan", "src")),
        P(("chan", "src")),
        P(("chan", "src")),
    )
    out_specs = P(("groups", "chan", "src"), "tm")
    return jax.shard_map(local, mesh=mesh, in_specs=in_specs, out_specs=out_specs, check_vma=False)
```

```python
import functools

import jax
import jax.numpy as jnp
from jax import lax
from jax.experimental import pallas as pl
from jax.experimental.pallas import tpu as pltpu
from jax.sharding import PartitionSpec as P

NFRAC = 16
GROUPS = 4
PARTS = 8
MESH = pl.DeviceIdType.MESH


def split(value):
    high = value.astype(jnp.bfloat16)
    return high, (value - high.astype(jnp.float32)).astype(jnp.bfloat16)


def mm(a, b):
    return jnp.dot(a, b, preferred_element_type=jnp.float32)


def kernel(
    dims,
    block_ref,
    owner_ref,
    sub_ref,
    delay_ref,
    frac_ref,
    record,
    taps_ref,
    table_ref,
    steer_ref,
    beam_ref,
    prev,
    after,
    band_hi,
    band_lo,
    tab,
    filt,
    shifted,
    out_slots,
    in_slots,
    out_label,
    in_label,
    sums,
    slot_pair,
    prev_send,
    prev_recv,
    after_send,
    after_recv,
    slot_send,
    slot_recv,
    label_send,
    label_recv,
):
    nchan, nsrc, ntm = dims
    owners = nchan * nsrc
    blocks, block_rows, seg = record.shape
    ntab, ntaps = taps_ref.shape
    pairs = block_ref.shape[0]
    cap = out_slots.shape[1]
    targets = steer_ref.shape[0]
    points = steer_ref.shape[1]
    step_rows = block_rows // GROUPS
    rows = blocks * step_rows
    me = lax.axis_index("chan") * nsrc + lax.axis_index("src")
    tm = lax.axis_index("tm")

    def place(owner):
        return {"chan": owner // nsrc, "src": owner % nsrc}

    barrier = pltpu.get_barrier_semaphore()

    @pl.when(tm > 0)
    def _():
        pl.semaphore_signal(barrier, inc=1, device_id={"tm": tm - 1}, device_id_type=MESH)

    @pl.when(tm < ntm - 1)
    def _():
        pl.semaphore_signal(barrier, inc=1, device_id={"tm": tm + 1}, device_id_type=MESH)

    def greet(i, carry):
        pl.semaphore_signal(
            barrier, inc=1, device_id=place((me + i) % owners), device_id_type=MESH
        )
        return carry

    lax.fori_loop(1, owners, greet, 0)

    build_band(taps_ref, band_hi, band_lo)

    @pl.when(tm == 0)
    def _():
        prev[...] = jnp.zeros_like(prev)

    @pl.when(tm == ntm - 1)
    def _():
        after[...] = jnp.zeros_like(after)

    pl.semaphore_wait(
        barrier,
        owners - 1 + jnp.where(tm > 0, 1, 0) + jnp.where(tm < ntm - 1, 1, 0),
    )

    def part(r):
        return pl.ds(pl.multiple_of(r * step_rows, step_rows), step_rows)

    def to_prev(r):
        return pltpu.make_async_remote_copy(
            src_ref=record.at[:, part(r), pl.ds(seg - ntaps, ntaps)],
            dst_ref=prev.at[:, part(r), :],
            send_sem=prev_send.at[r],
            recv_sem=prev_recv.at[r],
            device_id={"tm": tm + 1},
            device_id_type=MESH,
        )

    def to_after(r):
        return pltpu.make_async_remote_copy(
            src_ref=record.at[:, part(r), :],
            dst_ref=after.at[:, part(r), :],
            send_sem=after_send.at[r],
            recv_sem=after_recv.at[r],
            device_id={"tm": tm - 1},
            device_id_type=MESH,
        )

    def slots_to(r, other, landing):
        return pltpu.make_async_remote_copy(
            src_ref=out_slots.at[other, :, part(r), :],
            dst_ref=in_slots.at[landing, :, part(r), :],
            send_sem=slot_send.at[r, other],
            recv_sem=slot_recv.at[r, landing],
            device_id=place(other),
            device_id_type=MESH,
        )

    def label_to(other, landing):
        return pltpu.make_async_remote_copy(
            src_ref=out_label.at[other],
            dst_ref=in_label.at[landing],
            send_sem=label_send.at[other],
            recv_sem=label_recv.at[landing],
            device_id=place(other),
            device_id_type=MESH,
        )

    for r in range(GROUPS):

        @pl.when(tm > 0)
        def _():
            to_after(r).start()

        @pl.when(tm < ntm - 1)
        def _():
            to_prev(r).start()

    for g in range(blocks):
        tab[g] = jnp.broadcast_to(table_ref[g : g + 1, :], (block_rows, block_rows)).T

    def slots_of(owner, carry):
        def look(p, found):
            hit = owner_ref[p] == owner
            count = found[0]
            named = [
                jnp.where(jnp.logical_and(hit, count == k), p, found[1 + k]) for k in range(cap)
            ]
            return (count + jnp.where(hit, 1, 0), *named)

        found = lax.fori_loop(0, pairs, look, (0,) + (-1,) * cap, unroll=min(pairs, 8))
        line = lax.broadcasted_iota(jnp.int32, out_label.shape[1:], 0)
        labels = jnp.full(out_label.shape[1:], -1.0, jnp.float32)
        for k in range(cap):
            pair = jnp.maximum(found[1 + k], 0)
            slot_pair[owner * cap + k] = pair
            name = jnp.where(found[1 + k] >= 0, sub_ref[pair], -1).astype(jnp.float32)
            labels = jnp.where(line == k, name, labels)
        out_label[owner] = labels
        return carry

    lax.fori_loop(0, owners, slots_of, 0)

    def send_label(i, carry):
        label_to((me + i) % owners, me).start()
        return carry

    lax.fori_loop(1, owners, send_label, 0)

    def produce(r, carry):
        @pl.when(tm > 0)
        def _():
            to_prev(r).wait_recv()

        @pl.when(tm < ntm - 1)
        def _():
            to_after(r).wait_recv()

        window = jnp.concatenate(
            [
                prev[:, part(r), :].reshape(rows, ntaps),
                record[:, part(r), :].reshape(rows, seg),
                after[:, part(r), :].reshape(rows, seg),
            ],
            axis=1,
        )
        inside = jnp.where(tm < ntm - 1, 1.0, 0.0)
        which = tab[:, part(r), :].reshape(rows, block_rows)
        band_filter(window, band_hi, band_lo, which, inside, seg, ntab, filt)

        def one_pair(p, c):
            shifted[p] = shift_pair(filt[block_ref[p]], delay_ref[p], frac_ref[p], seg)
            return c

        lax.fori_loop(0, pairs, one_pair, 0, unroll=min(pairs, 4))

        def ship(i, c):
            other = (me + owners // 2 + i) % owners
            for k in range(cap):
                out_slots[other, k, part(r), :] = shifted[slot_pair[other * cap + k]]

            @pl.when(other != me)
            def _():
                slots_to(r, other, me).start()

            return c

        lax.fori_loop(0, owners, ship, 0)
        return carry

    lax.fori_loop(0, GROUPS, produce, 0)

    def wait_label(i, carry):
        source = (me + i) % owners
        label_to(source, source).wait_recv()
        return carry

    lax.fori_loop(1, owners, wait_label, 0)

    def add(total, values, labels):
        for k in range(cap):
            name = jnp.concatenate([labels[k : k + 1, :]] * (seg // labels.shape[1]), axis=1)
            value = values[k].astype(jnp.float32)
            total = [
                total[b] + value * jnp.where(name == float(b), 1.0, 0.0) for b in range(targets)
            ]
        return total

    def gather(r, carry):
        total = [jnp.zeros((step_rows, seg), jnp.float32)] * targets
        total = add(total, out_slots[me, :, part(r), :], out_label[me])

        def one_source(i, running):
            source = (me + i) % owners
            slots_to(r, source, source).wait_recv()
            return tuple(add(list(running), in_slots[source, :, part(r), :], in_label[source]))

        total = lax.fori_loop(1, owners, one_source, tuple(total))
        for b in range(targets):
            sums[b, part(r), :] = total[b]
        return carry

    lax.fori_loop(0, GROUPS, gather, 0)

    for b in range(targets):
        high, low = split(sums[b])
        beam_ref[b * points : (b + 1) * points, :] = mm(steer_ref[b], high) + mm(steer_ref[b], low)

    def finish(i, carry):
        other = (me + i) % owners
        label_to(other, me).wait_send()
        for r in range(GROUPS):
            slots_to(r, other, me).wait_send()
        return carry

    lax.fori_loop(1, owners, finish, 0)
    for r in range(GROUPS):

        @pl.when(tm > 0)
        def _():
            to_after(r).wait_send()

        @pl.when(tm < ntm - 1)
        def _():
            to_prev(r).wait_send()


def copy_to(source, target, send, receive, place):
    return pltpu.make_async_remote_copy(
        src_ref=source,
        dst_ref=target,
        send_sem=send,
        recv_sem=receive,
        device_id=place,
        device_id_type=MESH,
    )


def line_kernel(
    dims,
    block_ref,
    owner_ref,
    sub_ref,
    delay_ref,
    frac_ref,
    record,
    taps_ref,
    table_ref,
    sums,
    raw,
    prev_in,
    after_in,
    far_raw,
    far_prev,
    far_after,
    band_hi,
    band_lo,
    tab,
    far_tab,
    weight,
    filt,
    shifted,
    far_pairs,
    out_pairs,
    in_pairs,
    out_slots,
    in_slots,
    out_meta,
    in_meta,
    numbers,
    pick,
    pick_slots,
    pick_far,
    out_local,
    in_local,
    out_dense,
    in_dense,
    out_near,
    in_near,
    prev_send,
    prev_recv,
    after_send,
    after_recv,
    raw_send,
    raw_recv,
    far_prev_send,
    far_prev_recv,
    far_after_send,
    far_after_recv,
    pair_send,
    pair_recv,
    slot_send,
    slot_recv,
    meta_send,
    meta_recv,
    local_send,
    local_recv,
    dense_send,
    dense_recv,
    near_send,
    near_recv,
    number_sem,
):
    nchan, nsrc, ntm = dims
    owners = nchan * nsrc
    ranks = owners // 2
    blocks, block_rows, seg = record.shape
    ntab, ntaps = taps_ref.shape
    pairs = block_ref.shape[0]
    cap = out_slots.shape[2]
    targets = sums.shape[0]
    half = seg // nsrc
    late = PARTS - ranks
    step_rows = block_rows // PARTS
    rows = blocks * step_rows
    unit = pairs * step_rows
    lanes = 128
    chip = lax.axis_index("chan")
    core = lax.axis_index("src")
    mate = 1 - core
    tm = lax.axis_index("tm")
    me = chip * nsrc + core
    middle = jnp.logical_and(chip > 0, chip < nchan - 1)
    ending = jnp.logical_or(chip == 0, chip == nchan - 1)
    low_half = chip < nchan // 2
    outer = jnp.where(low_half, 0, nchan - 1)
    inner = jnp.where(low_half, 1, nchan - 2)
    other = nchan - 1 - inner
    far = nchan - 1 - outer
    rank = jnp.where(ending, 0, nsrc) + core

    def near_place(k):
        return {"chan": outer if k < nsrc else inner, "src": k % nsrc}

    def far_place(k):
        return {"chan": far if k < nsrc else other, "src": k % nsrc}

    at_mate = {"src": mate}

    barrier = pltpu.get_barrier_semaphore()

    def greet(place):
        pl.semaphore_signal(barrier, inc=1, device_id=place, device_id_type=MESH)

    @pl.when(tm > 0)
    def _():
        greet({"tm": tm - 1})

    @pl.when(tm < ntm - 1)
    def _():
        greet({"tm": tm + 1})

    for i in range(1, owners):
        to = (me + i) % owners
        greet({"chan": to // nsrc, "src": to % nsrc})

    def part(r):
        return pl.ds(pl.multiple_of(r * step_rows, step_rows), step_rows)

    for r in range(PARTS):
        raw[r] = record[:, part(r), :].astype(jnp.bfloat16)

    @pl.when(tm == 0)
    def _():
        prev_in[...] = jnp.zeros_like(prev_in)
        far_prev[...] = jnp.zeros_like(far_prev)

    @pl.when(tm == ntm - 1)
    def _():
        after_in[...] = jnp.zeros_like(after_in)
        far_after[...] = jnp.zeros_like(far_after)

    lane = lax.broadcasted_iota(jnp.int32, (8, lanes), 1)
    own_numbers = jnp.zeros((8, lanes), jnp.int32)
    own_names = jnp.zeros((8, lanes), jnp.int32)
    for p in range(pairs):
        name = owner_ref[p] * targets + sub_ref[p]
        own_names = jnp.where(lane // step_rows == p, name, own_names)
        for k, ref in enumerate((block_ref, delay_ref, frac_ref)):
            own_numbers = jnp.where(lane == k * pairs + p, ref[p], own_numbers)
    slot_pair = []
    for k in range(ranks):
        owner = (outer if k < nsrc else inner) * nsrc + k % nsrc
        count = 0
        found = [-1] * cap
        for p in range(pairs):
            hit = owner_ref[p] == owner
            found = [jnp.where(jnp.logical_and(hit, count == j), p, found[j]) for j in range(cap)]
            count = count + jnp.where(hit, 1, 0)
        labels = jnp.full((8, lanes), -1, jnp.int32)
        for j in range(cap):
            pair = jnp.maximum(found[j], 0)
            slot_pair.append(pair)
            name = jnp.where(found[j] >= 0, sub_ref[pair], -1)
            labels = jnp.where(lane // step_rows % cap == j, name, labels)
        out_meta[k, 3:4, :] = labels[0:1]
    for f in range(ranks):
        tables = jnp.zeros((8, lanes), jnp.int32)
        for g in range(blocks):
            row = jnp.broadcast_to(table_ref[g : g + 1, :], (8, lanes))
            row = pltpu.roll(row, (g - f) * step_rows % lanes, 1)
            tables = jnp.where(lane // step_rows == g, row, tables)
        out_meta[ranks + f, 1:2, :] = tables[0:1]
        out_meta[f, 1:2, :] = own_names[0:1]
        out_meta[ranks + f, 3:4, :] = own_names[0:1]
    for k in range(owners):
        out_meta[k, 0:1, :] = own_numbers[0:1]
        out_meta[k, 2:3, :] = own_names[0:1]
    in_meta[rank] = out_meta[rank]

    pl.semaphore_wait(
        barrier,
        owners - 1 + jnp.where(tm > 0, 1, 0) + jnp.where(tm < ntm - 1, 1, 0),
    )

    def tail(ref, r):
        return ref.at[r, :, :, pl.ds(seg - ntaps, ntaps)]

    def to_prev(r):
        return copy_to(
            tail(raw, r), prev_in.at[r], prev_send.at[r], prev_recv.at[r], {"tm": tm + 1}
        )

    def to_after(r):
        return copy_to(
            raw.at[r], after_in.at[r], after_send.at[r], after_recv.at[r], {"tm": tm - 1}
        )

    def far_to_prev(s):
        return copy_to(
            tail(far_raw, s),
            far_prev.at[s],
            far_prev_send.at[s],
            far_prev_recv.at[s],
            {"tm": tm + 1},
        )

    def far_to_after(s):
        return copy_to(
            far_raw.at[s],
            far_after.at[s],
            far_after_send.at[s],
            far_after_recv.at[s],
            {"tm": tm - 1},
        )

    def raw_to(f, landing):
        return copy_to(
            raw.at[f], far_raw.at[landing], raw_send.at[f], raw_recv.at[landing], far_place(f)
        )

    def meta_to(k, landing):
        place = near_place(k) if k < ranks else far_place(k - ranks)
        return copy_to(
            out_meta.at[k], in_meta.at[landing], meta_send.at[k], meta_recv.at[landing], place
        )

    def pairs_to(k, h, landing, place):
        return copy_to(
            out_pairs.at[h, k],
            in_pairs.at[h, landing],
            pair_send.at[h, k],
            pair_recv.at[h, landing],
            place,
        )

    def slots_to(k, r, landing, place):
        return copy_to(
            out_slots.at[r, k],
            in_slots.at[r, landing],
            slot_send.at[r, k],
            slot_recv.at[r, landing],
            place,
        )

    def local_to(h):
        return copy_to(
            out_local.at[h, mate], in_local.at[h], local_send.at[h], local_recv.at[h], at_mate
        )

    def dense_to(k, h, landing):
        return copy_to(
            out_dense.at[h, k],
            in_dense.at[h, landing],
            dense_send.at[h, k],
            dense_recv.at[h, landing],
            far_place(k),
        )

    def near_to(k, landing):
        return copy_to(
            out_near.at[k], in_near.at[landing], near_send.at[k], near_recv.at[landing], near_place(k)
        )

    def others(do):
        for k in range(ranks):

            @pl.when(rank != k)
            def _():
                do(k)

    def halo(r):
        @pl.when(tm > 0)
        def _():
            to_after(r).start()

        @pl.when(tm < ntm - 1)
        def _():
            to_prev(r).start()

    for i in range(ranks):
        halo(ranks + i)
        raw_to(i, rank).start()
    others(lambda k: meta_to(k, rank).start())
    for f in range(ranks):
        meta_to(ranks + f, ranks + rank).start()
    for i in range(ranks):
        halo(i)

    build_band(taps_ref, band_hi, band_lo)
    for g in range(blocks):
        tab[g] = jnp.broadcast_to(table_ref[g : g + 1, :], (block_rows, block_rows)).T
    for p in range(pairs):
        for k, value in enumerate(lagrange(frac_ref[p], lanes)):
            weight[p * 4 + k : p * 4 + k + 1, :] = value

    def filter_part(before, high, low, behind, which):
        inside = jnp.where(tm < ntm - 1, 1.0, 0.0)
        steps = 2 * seg // ntaps
        near = seg // ntaps + 1

        def stack(window, count):
            return jnp.concatenate(
                [window[:, j * ntaps : (j + 2) * ntaps] for j in range(count)], axis=0
            )

        lhs_hi = stack(jnp.concatenate([before, high, behind], axis=1), steps)
        every = mm(lhs_hi, band_lo[...]) + mm(lhs_hi, band_hi[...])
        if low is not None:
            none = jnp.zeros_like(before)
            lhs_lo = stack(jnp.concatenate([none, low, none], axis=1), near)
            fine = mm(lhs_lo, band_hi[...])
        pieces = []
        for j in range(steps):
            own = every[j * rows : (j + 1) * rows]
            if low is not None and j < near:
                own = own + fine[j * rows : (j + 1) * rows]
            value = own[:, :ntaps]
            for m in range(1, ntab):
                value = jnp.where(which == m, own[:, m * ntaps : (m + 1) * ntaps], value)
            if j >= seg // ntaps:
                value = value * inside
            pieces.append(value)
        whole = jnp.concatenate(pieces, axis=1)
        for k in range(4):
            moved = whole if k == 0 else pltpu.roll(whole, 2 * seg - k, 1)
            filt[k] = moved.reshape(blocks, step_rows, 2 * seg)

    def shift_one(source, delay, line):
        mixed = []
        for j in range(2 * seg // lanes):
            cols = slice(j * lanes, (j + 1) * lanes)
            total = weight[pl.ds(line, 1), :] * filt[0, source, :, cols]
            for k in range(1, 4):
                total = total + weight[pl.ds(line + k, 1), :] * filt[k, source, :, cols]
            mixed.append(total)
        moved = pltpu.roll(jnp.concatenate(mixed, axis=1), 2 * seg - (delay - 1), 1)
        return moved[:, :seg].astype(jnp.bfloat16)

    def filter_own(r):
        @pl.when(tm > 0)
        def _():
            to_prev(r).wait_recv()

        @pl.when(tm < ntm - 1)
        def _():
            to_after(r).wait_recv()

        high, low = split(record[:, part(r), :].reshape(rows, seg))
        which = tab[:, part(r), :].reshape(rows, block_rows)
        filter_part(
            prev_in[r].reshape(rows, ntaps), high, low, after_in[r].reshape(rows, seg), which
        )

    def fill_slots(r, k):
        for j in range(cap):
            out_slots[r, k, j] = shifted[slot_pair[k * cap + j]]

    def keep_slots(r):
        for k in range(ranks):

            @pl.when(rank == k)
            def _():
                for j in range(cap):
                    in_slots[r, k, j] = shifted[slot_pair[k * cap + j]]

    def produce_late(h, carry):
        r = late + h
        filter_own(r)

        def one_pair(p, c):
            moved = shift_one(block_ref[p], delay_ref[p], p * 4)
            shifted[p] = moved
            for k in range(nsrc):
                out_pairs[h, k, p] = moved[:, k * half : (k + 1) * half]
            in_pairs[h, rank, p] = jnp.where(core == 0, moved[:, :half], moved[:, half:])
            return c

        lax.fori_loop(0, pairs, one_pair, 0, unroll=min(pairs, 4))

        @pl.when(ending)
        def _():
            for k in range(nsrc):
                pairs_to(k, h, rank, near_place(nsrc + k)).start()

        @pl.when(middle)
        def _():
            pairs_to(mate, h, rank, at_mate).start()

        for k in range(nsrc):
            fill_slots(r, k)

        @pl.when(ending)
        def _():
            slots_to(mate, r, rank, at_mate).start()
            keep_slots(r)

        @pl.when(middle)
        def _():
            for k in range(nsrc):
                slots_to(k, r, rank, near_place(k)).start()

        return carry

    def produce_early(r):
        filter_own(r)

        def one_pair(p, c):
            shifted[p] = shift_one(block_ref[p], delay_ref[p], p * 4)
            return c

        lax.fori_loop(0, pairs, one_pair, 0, unroll=min(pairs, 4))
        for k in range(ranks):
            fill_slots(r, k)
        others(lambda k: slots_to(k, r, rank, near_place(k)).start())
        keep_slots(r)

    def forward(s):
        raw_to(0, s).wait_recv()

        @pl.when(tm > 0)
        def _():
            far_to_after(s).start()

        @pl.when(tm < ntm - 1)
        def _():
            far_to_prev(s).start()

    def produce_far(s):
        @pl.when(tm > 0)
        def _():
            far_to_prev(s).wait_recv()

        @pl.when(tm < ntm - 1)
        def _():
            far_to_after(s).wait_recv()

        filter_part(
            far_prev[s].reshape(rows, ntaps),
            far_raw[s].reshape(rows, seg),
            None,
            far_after[s].reshape(rows, seg),
            far_tab[s],
        )

        def one_pair(p, c):
            line = ((1 + s) * pairs + p) * 4
            far_pairs[s, p] = shift_one(numbers[s, 0, p], numbers[s, 0, pairs + p], line)
            return c

        lax.fori_loop(0, pairs, one_pair, 0, unroll=min(pairs, 4))

    def dense(h):
        others(lambda s: pairs_to(0, h, s, at_mate).wait_recv())
        total = mm(pick[...], in_pairs[h].reshape(ranks * unit, half))
        total = total.reshape(3 * nsrc, targets, step_rows, half)
        for k in range(2 * nsrc):
            out_dense[h, k] = total[k].astype(jnp.bfloat16)
            dense_to(k, h, core).start()
        for k in range(nsrc):
            out_local[h, k] = total[2 * nsrc + k]
        local_to(h).start()

    lax.fori_loop(0, PARTS - late, produce_late, 0)

    spot = lax.broadcasted_iota(jnp.int32, (unit, unit), 0)
    line = lax.broadcasted_iota(jnp.int32, (unit, unit), 1)
    diagonal = spot % step_rows == line % step_rows

    def fill(ref, i, kind, chan, names):
        hit = jnp.logical_and(chan * nsrc * targets + spot // step_rows == names, diagonal)
        ref[i * unit : (i + 1) * unit, kind * unit : (kind + 1) * unit] = jnp.where(
            hit, 1.0, 0.0
        ).astype(jnp.bfloat16)

    others(lambda k: meta_to(0, k).wait_recv())

    @pl.when(middle)
    def _():
        for i, chan in enumerate((far, other, chip)):
            for kind in range(ranks):
                fill(pick, i, kind, chan, in_meta[kind, 2:3, :])

    labels = in_meta[0, 3:4, :]
    for kind in range(1, ranks):
        labels = jnp.where(
            lane[0:1] // (cap * step_rows) == kind, in_meta[kind, 3:4, :], labels
        )
    hit = jnp.logical_and(spot // step_rows == labels, diagonal)
    pick_slots[...] = jnp.where(hit, 1.0, 0.0).astype(jnp.bfloat16)[: targets * step_rows]

    def early_step(i, carry):
        forward((i + nsrc) % ranks)
        produce_early(i)

        @pl.when(jnp.logical_and(middle, i >= 1))
        def _():
            dense(i - 1)

        return carry

    lax.fori_loop(0, ranks, early_step, 0)

    for s in range(ranks):
        meta_to(ranks, ranks + s).wait_recv()
    move = pltpu.make_async_copy(in_meta.at[pl.ds(ranks, ranks)], numbers, number_sem)
    move.start()
    for s in range(ranks):
        far_tab[s] = jnp.broadcast_to(in_meta[ranks + s, 1:2, :], (lanes, lanes)).T[:rows]
        for i, chan in enumerate((outer, inner)):
            fill(pick_far, i, s, chan, in_meta[ranks + s, 2:3, :])
    move.wait()

    def far_weights(i, carry):
        s, p = i // pairs, i % pairs
        for k, value in enumerate(lagrange(numbers[s, 0, 2 * pairs + p], lanes)):
            weight[pl.ds((pairs + i) * 4 + k, 1), :] = value
        return carry

    lax.fori_loop(0, ranks * pairs, far_weights, 0, unroll=4)

    def far_step(i, carry):
        produce_far((i + nsrc) % ranks)

        @pl.when(jnp.logical_and(middle, i == 0))
        def _():
            dense(PARTS - late - 1)

        return carry

    lax.fori_loop(0, ranks, far_step, 0)
    total = mm(pick_far[...], far_pairs[...].reshape(ranks * unit, seg))
    total = total.reshape(ranks, targets, step_rows, seg)
    for k in range(ranks):
        out_near[k] = total[k].astype(jnp.bfloat16)
    others(lambda k: near_to(k, rank).start())
    in_near[rank] = out_near[rank]

    def store(r, b, value):
        high, low = split(value)
        sums[b, part(r), :] = high
        sums[b, pl.ds(pl.multiple_of(block_rows + r * step_rows, step_rows), step_rows), :] = low

    def from_slots(r):
        others(lambda s: slots_to(0, r, s, at_mate).wait_recv())
        return mm(pick_slots[...], in_slots[r].reshape(ranks * cap * step_rows, seg))

    def finish_late(h, carry):
        r = late + h

        @pl.when(ending)
        def _():
            total = from_slots(r)
            for k in range(nsrc):
                dense_to(0, h, k).wait_recv()
            for b in range(targets):
                added = jnp.concatenate([in_dense[h, k, b] for k in range(nsrc)], axis=1)
                store(
                    r, b, total[b * step_rows : (b + 1) * step_rows] + added.astype(jnp.float32)
                )

        @pl.when(middle)
        def _():
            local_to(h).wait_recv()
            for k in range(nsrc):
                dense_to(0, h, k).wait_recv()
            for b in range(targets):
                mine, theirs = out_local[h, core, b], in_local[h, b]
                total = jnp.concatenate(
                    [jnp.where(core == k, mine, theirs) for k in range(nsrc)], axis=1
                )
                added = jnp.concatenate([in_dense[h, k, b] for k in range(nsrc)], axis=1)
                store(r, b, total + added.astype(jnp.float32))

        return carry

    lax.fori_loop(0, PARTS - late, finish_late, 0)

    def finish_early(r, carry):
        total = from_slots(r)

        @pl.when(rank != r)
        def _():
            near_to(0, r).wait_recv()

        for b in range(targets):
            store(
                r,
                b,
                total[b * step_rows : (b + 1) * step_rows] + in_near[r, b].astype(jnp.float32),
            )
        return carry

    lax.fori_loop(0, ranks, finish_early, 0)

    others(lambda k: meta_to(k, rank).wait_send())
    others(lambda k: near_to(k, rank).wait_send())
    for f in range(ranks):
        meta_to(ranks + f, ranks + rank).wait_send()
        raw_to(f, rank).wait_send()

    def leave(r, carry):
        @pl.when(tm > 0)
        def _():
            to_after(r).wait_send()

        @pl.when(tm < ntm - 1)
        def _():
            to_prev(r).wait_send()

        return carry

    lax.fori_loop(0, PARTS, leave, 0)

    def leave_early(r, carry):
        others(lambda k: slots_to(k, r, rank, near_place(k)).wait_send())

        @pl.when(tm > 0)
        def _():
            far_to_after(r).wait_send()

        @pl.when(tm < ntm - 1)
        def _():
            far_to_prev(r).wait_send()

        return carry

    lax.fori_loop(0, ranks, leave_early, 0)

    def leave_late(h, carry):
        @pl.when(ending)
        def _():
            for k in range(nsrc):
                pairs_to(k, h, rank, near_place(nsrc + k)).wait_send()
            slots_to(mate, late + h, rank, at_mate).wait_send()

        @pl.when(middle)
        def _():
            pairs_to(mate, h, rank, at_mate).wait_send()
            for k in range(nsrc):
                slots_to(k, late + h, rank, near_place(k)).wait_send()
            for k in range(2 * nsrc):
                dense_to(k, h, core).wait_send()
            local_to(h).wait_send()

        return carry

    lax.fori_loop(0, PARTS - late, leave_late, 0)


def lagrange(frac, width):
    mu = jnp.full((1, width), frac.astype(jnp.float32)) / NFRAC
    return (
        -mu * (mu - 1.0) * (mu - 2.0) / 6.0,
        (mu + 1.0) * (mu - 1.0) * (mu - 2.0) / 2.0,
        -(mu + 1.0) * mu * (mu - 2.0) / 2.0,
        (mu + 1.0) * mu * (mu - 1.0) / 6.0,
    )


def steer_kernel(steer_ref, sums, beam_ref, held, done):
    points = steer_ref.shape[1]
    sends = []
    for b in range(sums.shape[0]):
        rows = pl.ds(b * points, points)
        twice = jnp.concatenate([steer_ref[b], steer_ref[b]], axis=1)
        held[rows, :] = mm(twice, sums[b])
        send = pltpu.make_async_copy(held.at[rows, :], beam_ref.at[rows, :], done.at[b])
        send.start()
        sends.append(send)
    for send in sends:
        send.wait()


def build_band(taps_ref, band_hi, band_lo):
    ntab, ntaps = taps_ref.shape
    for m in range(ntab):
        row = jnp.concatenate([taps_ref[m : m + 1, :], jnp.zeros((1, ntaps), jnp.float32)], axis=1)
        full = jnp.broadcast_to(row, (2 * ntaps, 2 * ntaps))
        rolled = pltpu.roll(full, ntaps, 1, stride=1, stride_axis=0)[:, :ntaps]
        high, low = split(rolled)
        band_hi[:, m * ntaps : (m + 1) * ntaps] = high
        band_lo[:, m * ntaps : (m + 1) * ntaps] = low


def band_filter(window, band_hi, band_lo, which, inside, seg, ntab, filt):
    blocks, step_rows, _ = filt.shape
    rows = blocks * step_rows
    ntaps = band_hi.shape[0] // 2
    high, low = split(window)
    steps = 2 * seg // ntaps
    lhs_hi = jnp.concatenate([high[:, j * ntaps : (j + 2) * ntaps] for j in range(steps)], axis=0)
    lhs_lo = jnp.concatenate([low[:, j * ntaps : (j + 2) * ntaps] for j in range(steps)], axis=0)
    every = mm(lhs_lo, band_hi[...]) + mm(lhs_hi, band_lo[...]) + mm(lhs_hi, band_hi[...])
    for j in range(steps):
        own = every[j * rows : (j + 1) * rows]
        value = own[:, :ntaps]
        for m in range(1, ntab):
            value = jnp.where(which == m, own[:, m * ntaps : (m + 1) * ntaps], value)
        if j >= seg // ntaps:
            value = value * inside
        filt[:, :, j * ntaps : (j + 1) * ntaps] = value.reshape(blocks, step_rows, ntaps)


def shift_pair(source, delay, frac, seg):
    mu = jnp.full((1, seg), frac.astype(jnp.float32)) / NFRAC
    first = -mu * (mu - 1.0) * (mu - 2.0) / 6.0
    second = (mu + 1.0) * (mu - 1.0) * (mu - 2.0) / 2.0
    third = -(mu + 1.0) * mu * (mu - 2.0) / 2.0
    fourth = (mu + 1.0) * mu * (mu - 1.0) / 6.0
    base = pltpu.roll(source, 2 * seg - (delay - 1), 1)
    mixed = first * base[:, :seg]
    mixed = mixed + second * pltpu.roll(base, 2 * seg - 1, 1)[:, :seg]
    mixed = mixed + third * pltpu.roll(base, 2 * seg - 2, 1)[:, :seg]
    mixed = mixed + fourth * pltpu.roll(base, 2 * seg - 3, 1)[:, :seg]
    return mixed.astype(jnp.bfloat16)


def solution(mesh):
    nchan, nsrc, ntm = mesh.shape["chan"], mesh.shape["src"], mesh.shape["tm"]
    owners = nchan * nsrc

    def local(
        record, fir_taps, chan_table, steering, pair_block, pair_owner, pair_sub, pair_delay, pair_frac
    ):
        channels, seg = record.shape
        ntab, ntaps = fir_taps.shape
        targets, points, block_rows = steering.shape
        blocks = channels // block_rows
        pairs = pair_block.shape[0]
        cap = 2 * pairs // owners
        step_rows = block_rows // GROUPS
        smem = pl.BlockSpec(memory_space=pltpu.SMEM)
        vmem = pl.BlockSpec(memory_space=pltpu.VMEM)
        dma = pltpu.SemaphoreType.DMA
        operands = (
            pair_block,
            pair_owner.reshape(pairs),
            pair_sub,
            pair_delay,
            pair_frac,
            record.reshape(blocks, block_rows, seg),
            fir_taps,
            chan_table.reshape(blocks, block_rows),
            steering,
        )
        unit = pairs * block_rows // PARTS
        square = unit == 128 and pairs == nsrc * targets and cap * (2 * nsrc) == pairs
        if nchan == 4 and nsrc == 2 and square:
            step_rows = block_rows // PARTS
            half = seg // nsrc
            ranks = owners // 2
            late = PARTS - ranks
            whole = (blocks, step_rows, seg)
            edge = (blocks, step_rows, ntaps)
            bf16, f32, i32 = jnp.bfloat16, jnp.float32, jnp.int32
            held = pltpu.VMEM
            sums = pl.pallas_call(
                functools.partial(line_kernel, (nchan, nsrc, ntm)),
                out_shape=pltpu.VMEM((targets, 2 * block_rows, seg), bf16),
                in_specs=[smem] * 5 + [vmem] * 3,
                out_specs=vmem,
                scratch_shapes=[
                    held((PARTS, *whole), bf16),
                    held((PARTS, *edge), bf16),
                    held((PARTS, *whole), bf16),
                    held((ranks, *whole), bf16),
                    held((ranks, *edge), bf16),
                    held((ranks, *whole), bf16),
                    held((2 * ntaps, ntab * ntaps), bf16),
                    held((2 * ntaps, ntab * ntaps), bf16),
                    held((blocks, block_rows, block_rows), i32),
                    held((ranks, blocks * step_rows, 128), i32),
                    held(((1 + ranks) * pairs * 4, 128), f32),
                    held((4, blocks, step_rows, 2 * seg), f32),
                    held((pairs, step_rows, seg), bf16),
                    held((ranks, pairs, step_rows, seg), bf16),
                    held((late, nsrc, pairs, step_rows, half), bf16),
                    held((late, ranks, pairs, step_rows, half), bf16),
                    held((PARTS, ranks, cap, step_rows, seg), bf16),
                    held((PARTS, ranks, cap, step_rows, seg), bf16),
                    held((owners, 4, 128), i32),
                    held((owners, 4, 128), i32),
                    pltpu.SMEM((ranks, 4, 128), i32),
                    held((3 * unit, ranks * unit), bf16),
                    held((targets * step_rows, unit), bf16),
                    held((nsrc * unit, ranks * unit), bf16),
                    held((late, nsrc, targets, step_rows, half), f32),
                    held((late, targets, step_rows, half), f32),
                    held((late, ranks, targets, step_rows, half), bf16),
                    held((late, nsrc, targets, step_rows, half), bf16),
                    held((ranks, targets, step_rows, seg), bf16),
                    held((ranks, targets, step_rows, seg), bf16),
                    dma((PARTS,)),
                    dma((PARTS,)),
                    dma((PARTS,)),
                    dma((PARTS,)),
                    dma((ranks,)),
                    dma((ranks,)),
                    dma((ranks,)),
                    dma((ranks,)),
                    dma((ranks,)),
                    dma((ranks,)),
                    dma((late, nsrc)),
                    dma((late, ranks)),
                    dma((PARTS, ranks)),
                    dma((PARTS, ranks)),
                    dma((owners,)),
                    dma((owners,)),
                    dma((late,)),
                    dma((late,)),
                    dma((late, ranks)),
                    dma((late, nsrc)),
                    dma((ranks,)),
                    dma((ranks,)),
                    dma,
                ],
                compiler_params=pltpu.CompilerParams(collective_id=0, has_side_effects=True),
            )(*operands[:-1])
            return pl.pallas_call(
                steer_kernel,
                out_shape=jax.ShapeDtypeStruct((targets * points, seg), f32),
                in_specs=[vmem] * 2,
                out_specs=pl.BlockSpec(memory_space=pl.ANY),
                scratch_shapes=[held((targets * points, seg), f32), dma((targets,))],
                compiler_params=pltpu.CompilerParams(vmem_limit_bytes=16 << 20),
            )(steering, sums)
        return pl.pallas_call(
            functools.partial(kernel, (nchan, nsrc, ntm)),
            out_shape=jax.ShapeDtypeStruct((targets * points, seg), jnp.float32),
            in_specs=[smem] * 5 + [vmem] * 4,
            out_specs=vmem,
            scratch_shapes=[
                pltpu.VMEM((blocks, block_rows, ntaps), jnp.float32),
                pltpu.VMEM((blocks, block_rows, seg), jnp.float32),
                pltpu.VMEM((2 * ntaps, ntab * ntaps), jnp.bfloat16),
                pltpu.VMEM((2 * ntaps, ntab * ntaps), jnp.bfloat16),
                pltpu.VMEM((blocks, block_rows, block_rows), jnp.int32),
                pltpu.VMEM((blocks, step_rows, 2 * seg), jnp.float32),
                pltpu.VMEM((pairs, step_rows, seg), jnp.bfloat16),
                pltpu.VMEM((owners, cap, block_rows, seg), jnp.bfloat16),
                pltpu.VMEM((owners, cap, block_rows, seg), jnp.bfloat16),
                pltpu.VMEM((owners, 8, 128), jnp.float32),
                pltpu.VMEM((owners, 8, 128), jnp.float32),
                pltpu.VMEM((targets, block_rows, seg), jnp.float32),
                pltpu.SMEM((owners * cap,), jnp.int32),
                dma((GROUPS,)),
                dma((GROUPS,)),
                dma((GROUPS,)),
                dma((GROUPS,)),
                dma((GROUPS, owners)),
                dma((GROUPS, owners)),
                dma((owners,)),
                dma((owners,)),
            ],
            compiler_params=pltpu.CompilerParams(collective_id=0, has_side_effects=True),
        )(*operands)

    in_specs = (
        P(("groups", "chan", "src"), "tm"),
        P(),
        P(("chan", "src")),
        P(("chan", "src"), None, None),
        P(("chan", "src")),
        P(("chan", "src"), None),
        P(("chan", "src")),
        P(("chan", "src")),
        P(("chan", "src")),
    )
    out_specs = P(("groups", "chan", "src"), "tm")
    return jax.shard_map(local, mesh=mesh, in_specs=in_specs, out_specs=out_specs, check_vma=False)
```

```python
import functools

import jax
import jax.numpy as jnp
from jax import lax
from jax.experimental import pallas as pl
from jax.experimental.pallas import tpu as pltpu
from jax.sharding import PartitionSpec as P

NFRAC = 16
GROUPS = 4
PARTS = 8
MESH = pl.DeviceIdType.MESH


def split(value):
    high = value.astype(jnp.bfloat16)
    return high, (value - high.astype(jnp.float32)).astype(jnp.bfloat16)


def mm(a, b):
    return jnp.dot(a, b, preferred_element_type=jnp.float32)


def kernel(
    dims,
    block_ref,
    owner_ref,
    sub_ref,
    delay_ref,
    frac_ref,
    record,
    taps_ref,
    table_ref,
    steer_ref,
    beam_ref,
    prev,
    after,
    band_hi,
    band_lo,
    tab,
    filt,
    shifted,
    out_slots,
    in_slots,
    out_label,
    in_label,
    sums,
    slot_pair,
    prev_send,
    prev_recv,
    after_send,
    after_recv,
    slot_send,
    slot_recv,
    label_send,
    label_recv,
):
    nchan, nsrc, ntm = dims
    owners = nchan * nsrc
    blocks, block_rows, seg = record.shape
    ntab, ntaps = taps_ref.shape
    pairs = block_ref.shape[0]
    cap = out_slots.shape[1]
    targets = steer_ref.shape[0]
    points = steer_ref.shape[1]
    step_rows = block_rows // GROUPS
    rows = blocks * step_rows
    me = lax.axis_index("chan") * nsrc + lax.axis_index("src")
    tm = lax.axis_index("tm")

    def place(owner):
        return {"chan": owner // nsrc, "src": owner % nsrc}

    barrier = pltpu.get_barrier_semaphore()

    @pl.when(tm > 0)
    def _():
        pl.semaphore_signal(barrier, inc=1, device_id={"tm": tm - 1}, device_id_type=MESH)

    @pl.when(tm < ntm - 1)
    def _():
        pl.semaphore_signal(barrier, inc=1, device_id={"tm": tm + 1}, device_id_type=MESH)

    def greet(i, carry):
        pl.semaphore_signal(
            barrier, inc=1, device_id=place((me + i) % owners), device_id_type=MESH
        )
        return carry

    lax.fori_loop(1, owners, greet, 0)

    build_band(taps_ref, band_hi, band_lo)

    @pl.when(tm == 0)
    def _():
        prev[...] = jnp.zeros_like(prev)

    @pl.when(tm == ntm - 1)
    def _():
        after[...] = jnp.zeros_like(after)

    pl.semaphore_wait(
        barrier,
        owners - 1 + jnp.where(tm > 0, 1, 0) + jnp.where(tm < ntm - 1, 1, 0),
    )

    def part(r):
        return pl.ds(pl.multiple_of(r * step_rows, step_rows), step_rows)

    def to_prev(r):
        return pltpu.make_async_remote_copy(
            src_ref=record.at[:, part(r), pl.ds(seg - ntaps, ntaps)],
            dst_ref=prev.at[:, part(r), :],
            send_sem=prev_send.at[r],
            recv_sem=prev_recv.at[r],
            device_id={"tm": tm + 1},
            device_id_type=MESH,
        )

    def to_after(r):
        return pltpu.make_async_remote_copy(
            src_ref=record.at[:, part(r), :],
            dst_ref=after.at[:, part(r), :],
            send_sem=after_send.at[r],
            recv_sem=after_recv.at[r],
            device_id={"tm": tm - 1},
            device_id_type=MESH,
        )

    def slots_to(r, other, landing):
        return pltpu.make_async_remote_copy(
            src_ref=out_slots.at[other, :, part(r), :],
            dst_ref=in_slots.at[landing, :, part(r), :],
            send_sem=slot_send.at[r, other],
            recv_sem=slot_recv.at[r, landing],
            device_id=place(other),
            device_id_type=MESH,
        )

    def label_to(other, landing):
        return pltpu.make_async_remote_copy(
            src_ref=out_label.at[other],
            dst_ref=in_label.at[landing],
            send_sem=label_send.at[other],
            recv_sem=label_recv.at[landing],
            device_id=place(other),
            device_id_type=MESH,
        )

    for r in range(GROUPS):

        @pl.when(tm > 0)
        def _():
            to_after(r).start()

        @pl.when(tm < ntm - 1)
        def _():
            to_prev(r).start()

    for g in range(blocks):
        tab[g] = jnp.broadcast_to(table_ref[g : g + 1, :], (block_rows, block_rows)).T

    def slots_of(owner, carry):
        def look(p, found):
            hit = owner_ref[p] == owner
            count = found[0]
            named = [
                jnp.where(jnp.logical_and(hit, count == k), p, found[1 + k]) for k in range(cap)
            ]
            return (count + jnp.where(hit, 1, 0), *named)

        found = lax.fori_loop(0, pairs, look, (0,) + (-1,) * cap, unroll=min(pairs, 8))
        line = lax.broadcasted_iota(jnp.int32, out_label.shape[1:], 0)
        labels = jnp.full(out_label.shape[1:], -1.0, jnp.float32)
        for k in range(cap):
            pair = jnp.maximum(found[1 + k], 0)
            slot_pair[owner * cap + k] = pair
            name = jnp.where(found[1 + k] >= 0, sub_ref[pair], -1).astype(jnp.float32)
            labels = jnp.where(line == k, name, labels)
        out_label[owner] = labels
        return carry

    lax.fori_loop(0, owners, slots_of, 0)

    def send_label(i, carry):
        label_to((me + i) % owners, me).start()
        return carry

    lax.fori_loop(1, owners, send_label, 0)

    def produce(r, carry):
        @pl.when(tm > 0)
        def _():
            to_prev(r).wait_recv()

        @pl.when(tm < ntm - 1)
        def _():
            to_after(r).wait_recv()

        window = jnp.concatenate(
            [
                prev[:, part(r), :].reshape(rows, ntaps),
                record[:, part(r), :].reshape(rows, seg),
                after[:, part(r), :].reshape(rows, seg),
            ],
            axis=1,
        )
        inside = jnp.where(tm < ntm - 1, 1.0, 0.0)
        which = tab[:, part(r), :].reshape(rows, block_rows)
        band_filter(window, band_hi, band_lo, which, inside, seg, ntab, filt)

        def one_pair(p, c):
            shifted[p] = shift_pair(filt[block_ref[p]], delay_ref[p], frac_ref[p], seg)
            return c

        lax.fori_loop(0, pairs, one_pair, 0, unroll=min(pairs, 4))

        def ship(i, c):
            other = (me + owners // 2 + i) % owners
            for k in range(cap):
                out_slots[other, k, part(r), :] = shifted[slot_pair[other * cap + k]]

            @pl.when(other != me)
            def _():
                slots_to(r, other, me).start()

            return c

        lax.fori_loop(0, owners, ship, 0)
        return carry

    lax.fori_loop(0, GROUPS, produce, 0)

    def wait_label(i, carry):
        source = (me + i) % owners
        label_to(source, source).wait_recv()
        return carry

    lax.fori_loop(1, owners, wait_label, 0)

    def add(total, values, labels):
        for k in range(cap):
            name = jnp.concatenate([labels[k : k + 1, :]] * (seg // labels.shape[1]), axis=1)
            value = values[k].astype(jnp.float32)
            total = [
                total[b] + value * jnp.where(name == float(b), 1.0, 0.0) for b in range(targets)
            ]
        return total

    def gather(r, carry):
        total = [jnp.zeros((step_rows, seg), jnp.float32)] * targets
        total = add(total, out_slots[me, :, part(r), :], out_label[me])

        def one_source(i, running):
            source = (me + i) % owners
            slots_to(r, source, source).wait_recv()
            return tuple(add(list(running), in_slots[source, :, part(r), :], in_label[source]))

        total = lax.fori_loop(1, owners, one_source, tuple(total))
        for b in range(targets):
            sums[b, part(r), :] = total[b]
        return carry

    lax.fori_loop(0, GROUPS, gather, 0)

    for b in range(targets):
        high, low = split(sums[b])
        beam_ref[b * points : (b + 1) * points, :] = mm(steer_ref[b], high) + mm(steer_ref[b], low)

    def finish(i, carry):
        other = (me + i) % owners
        label_to(other, me).wait_send()
        for r in range(GROUPS):
            slots_to(r, other, me).wait_send()
        return carry

    lax.fori_loop(1, owners, finish, 0)
    for r in range(GROUPS):

        @pl.when(tm > 0)
        def _():
            to_after(r).wait_send()

        @pl.when(tm < ntm - 1)
        def _():
            to_prev(r).wait_send()


def copy_to(source, target, send, receive, place):
    return pltpu.make_async_remote_copy(
        src_ref=source,
        dst_ref=target,
        send_sem=send,
        recv_sem=receive,
        device_id=place,
        device_id_type=MESH,
    )


def line_kernel(
    dims,
    block_hbm,
    owner_hbm,
    sub_hbm,
    delay_hbm,
    frac_hbm,
    record_hbm,
    taps_hbm,
    table_hbm,
    sums,
    block_ref,
    owner_ref,
    sub_ref,
    delay_ref,
    frac_ref,
    record,
    taps_ref,
    table_ref,
    raw,
    prev_in,
    after_in,
    far_raw,
    far_prev,
    far_after,
    band,
    tab,
    far_tab,
    weight,
    filt,
    shifted,
    far_pairs,
    out_pairs,
    in_pairs,
    out_slots,
    in_slots,
    out_meta,
    in_meta,
    numbers,
    pick,
    pick_slots,
    pick_far,
    out_local,
    in_local,
    out_dense,
    in_dense,
    out_near,
    in_near,
    prev_send,
    prev_recv,
    after_send,
    after_recv,
    raw_send,
    raw_recv,
    far_prev_send,
    far_prev_recv,
    far_after_send,
    far_after_recv,
    pair_send,
    pair_recv,
    slot_send,
    slot_recv,
    meta_send,
    meta_recv,
    local_send,
    local_recv,
    dense_send,
    dense_recv,
    near_send,
    near_recv,
    number_sem,
    ready,
    load_sem,
):
    nchan, nsrc, ntm = dims
    loads = [
        pltpu.make_async_copy(source, target, load_sem.at[i])
        for i, (source, target) in enumerate(
            (
                (record_hbm, record),
                (block_hbm, block_ref),
                (owner_hbm, owner_ref),
                (sub_hbm, sub_ref),
                (delay_hbm, delay_ref),
                (frac_hbm, frac_ref),
                (taps_hbm, taps_ref),
                (table_hbm, table_ref),
            )
        )
    ]
    for load in loads:
        load.start()
    owners = nchan * nsrc
    ranks = owners // 2
    blocks, block_rows, seg = record.shape
    ntab, ntaps = taps_ref.shape
    pairs = block_ref.shape[0]
    cap = out_slots.shape[2]
    targets = sums.shape[0]
    half = seg // nsrc
    late = PARTS - ranks
    step_rows = block_rows // PARTS
    rows = blocks * step_rows
    unit = pairs * step_rows
    lanes = 128
    chip = lax.axis_index("chan")
    core = lax.axis_index("src")
    mate = 1 - core
    tm = lax.axis_index("tm")
    me = chip * nsrc + core
    middle = jnp.logical_and(chip > 0, chip < nchan - 1)
    ending = jnp.logical_or(chip == 0, chip == nchan - 1)
    low_half = chip < nchan // 2
    outer = jnp.where(low_half, 0, nchan - 1)
    inner = jnp.where(low_half, 1, nchan - 2)
    other = nchan - 1 - inner
    far = nchan - 1 - outer
    rank = jnp.where(ending, 0, nsrc) + core

    def near_place(k):
        return {"chan": outer if k < nsrc else inner, "src": k % nsrc}

    def far_place(k):
        return {"chan": far if k < nsrc else other, "src": k % nsrc}

    at_mate = {"src": mate}

    barrier = pltpu.get_barrier_semaphore()

    def greet(place):
        pl.semaphore_signal(barrier, inc=1, device_id=place, device_id_type=MESH)

    @pl.when(tm > 0)
    def _():
        greet({"tm": tm - 1})

    @pl.when(tm < ntm - 1)
    def _():
        greet({"tm": tm + 1})

    def others(do):
        for k in range(ranks):

            @pl.when(rank != k)
            def _():
                do(k)

    others(lambda k: greet(near_place(k)))

    for f in range(ranks):
        greet(far_place(f))

    def part(r):
        return pl.ds(pl.multiple_of(r * step_rows, step_rows), step_rows)

    @pl.when(tm == 0)
    def _():
        prev_in[...] = jnp.zeros_like(prev_in)
        far_prev[...] = jnp.zeros_like(far_prev)

    @pl.when(tm == ntm - 1)
    def _():
        after_in[...] = jnp.zeros_like(after_in)
        far_after[...] = jnp.zeros_like(far_after)

    loads[0].wait()
    for i in range(PARTS):
        r = (i + ranks) % PARTS
        raw[r] = record[:, part(r), :].astype(jnp.bfloat16)

    pl.semaphore_wait(
        barrier,
        owners - 1
        + jnp.where(tm > 0, 1, 0)
        + jnp.where(tm < ntm - 1, 1, 0),
    )

    def tail(ref, r):
        return ref.at[r, :, :, pl.ds(seg - ntaps, ntaps)]

    def to_prev(r):
        return copy_to(
            tail(raw, r), prev_in.at[r], prev_send.at[r], prev_recv.at[r], {"tm": tm + 1}
        )

    def to_after(r):
        return copy_to(
            raw.at[r], after_in.at[r], after_send.at[r], after_recv.at[r], {"tm": tm - 1}
        )

    def far_to_prev(s):
        return copy_to(
            tail(far_raw, s),
            far_prev.at[s],
            far_prev_send.at[s],
            far_prev_recv.at[s],
            {"tm": tm + 1},
        )

    def far_to_after(s):
        return copy_to(
            far_raw.at[s],
            far_after.at[s],
            far_after_send.at[s],
            far_after_recv.at[s],
            {"tm": tm - 1},
        )

    def raw_to(f, landing):
        return copy_to(
            raw.at[f], far_raw.at[landing], raw_send.at[f], raw_recv.at[landing], far_place(f)
        )

    def meta_to(k, landing):
        place = near_place(k) if k < ranks else far_place(k - ranks)
        return copy_to(
            out_meta.at[k], in_meta.at[landing], meta_send.at[k], meta_recv.at[landing], place
        )

    def pairs_to(k, h, landing, place):
        return copy_to(
            out_pairs.at[h, k],
            in_pairs.at[h, landing],
            pair_send.at[h, k],
            pair_recv.at[h, landing],
            place,
        )

    def slots_to(k, r, landing, place):
        return copy_to(
            out_slots.at[r, k],
            in_slots.at[r, landing],
            slot_send.at[r, k],
            slot_recv.at[r, landing],
            place,
        )

    def local_to(h):
        return copy_to(
            out_local.at[h, mate], in_local.at[h], local_send.at[h], local_recv.at[h], at_mate
        )

    def dense_to(k, h, landing):
        return copy_to(
            out_dense.at[h, k],
            in_dense.at[h, landing],
            dense_send.at[h, k],
            dense_recv.at[h, landing],
            far_place(k),
        )

    def near_to(k, landing):
        return copy_to(
            out_near.at[k], in_near.at[landing], near_send.at[k], near_recv.at[landing], near_place(k)
        )

    def halo(r):
        @pl.when(tm > 0)
        def _():
            to_after(r).start()

        @pl.when(tm < ntm - 1)
        def _():
            to_prev(r).start()

    def cross():
        for f in range(ranks):
            raw_to(f, rank).start()
            meta_to(ranks + f, ranks + rank).start()

    for i in range(ranks):
        halo(ranks + i)
        raw_to(i, rank).start()

    for i in range(ranks):
        halo(i)

    for load in loads[1:]:
        load.wait()
    lane = lax.broadcasted_iota(jnp.int32, (8, lanes), 1)
    own_numbers = jnp.zeros((8, lanes), jnp.int32)
    own_names = jnp.zeros((8, lanes), jnp.int32)
    for p in range(pairs):
        name = owner_ref[p] * targets + sub_ref[p]
        own_names = jnp.where(lane // step_rows == p, name, own_names)
        for k, ref in enumerate((block_ref, delay_ref, frac_ref)):
            own_numbers = jnp.where(lane == k * pairs + p, ref[p], own_numbers)
    slot_pair = []
    for k in range(ranks):
        owner = (outer if k < nsrc else inner) * nsrc + k % nsrc
        count = 0
        found = [-1] * cap
        for p in range(pairs):
            hit = owner_ref[p] == owner
            found = [jnp.where(jnp.logical_and(hit, count == j), p, found[j]) for j in range(cap)]
            count = count + jnp.where(hit, 1, 0)
        labels = jnp.full((8, lanes), -1, jnp.int32)
        for j in range(cap):
            pair = jnp.maximum(found[j], 0)
            slot_pair.append(pair)
            name = jnp.where(found[j] >= 0, sub_ref[pair], -1)
            labels = jnp.where(lane // step_rows % cap == j, name, labels)
        out_meta[k, 3:4, :] = labels[0:1]
    for f in range(ranks):
        tables = jnp.zeros((8, lanes), jnp.int32)
        for g in range(blocks):
            row = jnp.broadcast_to(table_ref[g : g + 1, :], (8, lanes))
            row = pltpu.roll(row, (g - f) * step_rows % lanes, 1)
            tables = jnp.where(lane // step_rows == g, row, tables)
        out_meta[ranks + f, 1:2, :] = tables[0:1]
        out_meta[f, 1:2, :] = own_names[0:1]
        out_meta[ranks + f, 3:4, :] = own_names[0:1]
    for k in range(owners):
        out_meta[k, 0:1, :] = own_numbers[0:1]
        out_meta[k, 2:3, :] = own_names[0:1]
    in_meta[rank] = out_meta[rank]
    others(lambda k: meta_to(k, rank).start())

    for f in range(ranks):
        meta_to(ranks + f, ranks + rank).start()

    depth = 2 * ntaps
    build_band(taps_ref, band.at[depth : 2 * depth, :], band.at[:depth, :])
    band[2 * depth :, :] = band[depth : 2 * depth, :]
    for g in range(blocks):
        tab[g] = jnp.broadcast_to(table_ref[g : g + 1, :], (block_rows, block_rows)).T
    step = lax.broadcasted_iota(jnp.int32, weight.shape, 0)
    value = jnp.zeros(weight.shape, jnp.float32)
    for k, rule in enumerate(lagrange((step // 4).astype(jnp.float32) / NFRAC)):
        value = jnp.where(step % 4 == k, rule, value)
    weight[...] = value

    def filter_part(before, high, low, behind, which):
        inside = jnp.where(tm < ntm - 1, 1.0, 0.0)
        steps = 2 * seg // ntaps

        def stack(window):
            return jnp.concatenate(
                [window[:, j * ntaps : (j + 2) * ntaps] for j in range(steps)], axis=0
            )

        lhs_hi = stack(jnp.concatenate([before, high, behind], axis=1))
        lhs = [lhs_hi, lhs_hi]
        if low is not None:
            none = jnp.zeros_like(before)
            lhs.append(stack(jnp.concatenate([none, low, none, none], axis=1)))
        every = mm(jnp.concatenate(lhs, axis=1), band[: len(lhs) * 2 * ntaps, :])
        pieces = []
        for j in range(steps):
            own = every[j * rows : (j + 1) * rows]
            value = own[:, :ntaps]
            for m in range(1, ntab):
                value = jnp.where(which == m, own[:, m * ntaps : (m + 1) * ntaps], value)
            if j >= seg // ntaps:
                value = value * inside
            pieces.append(value)
        whole = jnp.concatenate(pieces, axis=1)
        for k in range(4):
            moved = whole if k == 0 else pltpu.roll(whole, 2 * seg - k, 1)
            filt[k] = moved.reshape(blocks, step_rows, 2 * seg)

    def shift_one(source, delay, frac):
        line = frac * 4
        mixed = []
        for j in range(2 * seg // lanes):
            cols = slice(j * lanes, (j + 1) * lanes)
            total = weight[pl.ds(line, 1), :] * filt[0, source, :, cols]
            for k in range(1, 4):
                total = total + weight[pl.ds(line + k, 1), :] * filt[k, source, :, cols]
            mixed.append(total)
        moved = pltpu.roll(jnp.concatenate(mixed, axis=1), 2 * seg - (delay - 1), 1)
        return moved[:, :seg].astype(jnp.bfloat16)

    def filter_own(r):
        @pl.when(tm > 0)
        def _():
            to_prev(r).wait_recv()

        @pl.when(tm < ntm - 1)
        def _():
            to_after(r).wait_recv()

        high, low = split(record[:, part(r), :].reshape(rows, seg))
        which = tab[:, part(r), :].reshape(rows, block_rows)
        filter_part(
            prev_in[r].reshape(rows, ntaps), high, low, after_in[r].reshape(rows, seg), which
        )

    def fill_slots(r, k):
        for j in range(cap):
            out_slots[r, k, j] = shifted[slot_pair[k * cap + j]]

    def keep_slots(r):
        for k in range(ranks):

            @pl.when(rank == k)
            def _():
                for j in range(cap):
                    in_slots[r, k, j] = shifted[slot_pair[k * cap + j]]

    def produce_late(h, carry):
        r = ranks + h

        filter_own(r)

        def one_pair(p, c):
            moved = shift_one(block_ref[p], delay_ref[p], frac_ref[p])
            shifted[p] = moved
            for k in range(nsrc):
                out_pairs[h, k, p] = moved[:, k * half : (k + 1) * half]
            in_pairs[h, rank, p] = jnp.where(core == 0, moved[:, :half], moved[:, half:])
            return c

        lax.fori_loop(0, pairs, one_pair, 0, unroll=min(pairs, 4))

        @pl.when(ending)
        def _():
            for k in range(nsrc):
                pairs_to(k, h, rank, near_place(nsrc + k)).start()

        @pl.when(middle)
        def _():
            pairs_to(mate, h, rank, at_mate).start()

        for k in range(nsrc):
            fill_slots(r, k)

        @pl.when(ending)
        def _():
            slots_to(mate, r, rank, at_mate).start()
            keep_slots(r)

        @pl.when(middle)
        def _():
            for k in range(nsrc):
                slots_to(k, r, rank, near_place(k)).start()

        return carry

    def produce_early(r):
        filter_own(r)

        def one_pair(p, c):
            shifted[p] = shift_one(block_ref[p], delay_ref[p], frac_ref[p])
            return c

        lax.fori_loop(0, pairs, one_pair, 0, unroll=min(pairs, 4))
        for k in range(ranks):
            fill_slots(r, k)
        others(lambda k: slots_to(k, r, rank, near_place(k)).start())
        keep_slots(r)

    def forward(s):
        raw_to(0, s).wait_recv()

        @pl.when(tm > 0)
        def _():
            far_to_after(s).start()

        @pl.when(tm < ntm - 1)
        def _():
            far_to_prev(s).start()

    def produce_far(s):
        @pl.when(tm > 0)
        def _():
            far_to_prev(s).wait_recv()

        @pl.when(tm < ntm - 1)
        def _():
            far_to_after(s).wait_recv()

        filter_part(
            far_prev[s].reshape(rows, ntaps),
            far_raw[s].reshape(rows, seg),
            None,
            far_after[s].reshape(rows, seg),
            far_tab[s],
        )

        def one_pair(p, c):
            source, delay, frac = (numbers[s, 0, k * pairs + p] for k in range(3))
            far_pairs[s, p] = shift_one(source, delay, frac)
            return c

        lax.fori_loop(0, pairs, one_pair, 0, unroll=min(pairs, 4))

    def dense(h):
        others(lambda s: pairs_to(0, h, s, at_mate).wait_recv())
        total = mm(pick[...], in_pairs[h].reshape(ranks * unit, half))
        total = total.reshape(3 * nsrc, targets, step_rows, half)
        for k in range(2 * nsrc):
            out_dense[h, k] = total[k].astype(jnp.bfloat16)
            dense_to(k, h, core).start()
        for k in range(nsrc):
            out_local[h, k] = total[2 * nsrc + k]
        local_to(h).start()

    lax.fori_loop(0, late, produce_late, 0)

    spot = lax.broadcasted_iota(jnp.int32, (unit, unit), 0)
    line = lax.broadcasted_iota(jnp.int32, (unit, unit), 1)
    diagonal = spot % step_rows == line % step_rows

    def fill(ref, i, kind, chan, names):
        hit = jnp.logical_and(chan * nsrc * targets + spot // step_rows == names, diagonal)
        ref[i * unit : (i + 1) * unit, kind * unit : (kind + 1) * unit] = jnp.where(
            hit, 1.0, 0.0
        ).astype(jnp.bfloat16)

    others(lambda k: meta_to(0, k).wait_recv())

    @pl.when(middle)
    def _():
        for i, chan in enumerate((far, other, chip)):
            for kind in range(ranks):
                fill(pick, i, kind, chan, in_meta[kind, 2:3, :])

    labels = in_meta[0, 3:4, :]
    for kind in range(1, ranks):
        labels = jnp.where(
            lane[0:1] // (cap * step_rows) == kind, in_meta[kind, 3:4, :], labels
        )
    hit = jnp.logical_and(spot // step_rows == labels, diagonal)
    pick_slots[...] = jnp.where(hit, 1.0, 0.0).astype(jnp.bfloat16)[: targets * step_rows]

    def early_step(i, carry):
        forward((i + nsrc) % ranks)
        produce_early(i)

        @pl.when(jnp.logical_and(middle, i >= 1))
        def _():
            dense(i - 1)

        return carry

    lax.fori_loop(0, ranks, early_step, 0)

    for s in range(ranks):
        meta_to(ranks, ranks + s).wait_recv()
    move = pltpu.make_async_copy(in_meta.at[pl.ds(ranks, ranks)], numbers, number_sem)
    move.start()
    for s in range(ranks):
        far_tab[s] = jnp.broadcast_to(in_meta[ranks + s, 1:2, :], (lanes, lanes)).T[:rows]
        for i, chan in enumerate((outer, inner)):
            fill(pick_far, i, s, chan, in_meta[ranks + s, 2:3, :])
    move.wait()

    def far_step(i, carry):
        produce_far((i + nsrc) % ranks)

        @pl.when(jnp.logical_and(middle, i == 0))
        def _():
            dense(late - 1)

        return carry

    lax.fori_loop(0, ranks, far_step, 0)
    total = mm(pick_far[...], far_pairs[...].reshape(ranks * unit, seg))
    total = total.reshape(ranks, targets, step_rows, seg)
    for k in range(ranks):
        out_near[k] = total[k].astype(jnp.bfloat16)
    others(lambda k: near_to(k, rank).start())
    in_near[rank] = out_near[rank]

    others(lambda k: meta_to(k, rank).wait_send())
    for f in range(ranks):
        meta_to(ranks + f, ranks + rank).wait_send()
        raw_to(f, rank).wait_send()

    def leave(r, carry):
        @pl.when(tm > 0)
        def _():
            to_after(r).wait_send()

        @pl.when(tm < ntm - 1)
        def _():
            to_prev(r).wait_send()

        return carry

    lax.fori_loop(0, PARTS, leave, 0)

    def leave_early(r, carry):
        others(lambda k: slots_to(k, r, rank, near_place(k)).wait_send())

        @pl.when(tm > 0)
        def _():
            far_to_after(r).wait_send()

        @pl.when(tm < ntm - 1)
        def _():
            far_to_prev(r).wait_send()

        return carry

    lax.fori_loop(0, ranks, leave_early, 0)

    def leave_late(h, carry):
        @pl.when(ending)
        def _():
            for k in range(nsrc):
                pairs_to(k, h, rank, near_place(nsrc + k)).wait_send()
            slots_to(mate, ranks + h, rank, at_mate).wait_send()

        @pl.when(middle)
        def _():
            pairs_to(mate, h, rank, at_mate).wait_send()
            for k in range(nsrc):
                slots_to(k, ranks + h, rank, near_place(k)).wait_send()

        return carry

    lax.fori_loop(0, late, leave_late, 0)

    def store(r, b, value):
        high, low = split(value)
        sums[b, part(r), :] = high
        sums[b, pl.ds(pl.multiple_of(block_rows + r * step_rows, step_rows), step_rows), :] = low

    def from_slots(r):
        others(lambda s: slots_to(0, r, s, at_mate).wait_recv())
        return mm(pick_slots[...], in_slots[r].reshape(ranks * cap * step_rows, seg))

    def finish_late(h, carry):
        r = ranks + h

        @pl.when(ending)
        def _():
            total = from_slots(r)
            for k in range(nsrc):
                dense_to(0, h, k).wait_recv()
            for b in range(targets):
                added = jnp.concatenate([in_dense[h, k, b] for k in range(nsrc)], axis=1)
                store(
                    r, b, total[b * step_rows : (b + 1) * step_rows] + added.astype(jnp.float32)
                )

        @pl.when(middle)
        def _():
            local_to(h).wait_recv()
            for k in range(nsrc):
                dense_to(0, h, k).wait_recv()
            for b in range(targets):
                mine, theirs = out_local[h, core, b], in_local[h, b]
                total = jnp.concatenate(
                    [jnp.where(core == k, mine, theirs) for k in range(nsrc)], axis=1
                )
                added = jnp.concatenate([in_dense[h, k, b] for k in range(nsrc)], axis=1)
                store(r, b, total + added.astype(jnp.float32))

        return carry

    lax.fori_loop(0, late, finish_late, 0)

    def finish_early(r, carry):
        total = from_slots(r)

        @pl.when(rank != r)
        def _():
            near_to(0, r).wait_recv()

        for b in range(targets):
            store(
                r,
                b,
                total[b * step_rows : (b + 1) * step_rows] + in_near[r, b].astype(jnp.float32),
            )
        return carry

    lax.fori_loop(0, ranks, finish_early, 0)

    others(lambda k: near_to(k, rank).wait_send())

    @pl.when(middle)
    def _():
        for h in range(late):
            for k in range(2 * nsrc):
                dense_to(k, h, core).wait_send()
            local_to(h).wait_send()

def lagrange(mu):
    return (
        -mu * (mu - 1.0) * (mu - 2.0) / 6.0,
        (mu + 1.0) * (mu - 1.0) * (mu - 2.0) / 2.0,
        -(mu + 1.0) * mu * (mu - 2.0) / 2.0,
        (mu + 1.0) * mu * (mu - 1.0) / 6.0,
    )


def steer_kernel(steer_ref, sums, beam_ref, held, done):
    points = steer_ref.shape[1]
    sends = []
    for b in range(sums.shape[0]):
        rows = pl.ds(b * points, points)
        twice = jnp.concatenate([steer_ref[b], steer_ref[b]], axis=1)
        held[rows, :] = mm(twice, sums[b])
        send = pltpu.make_async_copy(held.at[rows, :], beam_ref.at[rows, :], done.at[b])
        send.start()
        sends.append(send)
    for send in sends:
        send.wait()


def build_band(taps_ref, band_hi, band_lo):
    ntab, ntaps = taps_ref.shape
    for m in range(ntab):
        row = jnp.concatenate([taps_ref[m : m + 1, :], jnp.zeros((1, ntaps), jnp.float32)], axis=1)
        full = jnp.broadcast_to(row, (2 * ntaps, 2 * ntaps))
        rolled = pltpu.roll(full, ntaps, 1, stride=1, stride_axis=0)[:, :ntaps]
        high, low = split(rolled)
        band_hi[:, m * ntaps : (m + 1) * ntaps] = high
        band_lo[:, m * ntaps : (m + 1) * ntaps] = low


def band_filter(window, band_hi, band_lo, which, inside, seg, ntab, filt):
    blocks, step_rows, _ = filt.shape
    rows = blocks * step_rows
    ntaps = band_hi.shape[0] // 2
    high, low = split(window)
    steps = 2 * seg // ntaps
    lhs_hi = jnp.concatenate([high[:, j * ntaps : (j + 2) * ntaps] for j in range(steps)], axis=0)
    lhs_lo = jnp.concatenate([low[:, j * ntaps : (j + 2) * ntaps] for j in range(steps)], axis=0)
    every = mm(lhs_lo, band_hi[...]) + mm(lhs_hi, band_lo[...]) + mm(lhs_hi, band_hi[...])
    for j in range(steps):
        own = every[j * rows : (j + 1) * rows]
        value = own[:, :ntaps]
        for m in range(1, ntab):
            value = jnp.where(which == m, own[:, m * ntaps : (m + 1) * ntaps], value)
        if j >= seg // ntaps:
            value = value * inside
        filt[:, :, j * ntaps : (j + 1) * ntaps] = value.reshape(blocks, step_rows, ntaps)


def shift_pair(source, delay, frac, seg):
    mu = jnp.full((1, seg), frac.astype(jnp.float32)) / NFRAC
    first = -mu * (mu - 1.0) * (mu - 2.0) / 6.0
    second = (mu + 1.0) * (mu - 1.0) * (mu - 2.0) / 2.0
    third = -(mu + 1.0) * mu * (mu - 2.0) / 2.0
    fourth = (mu + 1.0) * mu * (mu - 1.0) / 6.0
    base = pltpu.roll(source, 2 * seg - (delay - 1), 1)
    mixed = first * base[:, :seg]
    mixed = mixed + second * pltpu.roll(base, 2 * seg - 1, 1)[:, :seg]
    mixed = mixed + third * pltpu.roll(base, 2 * seg - 2, 1)[:, :seg]
    mixed = mixed + fourth * pltpu.roll(base, 2 * seg - 3, 1)[:, :seg]
    return mixed.astype(jnp.bfloat16)


def solution(mesh):
    nchan, nsrc, ntm = mesh.shape["chan"], mesh.shape["src"], mesh.shape["tm"]
    owners = nchan * nsrc

    def local(
        record, fir_taps, chan_table, steering, pair_block, pair_owner, pair_sub, pair_delay, pair_frac
    ):
        channels, seg = record.shape
        ntab, ntaps = fir_taps.shape
        targets, points, block_rows = steering.shape
        blocks = channels // block_rows
        pairs = pair_block.shape[0]
        cap = 2 * pairs // owners
        step_rows = block_rows // GROUPS
        smem = pl.BlockSpec(memory_space=pltpu.SMEM)
        vmem = pl.BlockSpec(memory_space=pltpu.VMEM)
        dma = pltpu.SemaphoreType.DMA
        operands = (
            pair_block,
            pair_owner.reshape(pairs),
            pair_sub,
            pair_delay,
            pair_frac,
            record.reshape(blocks, block_rows, seg),
            fir_taps,
            chan_table.reshape(blocks, block_rows),
            steering,
        )
        unit = pairs * block_rows // PARTS
        square = unit == 128 and pairs == nsrc * targets and cap * (2 * nsrc) == pairs
        if nchan == 4 and nsrc == 2 and square:
            step_rows = block_rows // PARTS
            half = seg // nsrc
            ranks = owners // 2
            late = PARTS - ranks
            whole = (blocks, step_rows, seg)
            edge = (blocks, step_rows, ntaps)
            bf16, f32, i32 = jnp.bfloat16, jnp.float32, jnp.int32
            held = pltpu.VMEM
            sums = pl.pallas_call(
                functools.partial(line_kernel, (nchan, nsrc, ntm)),
                out_shape=pltpu.VMEM((targets, 2 * block_rows, seg), bf16),
                in_specs=[pl.BlockSpec(memory_space=pltpu.HBM)] * 8,
                out_specs=vmem,
                scratch_shapes=[
                    *[pltpu.SMEM((pairs,), i32)] * 5,
                    held((blocks, block_rows, seg), f32),
                    held((ntab, ntaps), f32),
                    held((blocks, block_rows), i32),
                    held((PARTS, *whole), bf16),
                    held((PARTS, *edge), bf16),
                    held((PARTS, *whole), bf16),
                    held((ranks, *whole), bf16),
                    held((ranks, *edge), bf16),
                    held((ranks, *whole), bf16),
                    held((6 * ntaps, ntab * ntaps), bf16),
                    held((blocks, block_rows, block_rows), i32),
                    held((ranks, blocks * step_rows, 128), i32),
                    held((NFRAC * 4, 128), f32),
                    held((4, blocks, step_rows, 2 * seg), f32),
                    held((pairs, step_rows, seg), bf16),
                    held((ranks, pairs, step_rows, seg), bf16),
                    held((late, nsrc, pairs, step_rows, half), bf16),
                    held((late, ranks, pairs, step_rows, half), bf16),
                    held((PARTS, ranks, cap, step_rows, seg), bf16),
                    held((PARTS, ranks, cap, step_rows, seg), bf16),
                    held((owners, 4, 128), i32),
                    held((owners, 4, 128), i32),
                    pltpu.SMEM((ranks, 4, 128), i32),
                    held((3 * unit, ranks * unit), bf16),
                    held((targets * step_rows, unit), bf16),
                    held((nsrc * unit, ranks * unit), bf16),
                    held((late, nsrc, targets, step_rows, half), f32),
                    held((late, targets, step_rows, half), f32),
                    held((late, ranks, targets, step_rows, half), bf16),
                    held((late, nsrc, targets, step_rows, half), bf16),
                    held((ranks, targets, step_rows, seg), bf16),
                    held((ranks, targets, step_rows, seg), bf16),
                    dma((PARTS,)),
                    dma((PARTS,)),
                    dma((PARTS,)),
                    dma((PARTS,)),
                    dma((ranks,)),
                    dma((ranks,)),
                    dma((ranks,)),
                    dma((ranks,)),
                    dma((ranks,)),
                    dma((ranks,)),
                    dma((late, nsrc)),
                    dma((late, ranks)),
                    dma((PARTS, ranks)),
                    dma((PARTS, ranks)),
                    dma((owners,)),
                    dma((owners,)),
                    dma((late,)),
                    dma((late,)),
                    dma((late, ranks)),
                    dma((late, nsrc)),
                    dma((ranks,)),
                    dma((ranks,)),
                    dma,
                    pltpu.SemaphoreType.REGULAR,
                    dma((8,)),
                ],
                compiler_params=pltpu.CompilerParams(collective_id=0, has_side_effects=True),
            )(*operands[:-1])
            return pl.pallas_call(
                steer_kernel,
                out_shape=jax.ShapeDtypeStruct((targets * points, seg), f32),
                in_specs=[vmem] * 2,
                out_specs=pl.BlockSpec(memory_space=pl.ANY),
                scratch_shapes=[held((targets * points, seg), f32), dma((targets,))],
                compiler_params=pltpu.CompilerParams(vmem_limit_bytes=16 << 20),
            )(steering, sums)
        return pl.pallas_call(
            functools.partial(kernel, (nchan, nsrc, ntm)),
            out_shape=jax.ShapeDtypeStruct((targets * points, seg), jnp.float32),
            in_specs=[smem] * 5 + [vmem] * 4,
            out_specs=vmem,
            scratch_shapes=[
                pltpu.VMEM((blocks, block_rows, ntaps), jnp.float32),
                pltpu.VMEM((blocks, block_rows, seg), jnp.float32),
                pltpu.VMEM((2 * ntaps, ntab * ntaps), jnp.bfloat16),
                pltpu.VMEM((2 * ntaps, ntab * ntaps), jnp.bfloat16),
                pltpu.VMEM((blocks, block_rows, block_rows), jnp.int32),
                pltpu.VMEM((blocks, step_rows, 2 * seg), jnp.float32),
                pltpu.VMEM((pairs, step_rows, seg), jnp.bfloat16),
                pltpu.VMEM((owners, cap, block_rows, seg), jnp.bfloat16),
                pltpu.VMEM((owners, cap, block_rows, seg), jnp.bfloat16),
                pltpu.VMEM((owners, 8, 128), jnp.float32),
                pltpu.VMEM((owners, 8, 128), jnp.float32),
                pltpu.VMEM((targets, block_rows, seg), jnp.float32),
                pltpu.SMEM((owners * cap,), jnp.int32),
                dma((GROUPS,)),
                dma((GROUPS,)),
                dma((GROUPS,)),
                dma((GROUPS,)),
                dma((GROUPS, owners)),
                dma((GROUPS, owners)),
                dma((owners,)),
                dma((owners,)),
            ],
            compiler_params=pltpu.CompilerParams(collective_id=0, has_side_effects=True),
        )(*operands)

    in_specs = (
        P(("groups", "chan", "src"), "tm"),
        P(),
        P(("chan", "src")),
        P(("chan", "src"), None, None),
        P(("chan", "src")),
        P(("chan", "src"), None),
        P(("chan", "src")),
        P(("chan", "src")),
        P(("chan", "src")),
    )
    out_specs = P(("groups", "chan", "src"), "tm")
    return jax.shard_map(local, mesh=mesh, in_specs=in_specs, out_specs=out_specs, check_vma=False)
```

```python
import functools

import jax
import jax.numpy as jnp
from jax import lax
from jax.experimental import pallas as pl
from jax.experimental.pallas import tpu as pltpu
from jax.sharding import PartitionSpec as P

NFRAC = 16
GROUPS = 4
PARTS = 8
LAG = 1
MESH = pl.DeviceIdType.MESH


def split(value):
    high = value.astype(jnp.bfloat16)
    return high, (value - high.astype(jnp.float32)).astype(jnp.bfloat16)


def mm(a, b):
    return jnp.dot(a, b, preferred_element_type=jnp.float32)


def kernel(
    dims,
    block_ref,
    owner_ref,
    sub_ref,
    delay_ref,
    frac_ref,
    record,
    taps_ref,
    table_ref,
    steer_ref,
    beam_ref,
    prev,
    after,
    band_hi,
    band_lo,
    tab,
    filt,
    shifted,
    out_slots,
    in_slots,
    out_label,
    in_label,
    sums,
    slot_pair,
    prev_send,
    prev_recv,
    after_send,
    after_recv,
    slot_send,
    slot_recv,
    label_send,
    label_recv,
):
    nchan, nsrc, ntm = dims
    owners = nchan * nsrc
    blocks, block_rows, seg = record.shape
    ntab, ntaps = taps_ref.shape
    pairs = block_ref.shape[0]
    cap = out_slots.shape[1]
    targets = steer_ref.shape[0]
    points = steer_ref.shape[1]
    step_rows = block_rows // GROUPS
    rows = blocks * step_rows
    me = lax.axis_index("chan") * nsrc + lax.axis_index("src")
    tm = lax.axis_index("tm")

    def place(owner):
        return {"chan": owner // nsrc, "src": owner % nsrc}

    barrier = pltpu.get_barrier_semaphore()

    @pl.when(tm > 0)
    def _():
        pl.semaphore_signal(barrier, inc=1, device_id={"tm": tm - 1}, device_id_type=MESH)

    @pl.when(tm < ntm - 1)
    def _():
        pl.semaphore_signal(barrier, inc=1, device_id={"tm": tm + 1}, device_id_type=MESH)

    def greet(i, carry):
        pl.semaphore_signal(
            barrier, inc=1, device_id=place((me + i) % owners), device_id_type=MESH
        )
        return carry

    lax.fori_loop(1, owners, greet, 0)

    build_band(taps_ref, band_hi, band_lo)

    @pl.when(tm == 0)
    def _():
        prev[...] = jnp.zeros_like(prev)

    @pl.when(tm == ntm - 1)
    def _():
        after[...] = jnp.zeros_like(after)

    pl.semaphore_wait(
        barrier,
        owners - 1 + jnp.where(tm > 0, 1, 0) + jnp.where(tm < ntm - 1, 1, 0),
    )

    def part(r):
        return pl.ds(pl.multiple_of(r * step_rows, step_rows), step_rows)

    def to_prev(r):
        return pltpu.make_async_remote_copy(
            src_ref=record.at[:, part(r), pl.ds(seg - ntaps, ntaps)],
            dst_ref=prev.at[:, part(r), :],
            send_sem=prev_send.at[r],
            recv_sem=prev_recv.at[r],
            device_id={"tm": tm + 1},
            device_id_type=MESH,
        )

    def to_after(r):
        return pltpu.make_async_remote_copy(
            src_ref=record.at[:, part(r), :],
            dst_ref=after.at[:, part(r), :],
            send_sem=after_send.at[r],
            recv_sem=after_recv.at[r],
            device_id={"tm": tm - 1},
            device_id_type=MESH,
        )

    def slots_to(r, other, landing):
        return pltpu.make_async_remote_copy(
            src_ref=out_slots.at[other, :, part(r), :],
            dst_ref=in_slots.at[landing, :, part(r), :],
            send_sem=slot_send.at[r, other],
            recv_sem=slot_recv.at[r, landing],
            device_id=place(other),
            device_id_type=MESH,
        )

    def label_to(other, landing):
        return pltpu.make_async_remote_copy(
            src_ref=out_label.at[other],
            dst_ref=in_label.at[landing],
            send_sem=label_send.at[other],
            recv_sem=label_recv.at[landing],
            device_id=place(other),
            device_id_type=MESH,
        )

    for r in range(GROUPS):

        @pl.when(tm > 0)
        def _():
            to_after(r).start()

        @pl.when(tm < ntm - 1)
        def _():
            to_prev(r).start()

    for g in range(blocks):
        tab[g] = jnp.broadcast_to(table_ref[g : g + 1, :], (block_rows, block_rows)).T

    def slots_of(owner, carry):
        def look(p, found):
            hit = owner_ref[p] == owner
            count = found[0]
            named = [
                jnp.where(jnp.logical_and(hit, count == k), p, found[1 + k]) for k in range(cap)
            ]
            return (count + jnp.where(hit, 1, 0), *named)

        found = lax.fori_loop(0, pairs, look, (0,) + (-1,) * cap, unroll=min(pairs, 8))
        line = lax.broadcasted_iota(jnp.int32, out_label.shape[1:], 0)
        labels = jnp.full(out_label.shape[1:], -1.0, jnp.float32)
        for k in range(cap):
            pair = jnp.maximum(found[1 + k], 0)
            slot_pair[owner * cap + k] = pair
            name = jnp.where(found[1 + k] >= 0, sub_ref[pair], -1).astype(jnp.float32)
            labels = jnp.where(line == k, name, labels)
        out_label[owner] = labels
        return carry

    lax.fori_loop(0, owners, slots_of, 0)

    def send_label(i, carry):
        label_to((me + i) % owners, me).start()
        return carry

    lax.fori_loop(1, owners, send_label, 0)

    def produce(r, carry):
        @pl.when(tm > 0)
        def _():
            to_prev(r).wait_recv()

        @pl.when(tm < ntm - 1)
        def _():
            to_after(r).wait_recv()

        window = jnp.concatenate(
            [
                prev[:, part(r), :].reshape(rows, ntaps),
                record[:, part(r), :].reshape(rows, seg),
                after[:, part(r), :].reshape(rows, seg),
            ],
            axis=1,
        )
        inside = jnp.where(tm < ntm - 1, 1.0, 0.0)
        which = tab[:, part(r), :].reshape(rows, block_rows)
        band_filter(window, band_hi, band_lo, which, inside, seg, ntab, filt)

        def one_pair(p, c):
            shifted[p] = shift_pair(filt[block_ref[p]], delay_ref[p], frac_ref[p], seg)
            return c

        lax.fori_loop(0, pairs, one_pair, 0, unroll=pairs)

        def ship(i, c):
            other = (me + owners // 2 + i) % owners
            for k in range(cap):
                out_slots[other, k, part(r), :] = shifted[slot_pair[other * cap + k]]

            @pl.when(other != me)
            def _():
                slots_to(r, other, me).start()

            return c

        lax.fori_loop(0, owners, ship, 0)
        return carry

    lax.fori_loop(0, GROUPS, produce, 0)

    def wait_label(i, carry):
        source = (me + i) % owners
        label_to(source, source).wait_recv()
        return carry

    lax.fori_loop(1, owners, wait_label, 0)

    def add(total, values, labels):
        for k in range(cap):
            name = jnp.concatenate([labels[k : k + 1, :]] * (seg // labels.shape[1]), axis=1)
            value = values[k].astype(jnp.float32)
            total = [
                total[b] + value * jnp.where(name == float(b), 1.0, 0.0) for b in range(targets)
            ]
        return total

    def gather(r, carry):
        total = [jnp.zeros((step_rows, seg), jnp.float32)] * targets
        total = add(total, out_slots[me, :, part(r), :], out_label[me])

        def one_source(i, running):
            source = (me + i) % owners
            slots_to(r, source, source).wait_recv()
            return tuple(add(list(running), in_slots[source, :, part(r), :], in_label[source]))

        total = lax.fori_loop(1, owners, one_source, tuple(total))
        for b in range(targets):
            sums[b, part(r), :] = total[b]
        return carry

    lax.fori_loop(0, GROUPS, gather, 0)

    for b in range(targets):
        high, low = split(sums[b])
        beam_ref[b * points : (b + 1) * points, :] = mm(steer_ref[b], high) + mm(steer_ref[b], low)

    def finish(i, carry):
        other = (me + i) % owners
        label_to(other, me).wait_send()
        for r in range(GROUPS):
            slots_to(r, other, me).wait_send()
        return carry

    lax.fori_loop(1, owners, finish, 0)
    for r in range(GROUPS):

        @pl.when(tm > 0)
        def _():
            to_after(r).wait_send()

        @pl.when(tm < ntm - 1)
        def _():
            to_prev(r).wait_send()


def copy_to(source, target, send, receive, place):
    return pltpu.make_async_remote_copy(
        src_ref=source,
        dst_ref=target,
        send_sem=send,
        recv_sem=receive,
        device_id=place,
        device_id_type=MESH,
    )


def line_kernel(
    dims,
    block_hbm,
    owner_hbm,
    sub_hbm,
    delay_hbm,
    frac_hbm,
    record_hbm,
    taps_hbm,
    table_hbm,
    sums,
    block_ref,
    owner_ref,
    sub_ref,
    delay_ref,
    frac_ref,
    record,
    taps_ref,
    table_ref,
    raw,
    prev_in,
    after_in,
    far_raw,
    far_prev,
    far_after,
    band,
    tab,
    far_tab,
    weight,
    filt,
    shifted,
    far_pairs,
    out_pairs,
    in_pairs,
    out_slots,
    in_slots,
    out_meta,
    in_meta,
    numbers,
    pick,
    pick_slots,
    pick_far,
    out_local,
    in_local,
    out_dense,
    in_dense,
    out_near,
    in_near,
    near_sum,
    prev_send,
    prev_recv,
    after_send,
    after_recv,
    raw_send,
    raw_recv,
    far_prev_send,
    far_prev_recv,
    far_after_send,
    far_after_recv,
    pair_send,
    pair_recv,
    slot_send,
    slot_recv,
    meta_send,
    meta_recv,
    local_send,
    local_recv,
    dense_send,
    dense_recv,
    near_send,
    near_recv,
    number_sem,
    ready,
    load_sem,
):
    nchan, nsrc, ntm = dims
    loads = [
        pltpu.make_async_copy(source, target, load_sem.at[i])
        for i, (source, target) in enumerate(
            (
                (record_hbm, record),
                (block_hbm, block_ref),
                (owner_hbm, owner_ref),
                (sub_hbm, sub_ref),
                (delay_hbm, delay_ref),
                (frac_hbm, frac_ref),
                (taps_hbm, taps_ref),
                (table_hbm, table_ref),
            )
        )
    ]
    for load in loads:
        load.start()
    owners = nchan * nsrc
    ranks = owners // 2
    blocks, block_rows, seg = record.shape
    ntab, ntaps = taps_ref.shape
    pairs = block_ref.shape[0]
    cap = out_slots.shape[2]
    targets = sums.shape[0]
    half = seg // nsrc
    late = PARTS - ranks
    step_rows = block_rows // PARTS
    rows = blocks * step_rows
    unit = pairs * step_rows
    lanes = 128
    chip = lax.axis_index("chan")
    core = lax.axis_index("src")
    mate = 1 - core
    tm = lax.axis_index("tm")
    me = chip * nsrc + core
    middle = jnp.logical_and(chip > 0, chip < nchan - 1)
    ending = jnp.logical_or(chip == 0, chip == nchan - 1)
    low_half = chip < nchan // 2
    outer = jnp.where(low_half, 0, nchan - 1)
    inner = jnp.where(low_half, 1, nchan - 2)
    other = nchan - 1 - inner
    far = nchan - 1 - outer
    rank = jnp.where(ending, 0, nsrc) + core

    def near_place(k):
        return {"chan": outer if k < nsrc else inner, "src": k % nsrc}

    def far_place(k):
        return {"chan": far if k < nsrc else other, "src": k % nsrc}

    at_mate = {"src": mate}

    barrier = pltpu.get_barrier_semaphore()

    def greet(place):
        pl.semaphore_signal(barrier, inc=1, device_id=place, device_id_type=MESH)

    @pl.when(tm > 0)
    def _():
        greet({"tm": tm - 1})

    @pl.when(tm < ntm - 1)
    def _():
        greet({"tm": tm + 1})

    def others(do):
        for k in range(ranks):

            @pl.when(rank != k)
            def _():
                do(k)

    others(lambda k: greet(near_place(k)))

    for f in range(ranks):
        greet(far_place(f))

    def part(r):
        return pl.ds(pl.multiple_of(r * step_rows, step_rows), step_rows)

    @pl.when(tm == 0)
    def _():
        prev_in[...] = jnp.zeros_like(prev_in)
        far_prev[...] = jnp.zeros_like(far_prev)

    @pl.when(tm == ntm - 1)
    def _():
        after_in[...] = jnp.zeros_like(after_in)
        far_after[...] = jnp.zeros_like(far_after)

    loads[0].wait()
    for i in range(PARTS):
        r = (i + ranks) % PARTS
        raw[r] = record[:, part(r), :].astype(jnp.bfloat16)

    pl.semaphore_wait(
        barrier,
        owners - 1
        + jnp.where(tm > 0, 1, 0)
        + jnp.where(tm < ntm - 1, 1, 0),
    )

    def tail(ref, r):
        return ref.at[r, :, :, pl.ds(seg - ntaps, ntaps)]

    def to_prev(r):
        return copy_to(
            tail(raw, r), prev_in.at[r], prev_send.at[r], prev_recv.at[r], {"tm": tm + 1}
        )

    def to_after(r):
        return copy_to(
            raw.at[r], after_in.at[r], after_send.at[r], after_recv.at[r], {"tm": tm - 1}
        )

    def far_to_prev(s):
        return copy_to(
            tail(far_raw, s),
            far_prev.at[s],
            far_prev_send.at[s],
            far_prev_recv.at[s],
            {"tm": tm + 1},
        )

    def far_to_after(s):
        return copy_to(
            far_raw.at[s],
            far_after.at[s],
            far_after_send.at[s],
            far_after_recv.at[s],
            {"tm": tm - 1},
        )

    def raw_to(f, landing):
        return copy_to(
            raw.at[f], far_raw.at[landing], raw_send.at[f], raw_recv.at[landing], far_place(f)
        )

    def meta_to(k, landing):
        place = near_place(k) if k < ranks else far_place(k - ranks)
        return copy_to(
            out_meta.at[k], in_meta.at[landing], meta_send.at[k], meta_recv.at[landing], place
        )

    def pairs_to(k, h, landing, place):
        return copy_to(
            out_pairs.at[h, k],
            in_pairs.at[h, landing],
            pair_send.at[h, k],
            pair_recv.at[h, landing],
            place,
        )

    def slots_to(k, r, landing, place):
        return copy_to(
            out_slots.at[r, k],
            in_slots.at[r, landing],
            slot_send.at[r, k],
            slot_recv.at[r, landing],
            place,
        )

    def local_to(h):
        return copy_to(
            out_local.at[h, mate], in_local.at[h], local_send.at[h], local_recv.at[h], at_mate
        )

    def dense_to(k, h, landing):
        return copy_to(
            out_dense.at[h, k],
            in_dense.at[h, landing],
            dense_send.at[h, k],
            dense_recv.at[h, landing],
            far_place(k),
        )

    def near_to(k, landing):
        return copy_to(
            out_near.at[k], in_near.at[landing], near_send.at[k], near_recv.at[landing], near_place(k)
        )

    def halo(r):
        @pl.when(tm > 0)
        def _():
            to_after(r).start()

        @pl.when(tm < ntm - 1)
        def _():
            to_prev(r).start()

    def cross():
        for f in range(ranks):
            raw_to(f, rank).start()
            meta_to(ranks + f, ranks + rank).start()

    for i in range(ranks):
        halo(ranks + i)
        raw_to(i, rank).start()

    for i in range(ranks):
        halo(i)

    for load in loads[1:]:
        load.wait()
    lane = lax.broadcasted_iota(jnp.int32, (8, lanes), 1)
    own_numbers = jnp.zeros((8, lanes), jnp.int32)
    own_names = jnp.zeros((8, lanes), jnp.int32)
    for p in range(pairs):
        name = owner_ref[p] * targets + sub_ref[p]
        own_names = jnp.where(lane // step_rows == p, name, own_names)
        for k, ref in enumerate((block_ref, delay_ref, frac_ref)):
            own_numbers = jnp.where(lane == k * pairs + p, ref[p], own_numbers)
    slot_pair = []
    for k in range(ranks):
        owner = (outer if k < nsrc else inner) * nsrc + k % nsrc
        count = 0
        found = [-1] * cap
        for p in range(pairs):
            hit = owner_ref[p] == owner
            found = [jnp.where(jnp.logical_and(hit, count == j), p, found[j]) for j in range(cap)]
            count = count + jnp.where(hit, 1, 0)
        labels = jnp.full((8, lanes), -1, jnp.int32)
        for j in range(cap):
            pair = jnp.maximum(found[j], 0)
            slot_pair.append(pair)
            name = jnp.where(found[j] >= 0, sub_ref[pair], -1)
            labels = jnp.where(lane // step_rows % cap == j, name, labels)
        out_meta[k, 3:4, :] = labels[0:1]
    for f in range(ranks):
        tables = jnp.zeros((8, lanes), jnp.int32)
        for g in range(blocks):
            row = jnp.broadcast_to(table_ref[g : g + 1, :], (8, lanes))
            row = pltpu.roll(row, (g - f) * step_rows % lanes, 1)
            tables = jnp.where(lane // step_rows == g, row, tables)
        out_meta[ranks + f, 1:2, :] = tables[0:1]
        out_meta[f, 1:2, :] = own_names[0:1]
        out_meta[ranks + f, 3:4, :] = own_names[0:1]
    for k in range(owners):
        out_meta[k, 0:1, :] = own_numbers[0:1]
        out_meta[k, 2:3, :] = own_names[0:1]
    in_meta[rank] = out_meta[rank]
    others(lambda k: meta_to(k, rank).start())

    for f in range(ranks):
        meta_to(ranks + f, ranks + rank).start()

    depth = 2 * ntaps
    build_band(taps_ref, band.at[depth : 2 * depth, :], band.at[:depth, :])
    band[2 * depth :, :] = band[depth : 2 * depth, :]
    for g in range(blocks):
        tab[g] = jnp.broadcast_to(table_ref[g : g + 1, :], (block_rows, block_rows)).T
    step = lax.broadcasted_iota(jnp.int32, weight.shape, 0)
    value = jnp.zeros(weight.shape, jnp.float32)
    for k, rule in enumerate(lagrange((step // 4).astype(jnp.float32) / NFRAC)):
        value = jnp.where(step % 4 == k, rule, value)
    weight[...] = value

    def filter_part(before, high, low, behind, which):
        @pl.when(tm < ntm - 1)
        def _():
            filter_steps(before, high, low, behind, which, 2 * seg // ntaps)

        @pl.when(tm == ntm - 1)
        def _():
            filter_steps(before, high, low, behind, which, seg // ntaps)

    def filter_steps(before, high, low, behind, which, steps):

        def stack(window):
            return jnp.concatenate(
                [window[:, j * ntaps : (j + 2) * ntaps] for j in range(steps)], axis=0
            )

        lhs_hi = stack(jnp.concatenate([before, high, behind], axis=1))
        lhs = [lhs_hi, lhs_hi]
        if low is not None:
            none = jnp.zeros_like(before)
            lhs.append(stack(jnp.concatenate([none, low, none, none], axis=1)))
        every = mm(jnp.concatenate(lhs, axis=1), band[: len(lhs) * 2 * ntaps, :])
        pieces = []
        for j in range(steps):
            own = every[j * rows : (j + 1) * rows]
            value = own[:, :ntaps]
            for m in range(1, ntab):
                value = jnp.where(which == m, own[:, m * ntaps : (m + 1) * ntaps], value)
            pieces.append(value)
        if steps * ntaps < 2 * seg:
            pieces.append(jnp.zeros((rows, 2 * seg - steps * ntaps), jnp.float32))
        whole = jnp.concatenate(pieces, axis=1)
        for k in range(4):
            moved = whole if k == 0 else pltpu.roll(whole, 2 * seg - k, 1)
            filt[k] = moved.reshape(blocks, step_rows, 2 * seg)

    def shift_one(source, delay, frac):
        line = frac * 4
        mixed = []
        for j in range(2 * seg // lanes):
            cols = slice(j * lanes, (j + 1) * lanes)
            total = weight[pl.ds(line, 1), :] * filt[0, source, :, cols]
            for k in range(1, 4):
                total = total + weight[pl.ds(line + k, 1), :] * filt[k, source, :, cols]
            mixed.append(total)
        moved = pltpu.roll(jnp.concatenate(mixed, axis=1), 2 * seg - (delay - 1), 1)
        return moved[:, :seg].astype(jnp.bfloat16)

    def filter_own(r):
        @pl.when(tm > 0)
        def _():
            to_prev(r).wait_recv()

        @pl.when(tm < ntm - 1)
        def _():
            to_after(r).wait_recv()

        high, low = split(record[:, part(r), :].reshape(rows, seg))
        which = tab[:, part(r), :].reshape(rows, block_rows)
        filter_part(
            prev_in[r].reshape(rows, ntaps), high, low, after_in[r].reshape(rows, seg), which
        )

    def fill_slots(r, k):
        for j in range(cap):
            out_slots[r, k, j] = shifted[slot_pair[k * cap + j]]

    def keep_slots(r):
        for k in range(ranks):

            @pl.when(rank == k)
            def _():
                for j in range(cap):
                    in_slots[r, k, j] = shifted[slot_pair[k * cap + j]]

    def produce_late(h, carry):
        r = ranks + h

        filter_own(r)

        def one_pair(p, c):
            moved = shift_one(block_ref[p], delay_ref[p], frac_ref[p])
            shifted[p] = moved
            for k in range(nsrc):
                out_pairs[h, k, p] = moved[:, k * half : (k + 1) * half]
            in_pairs[h, rank, p] = jnp.where(core == 0, moved[:, :half], moved[:, half:])
            return c

        lax.fori_loop(0, pairs, one_pair, 0, unroll=pairs)

        @pl.when(ending)
        def _():
            for k in range(nsrc):
                pairs_to(k, h, rank, near_place(nsrc + k)).start()

        @pl.when(middle)
        def _():
            pairs_to(mate, h, rank, at_mate).start()

        for k in range(nsrc):
            fill_slots(r, k)

        @pl.when(ending)
        def _():
            slots_to(mate, r, rank, at_mate).start()
            keep_slots(r)

        @pl.when(middle)
        def _():
            for k in range(nsrc):
                slots_to(k, r, rank, near_place(k)).start()

        return carry

    def produce_early(r):
        filter_own(r)

        def one_pair(p, c):
            shifted[p] = shift_one(block_ref[p], delay_ref[p], frac_ref[p])
            return c

        lax.fori_loop(0, pairs, one_pair, 0, unroll=pairs)
        for k in range(ranks):
            fill_slots(r, k)
        others(lambda k: slots_to(k, r, rank, near_place(k)).start())
        keep_slots(r)

    def forward(s):
        raw_to(0, s).wait_recv()

        @pl.when(tm > 0)
        def _():
            far_to_after(s).start()

        @pl.when(tm < ntm - 1)
        def _():
            far_to_prev(s).start()

    def produce_far(s):
        @pl.when(tm > 0)
        def _():
            far_to_prev(s).wait_recv()

        @pl.when(tm < ntm - 1)
        def _():
            far_to_after(s).wait_recv()

        filter_part(
            far_prev[s].reshape(rows, ntaps),
            far_raw[s].reshape(rows, seg),
            None,
            far_after[s].reshape(rows, seg),
            far_tab[s],
        )

        def one_pair(p, c):
            source, delay, frac = (numbers[s, 0, k * pairs + p] for k in range(3))
            far_pairs[s, p] = shift_one(source, delay, frac)
            return c

        lax.fori_loop(0, pairs, one_pair, 0, unroll=pairs)

    def dense(h):
        others(lambda s: pairs_to(0, h, s, at_mate).wait_recv())
        total = mm(pick[...], in_pairs[h].reshape(ranks * unit, half))
        total = total.reshape(3 * nsrc, targets, step_rows, half)
        for k in range(2 * nsrc):
            out_dense[h, k] = total[k].astype(jnp.bfloat16)
            dense_to(k, h, core).start()
        for k in range(nsrc):
            out_local[h, k] = total[2 * nsrc + k]
        local_to(h).start()

    lax.fori_loop(0, late, produce_late, 0)

    spot = lax.broadcasted_iota(jnp.int32, (unit, unit), 0)
    line = lax.broadcasted_iota(jnp.int32, (unit, unit), 1)
    diagonal = spot % step_rows == line % step_rows

    def fill(ref, i, kind, chan, names):
        hit = jnp.logical_and(chan * nsrc * targets + spot // step_rows == names, diagonal)
        ref[i * unit : (i + 1) * unit, kind * unit : (kind + 1) * unit] = jnp.where(
            hit, 1.0, 0.0
        ).astype(jnp.bfloat16)

    for s in range(ranks):
        meta_to(ranks, ranks + s).wait_recv()
    move = pltpu.make_async_copy(in_meta.at[pl.ds(ranks, ranks)], numbers, number_sem)
    move.start()
    others(lambda k: meta_to(0, k).wait_recv())

    @pl.when(middle)
    def _():
        for i, chan in enumerate((far, other, chip)):
            for kind in range(ranks):
                fill(pick, i, kind, chan, in_meta[kind, 2:3, :])

    labels = in_meta[0, 3:4, :]
    for kind in range(1, ranks):
        labels = jnp.where(
            lane[0:1] // (cap * step_rows) == kind, in_meta[kind, 3:4, :], labels
        )
    hit = jnp.logical_and(spot // step_rows == labels, diagonal)
    pick_slots[...] = jnp.where(hit, 1.0, 0.0).astype(jnp.bfloat16)[: targets * step_rows]

    def early_step(i, carry):
        forward((i + nsrc) % ranks)
        produce_early(i)

        @pl.when(jnp.logical_and(middle, i >= LAG))
        def _():
            dense(i - LAG)

        return carry

    lax.fori_loop(0, ranks, early_step, 0)

    for s in range(ranks):
        far_tab[s] = jnp.broadcast_to(in_meta[ranks + s, 1:2, :], (lanes, lanes)).T[:rows]
        for i, chan in enumerate((outer, inner)):
            fill(pick_far, i, s, chan, in_meta[ranks + s, 2:3, :])
    move.wait()

    def far_step(i, carry):
        produce_far((i + nsrc) % ranks)

        @pl.when(jnp.logical_and(middle, i < LAG))
        def _():
            dense(late - LAG + i)

        return carry

    lax.fori_loop(0, ranks, far_step, 0)
    total = mm(pick_far[...], far_pairs[...].reshape(ranks * unit, seg))
    total = total.reshape(ranks, targets, step_rows, seg)
    for k in range(ranks):
        out_near[k] = total[k].astype(jnp.bfloat16)
    others(lambda k: near_to(k, rank).start())
    in_near[rank] = out_near[rank]

    others(lambda k: meta_to(k, rank).wait_send())
    for f in range(ranks):
        meta_to(ranks + f, ranks + rank).wait_send()
        raw_to(f, rank).wait_send()

    def leave(r, carry):
        @pl.when(tm > 0)
        def _():
            to_after(r).wait_send()

        @pl.when(tm < ntm - 1)
        def _():
            to_prev(r).wait_send()

        return carry

    lax.fori_loop(0, PARTS, leave, 0)

    def leave_early(r, carry):
        others(lambda k: slots_to(k, r, rank, near_place(k)).wait_send())

        @pl.when(tm > 0)
        def _():
            far_to_after(r).wait_send()

        @pl.when(tm < ntm - 1)
        def _():
            far_to_prev(r).wait_send()

        return carry

    lax.fori_loop(0, ranks, leave_early, 0)

    def leave_late(h, carry):
        @pl.when(ending)
        def _():
            for k in range(nsrc):
                pairs_to(k, h, rank, near_place(nsrc + k)).wait_send()
            slots_to(mate, ranks + h, rank, at_mate).wait_send()

        @pl.when(middle)
        def _():
            pairs_to(mate, h, rank, at_mate).wait_send()
            for k in range(nsrc):
                slots_to(k, ranks + h, rank, near_place(k)).wait_send()

        return carry

    lax.fori_loop(0, late, leave_late, 0)

    def store(r, b, value):
        high, low = split(value)
        sums[b, part(r), :] = high
        sums[b, pl.ds(pl.multiple_of(block_rows + r * step_rows, step_rows), step_rows), :] = low

    def from_slots(r):
        others(lambda s: slots_to(0, r, s, at_mate).wait_recv())
        return mm(pick_slots[...], in_slots[r].reshape(ranks * cap * step_rows, seg))

    def slots_first(r, carry):
        near_sum[r] = from_slots(r)
        return carry

    lax.fori_loop(0, ranks, slots_first, 0)

    def finish_late(h, carry):
        r = ranks + h

        @pl.when(ending)
        def _():
            total = from_slots(r)
            for k in range(nsrc):
                dense_to(0, h, k).wait_recv()
            for b in range(targets):
                added = jnp.concatenate([in_dense[h, k, b] for k in range(nsrc)], axis=1)
                store(
                    r, b, total[b * step_rows : (b + 1) * step_rows] + added.astype(jnp.float32)
                )

        @pl.when(middle)
        def _():
            local_to(h).wait_recv()
            for k in range(nsrc):
                dense_to(0, h, k).wait_recv()
            for b in range(targets):
                mine, theirs = out_local[h, core, b], in_local[h, b]
                total = jnp.concatenate(
                    [jnp.where(core == k, mine, theirs) for k in range(nsrc)], axis=1
                )
                added = jnp.concatenate([in_dense[h, k, b] for k in range(nsrc)], axis=1)
                store(r, b, total + added.astype(jnp.float32))

        return carry

    lax.fori_loop(0, late, finish_late, 0)

    def finish_early(r, carry):
        @pl.when(rank != r)
        def _():
            near_to(0, r).wait_recv()

        for b in range(targets):
            store(
                r,
                b,
                near_sum[r, b * step_rows : (b + 1) * step_rows, :]
                + in_near[r, b].astype(jnp.float32),
            )
        return carry

    lax.fori_loop(0, ranks, finish_early, 0)

    others(lambda k: near_to(k, rank).wait_send())

    @pl.when(middle)
    def _():
        for h in range(late):
            for k in range(2 * nsrc):
                dense_to(k, h, core).wait_send()
            local_to(h).wait_send()

def lagrange(mu):
    return (
        -mu * (mu - 1.0) * (mu - 2.0) / 6.0,
        (mu + 1.0) * (mu - 1.0) * (mu - 2.0) / 2.0,
        -(mu + 1.0) * mu * (mu - 2.0) / 2.0,
        (mu + 1.0) * mu * (mu - 1.0) / 6.0,
    )


def steer_kernel(steer_ref, sums, beam_ref, held, done):
    points = steer_ref.shape[1]
    sends = []
    for b in range(sums.shape[0]):
        rows = pl.ds(b * points, points)
        twice = jnp.concatenate([steer_ref[b], steer_ref[b]], axis=1)
        held[rows, :] = mm(twice, sums[b])
        send = pltpu.make_async_copy(held.at[rows, :], beam_ref.at[rows, :], done.at[b])
        send.start()
        sends.append(send)
    for send in sends:
        send.wait()


def build_band(taps_ref, band_hi, band_lo):
    ntab, ntaps = taps_ref.shape
    for m in range(ntab):
        row = jnp.concatenate([taps_ref[m : m + 1, :], jnp.zeros((1, ntaps), jnp.float32)], axis=1)
        full = jnp.broadcast_to(row, (2 * ntaps, 2 * ntaps))
        rolled = pltpu.roll(full, ntaps, 1, stride=1, stride_axis=0)[:, :ntaps]
        high, low = split(rolled)
        band_hi[:, m * ntaps : (m + 1) * ntaps] = high
        band_lo[:, m * ntaps : (m + 1) * ntaps] = low


def band_filter(window, band_hi, band_lo, which, inside, seg, ntab, filt):
    blocks, step_rows, _ = filt.shape
    rows = blocks * step_rows
    ntaps = band_hi.shape[0] // 2
    high, low = split(window)
    steps = 2 * seg // ntaps
    lhs_hi = jnp.concatenate([high[:, j * ntaps : (j + 2) * ntaps] for j in range(steps)], axis=0)
    lhs_lo = jnp.concatenate([low[:, j * ntaps : (j + 2) * ntaps] for j in range(steps)], axis=0)
    every = mm(lhs_lo, band_hi[...]) + mm(lhs_hi, band_lo[...]) + mm(lhs_hi, band_hi[...])
    for j in range(steps):
        own = every[j * rows : (j + 1) * rows]
        value = own[:, :ntaps]
        for m in range(1, ntab):
            value = jnp.where(which == m, own[:, m * ntaps : (m + 1) * ntaps], value)
        if j >= seg // ntaps:
            value = value * inside
        filt[:, :, j * ntaps : (j + 1) * ntaps] = value.reshape(blocks, step_rows, ntaps)


def shift_pair(source, delay, frac, seg):
    mu = jnp.full((1, seg), frac.astype(jnp.float32)) / NFRAC
    first = -mu * (mu - 1.0) * (mu - 2.0) / 6.0
    second = (mu + 1.0) * (mu - 1.0) * (mu - 2.0) / 2.0
    third = -(mu + 1.0) * mu * (mu - 2.0) / 2.0
    fourth = (mu + 1.0) * mu * (mu - 1.0) / 6.0
    base = pltpu.roll(source, 2 * seg - (delay - 1), 1)
    mixed = first * base[:, :seg]
    mixed = mixed + second * pltpu.roll(base, 2 * seg - 1, 1)[:, :seg]
    mixed = mixed + third * pltpu.roll(base, 2 * seg - 2, 1)[:, :seg]
    mixed = mixed + fourth * pltpu.roll(base, 2 * seg - 3, 1)[:, :seg]
    return mixed.astype(jnp.bfloat16)


def solution(mesh):
    nchan, nsrc, ntm = mesh.shape["chan"], mesh.shape["src"], mesh.shape["tm"]
    owners = nchan * nsrc

    def local(
        record, fir_taps, chan_table, steering, pair_block, pair_owner, pair_sub, pair_delay, pair_frac
    ):
        channels, seg = record.shape
        ntab, ntaps = fir_taps.shape
        targets, points, block_rows = steering.shape
        blocks = channels // block_rows
        pairs = pair_block.shape[0]
        cap = 2 * pairs // owners
        step_rows = block_rows // GROUPS
        smem = pl.BlockSpec(memory_space=pltpu.SMEM)
        vmem = pl.BlockSpec(memory_space=pltpu.VMEM)
        dma = pltpu.SemaphoreType.DMA
        operands = (
            pair_block,
            pair_owner.reshape(pairs),
            pair_sub,
            pair_delay,
            pair_frac,
            record.reshape(blocks, block_rows, seg),
            fir_taps,
            chan_table.reshape(blocks, block_rows),
            steering,
        )
        unit = pairs * block_rows // PARTS
        square = unit == 128 and pairs == nsrc * targets and cap * (2 * nsrc) == pairs
        if nchan == 4 and nsrc == 2 and square:
            step_rows = block_rows // PARTS
            half = seg // nsrc
            ranks = owners // 2
            late = PARTS - ranks
            whole = (blocks, step_rows, seg)
            edge = (blocks, step_rows, ntaps)
            bf16, f32, i32 = jnp.bfloat16, jnp.float32, jnp.int32
            held = pltpu.VMEM
            sums = pl.pallas_call(
                functools.partial(line_kernel, (nchan, nsrc, ntm)),
                out_shape=pltpu.VMEM((targets, 2 * block_rows, seg), bf16),
                in_specs=[pl.BlockSpec(memory_space=pltpu.HBM)] * 8,
                out_specs=vmem,
                scratch_shapes=[
                    *[pltpu.SMEM((pairs,), i32)] * 5,
                    held((blocks, block_rows, seg), f32),
                    held((ntab, ntaps), f32),
                    held((blocks, block_rows), i32),
                    held((PARTS, *whole), bf16),
                    held((PARTS, *edge), bf16),
                    held((PARTS, *whole), bf16),
                    held((ranks, *whole), bf16),
                    held((ranks, *edge), bf16),
                    held((ranks, *whole), bf16),
                    held((6 * ntaps, ntab * ntaps), bf16),
                    held((blocks, block_rows, block_rows), i32),
                    held((ranks, blocks * step_rows, 128), i32),
                    held((NFRAC * 4, 128), f32),
                    held((4, blocks, step_rows, 2 * seg), f32),
                    held((pairs, step_rows, seg), bf16),
                    held((ranks, pairs, step_rows, seg), bf16),
                    held((late, nsrc, pairs, step_rows, half), bf16),
                    held((late, ranks, pairs, step_rows, half), bf16),
                    held((PARTS, ranks, cap, step_rows, seg), bf16),
                    held((PARTS, ranks, cap, step_rows, seg), bf16),
                    held((owners, 4, 128), i32),
                    held((owners, 4, 128), i32),
                    pltpu.SMEM((ranks, 4, 128), i32),
                    held((3 * unit, ranks * unit), bf16),
                    held((targets * step_rows, unit), bf16),
                    held((nsrc * unit, ranks * unit), bf16),
                    held((late, nsrc, targets, step_rows, half), f32),
                    held((late, targets, step_rows, half), f32),
                    held((late, ranks, targets, step_rows, half), bf16),
                    held((late, nsrc, targets, step_rows, half), bf16),
                    held((ranks, targets, step_rows, seg), bf16),
                    held((ranks, targets, step_rows, seg), bf16),
                    held((ranks, targets * step_rows, seg), f32),
                    dma((PARTS,)),
                    dma((PARTS,)),
                    dma((PARTS,)),
                    dma((PARTS,)),
                    dma((ranks,)),
                    dma((ranks,)),
                    dma((ranks,)),
                    dma((ranks,)),
                    dma((ranks,)),
                    dma((ranks,)),
                    dma((late, nsrc)),
                    dma((late, ranks)),
                    dma((PARTS, ranks)),
                    dma((PARTS, ranks)),
                    dma((owners,)),
                    dma((owners,)),
                    dma((late,)),
                    dma((late,)),
                    dma((late, ranks)),
                    dma((late, nsrc)),
                    dma((ranks,)),
                    dma((ranks,)),
                    dma,
                    pltpu.SemaphoreType.REGULAR,
                    dma((8,)),
                ],
                compiler_params=pltpu.CompilerParams(collective_id=0, has_side_effects=True),
            )(*operands[:-1])
            return pl.pallas_call(
                steer_kernel,
                out_shape=jax.ShapeDtypeStruct((targets * points, seg), f32),
                in_specs=[vmem] * 2,
                out_specs=pl.BlockSpec(memory_space=pl.ANY),
                scratch_shapes=[held((targets * points, seg), f32), dma((targets,))],
                compiler_params=pltpu.CompilerParams(vmem_limit_bytes=16 << 20),
            )(steering, sums)
        return pl.pallas_call(
            functools.partial(kernel, (nchan, nsrc, ntm)),
            out_shape=jax.ShapeDtypeStruct((targets * points, seg), jnp.float32),
            in_specs=[smem] * 5 + [vmem] * 4,
            out_specs=vmem,
            scratch_shapes=[
                pltpu.VMEM((blocks, block_rows, ntaps), jnp.float32),
                pltpu.VMEM((blocks, block_rows, seg), jnp.float32),
                pltpu.VMEM((2 * ntaps, ntab * ntaps), jnp.bfloat16),
                pltpu.VMEM((2 * ntaps, ntab * ntaps), jnp.bfloat16),
                pltpu.VMEM((blocks, block_rows, block_rows), jnp.int32),
                pltpu.VMEM((blocks, step_rows, 2 * seg), jnp.float32),
                pltpu.VMEM((pairs, step_rows, seg), jnp.bfloat16),
                pltpu.VMEM((owners, cap, block_rows, seg), jnp.bfloat16),
                pltpu.VMEM((owners, cap, block_rows, seg), jnp.bfloat16),
                pltpu.VMEM((owners, 8, 128), jnp.float32),
                pltpu.VMEM((owners, 8, 128), jnp.float32),
                pltpu.VMEM((targets, block_rows, seg), jnp.float32),
                pltpu.SMEM((owners * cap,), jnp.int32),
                dma((GROUPS,)),
                dma((GROUPS,)),
                dma((GROUPS,)),
                dma((GROUPS,)),
                dma((GROUPS, owners)),
                dma((GROUPS, owners)),
                dma((owners,)),
                dma((owners,)),
            ],
            compiler_params=pltpu.CompilerParams(collective_id=0, has_side_effects=True),
        )(*operands)

    in_specs = (
        P(("groups", "chan", "src"), "tm"),
        P(),
        P(("chan", "src")),
        P(("chan", "src"), None, None),
        P(("chan", "src")),
        P(("chan", "src"), None),
        P(("chan", "src")),
        P(("chan", "src")),
        P(("chan", "src")),
    )
    out_specs = P(("groups", "chan", "src"), "tm")
    return jax.shard_map(local, mesh=mesh, in_specs=in_specs, out_specs=out_specs, check_vma=False)
```

```python
import functools

import jax
import jax.numpy as jnp
from jax import lax
from jax.experimental import pallas as pl
from jax.experimental.pallas import tpu as pltpu
from jax.sharding import PartitionSpec as P

NFRAC = 16
GROUPS = 4
PARTS = 8
LAG = 1
MESH = pl.DeviceIdType.MESH


def split(value):
    high = value.astype(jnp.bfloat16)
    return high, (value - high.astype(jnp.float32)).astype(jnp.bfloat16)


def mm(a, b):
    return jnp.dot(a, b, preferred_element_type=jnp.float32)


def kernel(
    dims,
    block_ref,
    owner_ref,
    sub_ref,
    delay_ref,
    frac_ref,
    record,
    taps_ref,
    table_ref,
    steer_ref,
    beam_ref,
    prev,
    after,
    band_hi,
    band_lo,
    tab,
    filt,
    shifted,
    out_slots,
    in_slots,
    out_label,
    in_label,
    sums,
    slot_pair,
    prev_send,
    prev_recv,
    after_send,
    after_recv,
    slot_send,
    slot_recv,
    label_send,
    label_recv,
):
    nchan, nsrc, ntm = dims
    owners = nchan * nsrc
    blocks, block_rows, seg = record.shape
    ntab, ntaps = taps_ref.shape
    pairs = block_ref.shape[0]
    cap = out_slots.shape[1]
    targets = steer_ref.shape[0]
    points = steer_ref.shape[1]
    step_rows = block_rows // GROUPS
    rows = blocks * step_rows
    me = lax.axis_index("chan") * nsrc + lax.axis_index("src")
    tm = lax.axis_index("tm")

    def place(owner):
        return {"chan": owner // nsrc, "src": owner % nsrc}

    barrier = pltpu.get_barrier_semaphore()

    @pl.when(tm > 0)
    def _():
        pl.semaphore_signal(barrier, inc=1, device_id={"tm": tm - 1}, device_id_type=MESH)

    @pl.when(tm < ntm - 1)
    def _():
        pl.semaphore_signal(barrier, inc=1, device_id={"tm": tm + 1}, device_id_type=MESH)

    def greet(i, carry):
        pl.semaphore_signal(
            barrier, inc=1, device_id=place((me + i) % owners), device_id_type=MESH
        )
        return carry

    lax.fori_loop(1, owners, greet, 0)

    build_band(taps_ref, band_hi, band_lo)

    @pl.when(tm == 0)
    def _():
        prev[...] = jnp.zeros_like(prev)

    @pl.when(tm == ntm - 1)
    def _():
        after[...] = jnp.zeros_like(after)

    pl.semaphore_wait(
        barrier,
        owners - 1 + jnp.where(tm > 0, 1, 0) + jnp.where(tm < ntm - 1, 1, 0),
    )

    def part(r):
        return pl.ds(pl.multiple_of(r * step_rows, step_rows), step_rows)

    def to_prev(r):
        return pltpu.make_async_remote_copy(
            src_ref=record.at[:, part(r), pl.ds(seg - ntaps, ntaps)],
            dst_ref=prev.at[:, part(r), :],
            send_sem=prev_send.at[r],
            recv_sem=prev_recv.at[r],
            device_id={"tm": tm + 1},
            device_id_type=MESH,
        )

    def to_after(r):
        return pltpu.make_async_remote_copy(
            src_ref=record.at[:, part(r), :],
            dst_ref=after.at[:, part(r), :],
            send_sem=after_send.at[r],
            recv_sem=after_recv.at[r],
            device_id={"tm": tm - 1},
            device_id_type=MESH,
        )

    def slots_to(r, other, landing):
        return pltpu.make_async_remote_copy(
            src_ref=out_slots.at[other, :, part(r), :],
            dst_ref=in_slots.at[landing, :, part(r), :],
            send_sem=slot_send.at[r, other],
            recv_sem=slot_recv.at[r, landing],
            device_id=place(other),
            device_id_type=MESH,
        )

    def label_to(other, landing):
        return pltpu.make_async_remote_copy(
            src_ref=out_label.at[other],
            dst_ref=in_label.at[landing],
            send_sem=label_send.at[other],
            recv_sem=label_recv.at[landing],
            device_id=place(other),
            device_id_type=MESH,
        )

    for r in range(GROUPS):

        @pl.when(tm > 0)
        def _():
            to_after(r).start()

        @pl.when(tm < ntm - 1)
        def _():
            to_prev(r).start()

    for g in range(blocks):
        tab[g] = jnp.broadcast_to(table_ref[g : g + 1, :], (block_rows, block_rows)).T

    def slots_of(owner, carry):
        def look(p, found):
            hit = owner_ref[p] == owner
            count = found[0]
            named = [
                jnp.where(jnp.logical_and(hit, count == k), p, found[1 + k]) for k in range(cap)
            ]
            return (count + jnp.where(hit, 1, 0), *named)

        found = lax.fori_loop(0, pairs, look, (0,) + (-1,) * cap, unroll=min(pairs, 8))
        line = lax.broadcasted_iota(jnp.int32, out_label.shape[1:], 0)
        labels = jnp.full(out_label.shape[1:], -1.0, jnp.float32)
        for k in range(cap):
            pair = jnp.maximum(found[1 + k], 0)
            slot_pair[owner * cap + k] = pair
            name = jnp.where(found[1 + k] >= 0, sub_ref[pair], -1).astype(jnp.float32)
            labels = jnp.where(line == k, name, labels)
        out_label[owner] = labels
        return carry

    lax.fori_loop(0, owners, slots_of, 0)

    def send_label(i, carry):
        label_to((me + i) % owners, me).start()
        return carry

    lax.fori_loop(1, owners, send_label, 0)

    def produce(r, carry):
        @pl.when(tm > 0)
        def _():
            to_prev(r).wait_recv()

        @pl.when(tm < ntm - 1)
        def _():
            to_after(r).wait_recv()

        window = jnp.concatenate(
            [
                prev[:, part(r), :].reshape(rows, ntaps),
                record[:, part(r), :].reshape(rows, seg),
                after[:, part(r), :].reshape(rows, seg),
            ],
            axis=1,
        )
        inside = jnp.where(tm < ntm - 1, 1.0, 0.0)
        which = tab[:, part(r), :].reshape(rows, block_rows)
        band_filter(window, band_hi, band_lo, which, inside, seg, ntab, filt)

        def one_pair(p, c):
            shifted[p] = shift_pair(filt[block_ref[p]], delay_ref[p], frac_ref[p], seg)
            return c

        lax.fori_loop(0, pairs, one_pair, 0, unroll=pairs)

        def ship(i, c):
            other = (me + owners // 2 + i) % owners
            for k in range(cap):
                out_slots[other, k, part(r), :] = shifted[slot_pair[other * cap + k]]

            @pl.when(other != me)
            def _():
                slots_to(r, other, me).start()

            return c

        lax.fori_loop(0, owners, ship, 0)
        return carry

    lax.fori_loop(0, GROUPS, produce, 0)

    def wait_label(i, carry):
        source = (me + i) % owners
        label_to(source, source).wait_recv()
        return carry

    lax.fori_loop(1, owners, wait_label, 0)

    def add(total, values, labels):
        for k in range(cap):
            name = jnp.concatenate([labels[k : k + 1, :]] * (seg // labels.shape[1]), axis=1)
            value = values[k].astype(jnp.float32)
            total = [
                total[b] + value * jnp.where(name == float(b), 1.0, 0.0) for b in range(targets)
            ]
        return total

    def gather(r, carry):
        total = [jnp.zeros((step_rows, seg), jnp.float32)] * targets
        total = add(total, out_slots[me, :, part(r), :], out_label[me])

        def one_source(i, running):
            source = (me + i) % owners
            slots_to(r, source, source).wait_recv()
            return tuple(add(list(running), in_slots[source, :, part(r), :], in_label[source]))

        total = lax.fori_loop(1, owners, one_source, tuple(total))
        for b in range(targets):
            sums[b, part(r), :] = total[b]
        return carry

    lax.fori_loop(0, GROUPS, gather, 0)

    for b in range(targets):
        high, low = split(sums[b])
        beam_ref[b * points : (b + 1) * points, :] = mm(steer_ref[b], high) + mm(steer_ref[b], low)

    def finish(i, carry):
        other = (me + i) % owners
        label_to(other, me).wait_send()
        for r in range(GROUPS):
            slots_to(r, other, me).wait_send()
        return carry

    lax.fori_loop(1, owners, finish, 0)
    for r in range(GROUPS):

        @pl.when(tm > 0)
        def _():
            to_after(r).wait_send()

        @pl.when(tm < ntm - 1)
        def _():
            to_prev(r).wait_send()


def copy_to(source, target, send, receive, place):
    return pltpu.make_async_remote_copy(
        src_ref=source,
        dst_ref=target,
        send_sem=send,
        recv_sem=receive,
        device_id=place,
        device_id_type=MESH,
    )


def line_kernel(
    dims,
    block_hbm,
    owner_hbm,
    sub_hbm,
    delay_hbm,
    frac_hbm,
    record_hbm,
    taps_hbm,
    table_hbm,
    sums,
    block_ref,
    owner_ref,
    sub_ref,
    delay_ref,
    frac_ref,
    record,
    taps_ref,
    table_ref,
    raw,
    prev_in,
    after_in,
    far_raw,
    far_prev,
    far_after,
    band,
    tab,
    far_tab,
    weight,
    filt,
    shifted,
    far_pairs,
    out_pairs,
    in_pairs,
    out_slots,
    in_slots,
    out_meta,
    in_meta,
    numbers,
    pick,
    pick_slots,
    pick_far,
    out_local,
    in_local,
    out_dense,
    in_dense,
    out_near,
    in_near,
    near_sum,
    prev_send,
    prev_recv,
    after_send,
    after_recv,
    raw_send,
    raw_recv,
    far_prev_send,
    far_prev_recv,
    far_after_send,
    far_after_recv,
    pair_send,
    pair_recv,
    slot_send,
    slot_recv,
    meta_send,
    meta_recv,
    local_send,
    local_recv,
    dense_send,
    dense_recv,
    near_send,
    near_recv,
    number_sem,
    ready,
    load_sem,
):
    nchan, nsrc, ntm = dims
    loads = [
        pltpu.make_async_copy(source, target, load_sem.at[i])
        for i, (source, target) in enumerate(
            (
                (record_hbm, record),
                (block_hbm, block_ref),
                (owner_hbm, owner_ref),
                (sub_hbm, sub_ref),
                (delay_hbm, delay_ref),
                (frac_hbm, frac_ref),
                (taps_hbm, taps_ref),
                (table_hbm, table_ref),
            )
        )
    ]
    for load in loads:
        load.start()
    owners = nchan * nsrc
    ranks = owners // 2
    blocks, block_rows, seg = record.shape
    ntab, ntaps = taps_ref.shape
    pairs = block_ref.shape[0]
    cap = out_slots.shape[2]
    targets = sums.shape[0]
    half = seg // nsrc
    late = PARTS - ranks
    step_rows = block_rows // PARTS
    rows = blocks * step_rows
    unit = pairs * step_rows
    lanes = 128
    chip = lax.axis_index("chan")
    core = lax.axis_index("src")
    mate = 1 - core
    tm = lax.axis_index("tm")
    me = chip * nsrc + core
    middle = jnp.logical_and(chip > 0, chip < nchan - 1)
    ending = jnp.logical_or(chip == 0, chip == nchan - 1)
    low_half = chip < nchan // 2
    outer = jnp.where(low_half, 0, nchan - 1)
    inner = jnp.where(low_half, 1, nchan - 2)
    other = nchan - 1 - inner
    far = nchan - 1 - outer
    rank = jnp.where(ending, 0, nsrc) + core

    def near_place(k):
        return {"chan": outer if k < nsrc else inner, "src": k % nsrc}

    def far_place(k):
        return {"chan": far if k < nsrc else other, "src": k % nsrc}

    at_mate = {"src": mate}

    barrier = pltpu.get_barrier_semaphore()

    def greet(place):
        pl.semaphore_signal(barrier, inc=1, device_id=place, device_id_type=MESH)

    @pl.when(tm > 0)
    def _():
        greet({"tm": tm - 1})

    @pl.when(tm < ntm - 1)
    def _():
        greet({"tm": tm + 1})

    def others(do):
        for k in range(ranks):

            @pl.when(rank != k)
            def _():
                do(k)

    others(lambda k: greet(near_place(k)))

    for f in range(ranks):
        greet(far_place(f))

    def part(r):
        return pl.ds(pl.multiple_of(r * step_rows, step_rows), step_rows)

    @pl.when(tm == 0)
    def _():
        prev_in[...] = jnp.zeros_like(prev_in)
        far_prev[...] = jnp.zeros_like(far_prev)

    @pl.when(tm == ntm - 1)
    def _():
        after_in[...] = jnp.zeros_like(after_in)
        far_after[...] = jnp.zeros_like(far_after)

    loads[0].wait()
    def narrow(r):
        raw[r] = record[:, part(r), :].astype(jnp.bfloat16)

    narrow(ranks)
    narrow(0)

    for load in loads[1:]:
        load.wait()
    lane = lax.broadcasted_iota(jnp.int32, (8, lanes), 1)
    own_numbers = jnp.zeros((8, lanes), jnp.int32)
    own_names = jnp.zeros((8, lanes), jnp.int32)
    for p in range(pairs):
        name = owner_ref[p] * targets + sub_ref[p]
        own_names = jnp.where(lane // step_rows == p, name, own_names)
        for k, ref in enumerate((block_ref, delay_ref, frac_ref)):
            own_numbers = jnp.where(lane == k * pairs + p, ref[p], own_numbers)
    slot_pair = []
    for k in range(ranks):
        owner = (outer if k < nsrc else inner) * nsrc + k % nsrc
        count = 0
        found = [-1] * cap
        for p in range(pairs):
            hit = owner_ref[p] == owner
            found = [jnp.where(jnp.logical_and(hit, count == j), p, found[j]) for j in range(cap)]
            count = count + jnp.where(hit, 1, 0)
        labels = jnp.full((8, lanes), -1, jnp.int32)
        for j in range(cap):
            pair = jnp.maximum(found[j], 0)
            slot_pair.append(pair)
            name = jnp.where(found[j] >= 0, sub_ref[pair], -1)
            labels = jnp.where(lane // step_rows % cap == j, name, labels)
        out_meta[k, 3:4, :] = labels[0:1]
    for f in range(ranks):
        tables = jnp.zeros((8, lanes), jnp.int32)
        for g in range(blocks):
            row = jnp.broadcast_to(table_ref[g : g + 1, :], (8, lanes))
            row = pltpu.roll(row, (g - f) * step_rows % lanes, 1)
            tables = jnp.where(lane // step_rows == g, row, tables)
        out_meta[ranks + f, 1:2, :] = tables[0:1]
        out_meta[f, 1:2, :] = own_names[0:1]
        out_meta[ranks + f, 3:4, :] = own_names[0:1]
    for k in range(owners):
        out_meta[k, 0:1, :] = own_numbers[0:1]
        out_meta[k, 2:3, :] = own_names[0:1]
    in_meta[rank] = out_meta[rank]

    pl.semaphore_wait(
        barrier,
        owners - 1
        + jnp.where(tm > 0, 1, 0)
        + jnp.where(tm < ntm - 1, 1, 0),
    )

    def tail(ref, r):
        return ref.at[r, :, :, pl.ds(seg - ntaps, ntaps)]

    def to_prev(r):
        return copy_to(
            tail(raw, r), prev_in.at[r], prev_send.at[r], prev_recv.at[r], {"tm": tm + 1}
        )

    def to_after(r):
        return copy_to(
            raw.at[r], after_in.at[r], after_send.at[r], after_recv.at[r], {"tm": tm - 1}
        )

    def far_to_prev(s):
        return copy_to(
            tail(far_raw, s),
            far_prev.at[s],
            far_prev_send.at[s],
            far_prev_recv.at[s],
            {"tm": tm + 1},
        )

    def far_to_after(s):
        return copy_to(
            far_raw.at[s],
            far_after.at[s],
            far_after_send.at[s],
            far_after_recv.at[s],
            {"tm": tm - 1},
        )

    def raw_to(f, landing):
        return copy_to(
            raw.at[f], far_raw.at[landing], raw_send.at[f], raw_recv.at[landing], far_place(f)
        )

    def meta_to(k, landing):
        place = near_place(k) if k < ranks else far_place(k - ranks)
        return copy_to(
            out_meta.at[k], in_meta.at[landing], meta_send.at[k], meta_recv.at[landing], place
        )

    def pairs_to(k, h, landing, place):
        return copy_to(
            out_pairs.at[h, k],
            in_pairs.at[h, landing],
            pair_send.at[h, k],
            pair_recv.at[h, landing],
            place,
        )

    def slots_to(k, r, landing, place):
        return copy_to(
            out_slots.at[r, k],
            in_slots.at[r, landing],
            slot_send.at[r, k],
            slot_recv.at[r, landing],
            place,
        )

    def local_to(h):
        return copy_to(
            out_local.at[h, mate], in_local.at[h], local_send.at[h], local_recv.at[h], at_mate
        )

    def dense_to(k, h, landing):
        return copy_to(
            out_dense.at[h, k],
            in_dense.at[h, landing],
            dense_send.at[h, k],
            dense_recv.at[h, landing],
            far_place(k),
        )

    def near_to(k, landing):
        return copy_to(
            out_near.at[k], in_near.at[landing], near_send.at[k], near_recv.at[landing], near_place(k)
        )

    def halo(r):
        @pl.when(tm > 0)
        def _():
            to_after(r).start()

        @pl.when(tm < ntm - 1)
        def _():
            to_prev(r).start()

    def cross():
        for f in range(ranks):
            raw_to(f, rank).start()
            meta_to(ranks + f, ranks + rank).start()

    halo(ranks)
    others(lambda k: meta_to(k, rank).start())

    for f in range(ranks):
        meta_to(ranks + f, ranks + rank).start()

    for i in range(ranks):
        if i > 0:
            narrow(ranks + i)
            narrow(i)
        if i > 0:
            halo(ranks + i)

        @pl.when(ending)
        def _():
            raw_to(i, rank).start()


    for i in range(ranks):
        halo(i)


    @pl.when(middle)
    def _():
        for f in range(ranks):
            raw_to(f, rank).start()

    depth = 2 * ntaps
    build_band(taps_ref, band.at[depth : 2 * depth, :], band.at[:depth, :])
    band[2 * depth :, :] = band[depth : 2 * depth, :]
    for g in range(blocks):
        tab[g] = jnp.broadcast_to(table_ref[g : g + 1, :], (block_rows, block_rows)).T
    step = lax.broadcasted_iota(jnp.int32, weight.shape, 0)
    value = jnp.zeros(weight.shape, jnp.float32)
    for k, rule in enumerate(lagrange((step // 4).astype(jnp.float32) / NFRAC)):
        value = jnp.where(step % 4 == k, rule, value)
    weight[...] = value

    def filter_part(before, high, low, behind, which):
        @pl.when(tm < ntm - 1)
        def _():
            filter_steps(before, high, low, behind, which, 2 * seg // ntaps)

        @pl.when(tm == ntm - 1)
        def _():
            filter_steps(before, high, low, behind, which, seg // ntaps)

    def filter_steps(before, high, low, behind, which, steps):

        def stack(window):
            return jnp.concatenate(
                [window[:, j * ntaps : (j + 2) * ntaps] for j in range(steps)], axis=0
            )

        lhs_hi = stack(jnp.concatenate([before, high, behind], axis=1))
        lhs = [lhs_hi, lhs_hi]
        if low is not None:
            none = jnp.zeros_like(before)
            lhs.append(stack(jnp.concatenate([none, low, none, none], axis=1)))
        every = mm(jnp.concatenate(lhs, axis=1), band[: len(lhs) * 2 * ntaps, :])
        pieces = []
        for j in range(steps):
            own = every[j * rows : (j + 1) * rows]
            value = own[:, :ntaps]
            for m in range(1, ntab):
                value = jnp.where(which == m, own[:, m * ntaps : (m + 1) * ntaps], value)
            pieces.append(value)
        if steps * ntaps < 2 * seg:
            pieces.append(jnp.zeros((rows, 2 * seg - steps * ntaps), jnp.float32))
        whole = jnp.concatenate(pieces, axis=1)
        for k in range(4):
            moved = whole if k == 0 else pltpu.roll(whole, 2 * seg - k, 1)
            filt[k] = moved.reshape(blocks, step_rows, 2 * seg)

    def shift_one(source, delay, frac):
        line = frac * 4
        mixed = []
        for j in range(2 * seg // lanes):
            cols = slice(j * lanes, (j + 1) * lanes)
            total = weight[pl.ds(line, 1), :] * filt[0, source, :, cols]
            for k in range(1, 4):
                total = total + weight[pl.ds(line + k, 1), :] * filt[k, source, :, cols]
            mixed.append(total)
        moved = pltpu.roll(jnp.concatenate(mixed, axis=1), 2 * seg - (delay - 1), 1)
        return moved[:, :seg].astype(jnp.bfloat16)

    def filter_own(r):
        @pl.when(tm > 0)
        def _():
            to_prev(r).wait_recv()

        @pl.when(tm < ntm - 1)
        def _():
            to_after(r).wait_recv()

        high, low = split(record[:, part(r), :].reshape(rows, seg))
        which = tab[:, part(r), :].reshape(rows, block_rows)
        filter_part(
            prev_in[r].reshape(rows, ntaps), high, low, after_in[r].reshape(rows, seg), which
        )

    def fill_slots(r, k):
        for j in range(cap):
            out_slots[r, k, j] = shifted[slot_pair[k * cap + j]]

    def keep_slots(r):
        for k in range(ranks):

            @pl.when(rank == k)
            def _():
                for j in range(cap):
                    in_slots[r, k, j] = shifted[slot_pair[k * cap + j]]

    def produce_late(h, carry):
        r = ranks + h

        filter_own(r)

        def one_pair(p, c):
            moved = shift_one(block_ref[p], delay_ref[p], frac_ref[p])
            shifted[p] = moved
            for k in range(nsrc):
                out_pairs[h, k, p] = moved[:, k * half : (k + 1) * half]
            in_pairs[h, rank, p] = jnp.where(core == 0, moved[:, :half], moved[:, half:])
            return c

        lax.fori_loop(0, pairs, one_pair, 0, unroll=pairs)

        @pl.when(ending)
        def _():
            for k in range(nsrc):
                pairs_to(k, h, rank, near_place(nsrc + k)).start()

        @pl.when(middle)
        def _():
            pairs_to(mate, h, rank, at_mate).start()

        for k in range(nsrc):
            fill_slots(r, k)

        @pl.when(ending)
        def _():
            slots_to(mate, r, rank, at_mate).start()
            keep_slots(r)

        @pl.when(middle)
        def _():
            for k in range(nsrc):
                slots_to(k, r, rank, near_place(k)).start()

        return carry

    def produce_early(r):
        filter_own(r)

        def one_pair(p, c):
            shifted[p] = shift_one(block_ref[p], delay_ref[p], frac_ref[p])
            return c

        lax.fori_loop(0, pairs, one_pair, 0, unroll=pairs)
        for k in range(ranks):
            fill_slots(r, k)
        others(lambda k: slots_to(k, r, rank, near_place(k)).start())
        keep_slots(r)

    def forward(s):
        raw_to(0, s).wait_recv()

        @pl.when(tm > 0)
        def _():
            far_to_after(s).start()

        @pl.when(tm < ntm - 1)
        def _():
            far_to_prev(s).start()

    def produce_far(s):
        @pl.when(tm > 0)
        def _():
            far_to_prev(s).wait_recv()

        @pl.when(tm < ntm - 1)
        def _():
            far_to_after(s).wait_recv()

        filter_part(
            far_prev[s].reshape(rows, ntaps),
            far_raw[s].reshape(rows, seg),
            None,
            far_after[s].reshape(rows, seg),
            far_tab[s],
        )

        def one_pair(p, c):
            source, delay, frac = (numbers[s, 0, k * pairs + p] for k in range(3))
            far_pairs[s, p] = shift_one(source, delay, frac)
            return c

        lax.fori_loop(0, pairs, one_pair, 0, unroll=pairs)

    def dense(h):
        others(lambda s: pairs_to(0, h, s, at_mate).wait_recv())
        total = mm(pick[...], in_pairs[h].reshape(ranks * unit, half))
        total = total.reshape(3 * nsrc, targets, step_rows, half)
        for k in range(2 * nsrc):
            out_dense[h, k] = total[k].astype(jnp.bfloat16)
            dense_to(k, h, core).start()
        for k in range(nsrc):
            out_local[h, k] = total[2 * nsrc + k]
        local_to(h).start()

    lax.fori_loop(0, late, produce_late, 0)

    spot = lax.broadcasted_iota(jnp.int32, (unit, unit), 0)
    line = lax.broadcasted_iota(jnp.int32, (unit, unit), 1)
    diagonal = spot % step_rows == line % step_rows

    def fill(ref, i, kind, chan, names):
        hit = jnp.logical_and(chan * nsrc * targets + spot // step_rows == names, diagonal)
        ref[i * unit : (i + 1) * unit, kind * unit : (kind + 1) * unit] = jnp.where(
            hit, 1.0, 0.0
        ).astype(jnp.bfloat16)

    for s in range(ranks):
        meta_to(ranks, ranks + s).wait_recv()
    move = pltpu.make_async_copy(in_meta.at[pl.ds(ranks, ranks)], numbers, number_sem)
    move.start()
    others(lambda k: meta_to(0, k).wait_recv())

    @pl.when(middle)
    def _():
        for i, chan in enumerate((far, other, chip)):
            for kind in range(ranks):
                fill(pick, i, kind, chan, in_meta[kind, 2:3, :])

    labels = in_meta[0, 3:4, :]
    for kind in range(1, ranks):
        labels = jnp.where(
            lane[0:1] // (cap * step_rows) == kind, in_meta[kind, 3:4, :], labels
        )
    hit = jnp.logical_and(spot // step_rows == labels, diagonal)
    pick_slots[...] = jnp.where(hit, 1.0, 0.0).astype(jnp.bfloat16)[: targets * step_rows]

    def early_step(i, carry):
        forward(i)
        produce_early(i)

        @pl.when(jnp.logical_and(middle, jnp.logical_and(i >= 1, i < ranks - 1)))
        def _():
            dense(i - 1)

        return carry

    lax.fori_loop(0, ranks, early_step, 0)

    for s in range(ranks):
        far_tab[s] = jnp.broadcast_to(in_meta[ranks + s, 1:2, :], (lanes, lanes)).T[:rows]
        for i, chan in enumerate((outer, inner)):
            fill(pick_far, i, s, chan, in_meta[ranks + s, 2:3, :])
    move.wait()

    def far_step(i, carry):
        produce_far(i)

        @pl.when(jnp.logical_and(middle, i % 2 == 0))
        def _():
            dense(late - 2 + i // 2)

        return carry

    lax.fori_loop(0, ranks, far_step, 0)
    total = mm(pick_far[...], far_pairs[...].reshape(ranks * unit, seg))
    total = total.reshape(ranks, targets, step_rows, seg)
    for k in range(ranks):
        out_near[k] = total[k].astype(jnp.bfloat16)
    others(lambda k: near_to(k, rank).start())
    in_near[rank] = out_near[rank]

    others(lambda k: meta_to(k, rank).wait_send())
    for f in range(ranks):
        meta_to(ranks + f, ranks + rank).wait_send()
        raw_to(f, rank).wait_send()

    def leave(r, carry):
        @pl.when(tm > 0)
        def _():
            to_after(r).wait_send()

        @pl.when(tm < ntm - 1)
        def _():
            to_prev(r).wait_send()

        return carry

    lax.fori_loop(0, PARTS, leave, 0)

    def leave_early(r, carry):
        others(lambda k: slots_to(k, r, rank, near_place(k)).wait_send())

        @pl.when(tm > 0)
        def _():
            far_to_after(r).wait_send()

        @pl.when(tm < ntm - 1)
        def _():
            far_to_prev(r).wait_send()

        return carry

    lax.fori_loop(0, ranks, leave_early, 0)

    def leave_late(h, carry):
        @pl.when(ending)
        def _():
            for k in range(nsrc):
                pairs_to(k, h, rank, near_place(nsrc + k)).wait_send()
            slots_to(mate, ranks + h, rank, at_mate).wait_send()

        @pl.when(middle)
        def _():
            pairs_to(mate, h, rank, at_mate).wait_send()
            for k in range(nsrc):
                slots_to(k, ranks + h, rank, near_place(k)).wait_send()

        return carry

    lax.fori_loop(0, late, leave_late, 0)

    def store(r, b, value):
        high, low = split(value)
        sums[b, part(r), :] = high
        sums[b, pl.ds(pl.multiple_of(block_rows + r * step_rows, step_rows), step_rows), :] = low

    def from_slots(r):
        others(lambda s: slots_to(0, r, s, at_mate).wait_recv())
        return mm(pick_slots[...], in_slots[r].reshape(ranks * cap * step_rows, seg))

    def slots_first(r, carry):
        near_sum[r] = from_slots(r)
        return carry

    lax.fori_loop(0, ranks, slots_first, 0)

    def finish_late(h, carry):
        r = ranks + h

        @pl.when(ending)
        def _():
            total = from_slots(r)
            for k in range(nsrc):
                dense_to(0, h, k).wait_recv()
            for b in range(targets):
                added = jnp.concatenate([in_dense[h, k, b] for k in range(nsrc)], axis=1)
                store(
                    r, b, total[b * step_rows : (b + 1) * step_rows] + added.astype(jnp.float32)
                )

        @pl.when(middle)
        def _():
            local_to(h).wait_recv()
            for k in range(nsrc):
                dense_to(0, h, k).wait_recv()
            for b in range(targets):
                mine, theirs = out_local[h, core, b], in_local[h, b]
                total = jnp.concatenate(
                    [jnp.where(core == k, mine, theirs) for k in range(nsrc)], axis=1
                )
                added = jnp.concatenate([in_dense[h, k, b] for k in range(nsrc)], axis=1)
                store(r, b, total + added.astype(jnp.float32))

        return carry

    lax.fori_loop(0, late, finish_late, 0)

    def finish_early(r, carry):
        @pl.when(rank != r)
        def _():
            near_to(0, r).wait_recv()

        for b in range(targets):
            store(
                r,
                b,
                near_sum[r, b * step_rows : (b + 1) * step_rows, :]
                + in_near[r, b].astype(jnp.float32),
            )
        return carry

    lax.fori_loop(0, ranks, finish_early, 0)

    others(lambda k: near_to(k, rank).wait_send())

    @pl.when(middle)
    def _():
        for h in range(late):
            for k in range(2 * nsrc):
                dense_to(k, h, core).wait_send()
            local_to(h).wait_send()

def lagrange(mu):
    return (
        -mu * (mu - 1.0) * (mu - 2.0) / 6.0,
        (mu + 1.0) * (mu - 1.0) * (mu - 2.0) / 2.0,
        -(mu + 1.0) * mu * (mu - 2.0) / 2.0,
        (mu + 1.0) * mu * (mu - 1.0) / 6.0,
    )


def steer_kernel(steer_ref, sums, beam_ref, held, done):
    points = steer_ref.shape[1]
    sends = []
    for b in range(sums.shape[0]):
        rows = pl.ds(b * points, points)
        twice = jnp.concatenate([steer_ref[b], steer_ref[b]], axis=1)
        held[rows, :] = mm(twice, sums[b])
        send = pltpu.make_async_copy(held.at[rows, :], beam_ref.at[rows, :], done.at[b])
        send.start()
        sends.append(send)
    for send in sends:
        send.wait()


def build_band(taps_ref, band_hi, band_lo):
    ntab, ntaps = taps_ref.shape
    for m in range(ntab):
        row = jnp.concatenate([taps_ref[m : m + 1, :], jnp.zeros((1, ntaps), jnp.float32)], axis=1)
        full = jnp.broadcast_to(row, (2 * ntaps, 2 * ntaps))
        rolled = pltpu.roll(full, ntaps, 1, stride=1, stride_axis=0)[:, :ntaps]
        high, low = split(rolled)
        band_hi[:, m * ntaps : (m + 1) * ntaps] = high
        band_lo[:, m * ntaps : (m + 1) * ntaps] = low


def band_filter(window, band_hi, band_lo, which, inside, seg, ntab, filt):
    blocks, step_rows, _ = filt.shape
    rows = blocks * step_rows
    ntaps = band_hi.shape[0] // 2
    high, low = split(window)
    steps = 2 * seg // ntaps
    lhs_hi = jnp.concatenate([high[:, j * ntaps : (j + 2) * ntaps] for j in range(steps)], axis=0)
    lhs_lo = jnp.concatenate([low[:, j * ntaps : (j + 2) * ntaps] for j in range(steps)], axis=0)
    every = mm(lhs_lo, band_hi[...]) + mm(lhs_hi, band_lo[...]) + mm(lhs_hi, band_hi[...])
    for j in range(steps):
        own = every[j * rows : (j + 1) * rows]
        value = own[:, :ntaps]
        for m in range(1, ntab):
            value = jnp.where(which == m, own[:, m * ntaps : (m + 1) * ntaps], value)
        if j >= seg // ntaps:
            value = value * inside
        filt[:, :, j * ntaps : (j + 1) * ntaps] = value.reshape(blocks, step_rows, ntaps)


def shift_pair(source, delay, frac, seg):
    mu = jnp.full((1, seg), frac.astype(jnp.float32)) / NFRAC
    first = -mu * (mu - 1.0) * (mu - 2.0) / 6.0
    second = (mu + 1.0) * (mu - 1.0) * (mu - 2.0) / 2.0
    third = -(mu + 1.0) * mu * (mu - 2.0) / 2.0
    fourth = (mu + 1.0) * mu * (mu - 1.0) / 6.0
    base = pltpu.roll(source, 2 * seg - (delay - 1), 1)
    mixed = first * base[:, :seg]
    mixed = mixed + second * pltpu.roll(base, 2 * seg - 1, 1)[:, :seg]
    mixed = mixed + third * pltpu.roll(base, 2 * seg - 2, 1)[:, :seg]
    mixed = mixed + fourth * pltpu.roll(base, 2 * seg - 3, 1)[:, :seg]
    return mixed.astype(jnp.bfloat16)


def solution(mesh):
    nchan, nsrc, ntm = mesh.shape["chan"], mesh.shape["src"], mesh.shape["tm"]
    owners = nchan * nsrc

    def local(
        record, fir_taps, chan_table, steering, pair_block, pair_owner, pair_sub, pair_delay, pair_frac
    ):
        channels, seg = record.shape
        ntab, ntaps = fir_taps.shape
        targets, points, block_rows = steering.shape
        blocks = channels // block_rows
        pairs = pair_block.shape[0]
        cap = 2 * pairs // owners
        step_rows = block_rows // GROUPS
        smem = pl.BlockSpec(memory_space=pltpu.SMEM)
        vmem = pl.BlockSpec(memory_space=pltpu.VMEM)
        dma = pltpu.SemaphoreType.DMA
        operands = (
            pair_block,
            pair_owner.reshape(pairs),
            pair_sub,
            pair_delay,
            pair_frac,
            record.reshape(blocks, block_rows, seg),
            fir_taps,
            chan_table.reshape(blocks, block_rows),
            steering,
        )
        unit = pairs * block_rows // PARTS
        square = unit == 128 and pairs == nsrc * targets and cap * (2 * nsrc) == pairs
        if nchan == 4 and nsrc == 2 and square:
            step_rows = block_rows // PARTS
            half = seg // nsrc
            ranks = owners // 2
            late = PARTS - ranks
            whole = (blocks, step_rows, seg)
            edge = (blocks, step_rows, ntaps)
            bf16, f32, i32 = jnp.bfloat16, jnp.float32, jnp.int32
            held = pltpu.VMEM
            sums = pl.pallas_call(
                functools.partial(line_kernel, (nchan, nsrc, ntm)),
                out_shape=pltpu.VMEM((targets, 2 * block_rows, seg), bf16),
                in_specs=[pl.BlockSpec(memory_space=pltpu.HBM)] * 8,
                out_specs=vmem,
                scratch_shapes=[
                    *[pltpu.SMEM((pairs,), i32)] * 5,
                    held((blocks, block_rows, seg), f32),
                    held((ntab, ntaps), f32),
                    held((blocks, block_rows), i32),
                    held((PARTS, *whole), bf16),
                    held((PARTS, *edge), bf16),
                    held((PARTS, *whole), bf16),
                    held((ranks, *whole), bf16),
                    held((ranks, *edge), bf16),
                    held((ranks, *whole), bf16),
                    held((6 * ntaps, ntab * ntaps), bf16),
                    held((blocks, block_rows, block_rows), i32),
                    held((ranks, blocks * step_rows, 128), i32),
                    held((NFRAC * 4, 128), f32),
                    held((4, blocks, step_rows, 2 * seg), f32),
                    held((pairs, step_rows, seg), bf16),
                    held((ranks, pairs, step_rows, seg), bf16),
                    held((late, nsrc, pairs, step_rows, half), bf16),
                    held((late, ranks, pairs, step_rows, half), bf16),
                    held((PARTS, ranks, cap, step_rows, seg), bf16),
                    held((PARTS, ranks, cap, step_rows, seg), bf16),
                    held((owners, 4, 128), i32),
                    held((owners, 4, 128), i32),
                    pltpu.SMEM((ranks, 4, 128), i32),
                    held((3 * unit, ranks * unit), bf16),
                    held((targets * step_rows, unit), bf16),
                    held((nsrc * unit, ranks * unit), bf16),
                    held((late, nsrc, targets, step_rows, half), f32),
                    held((late, targets, step_rows, half), f32),
                    held((late, ranks, targets, step_rows, half), bf16),
                    held((late, nsrc, targets, step_rows, half), bf16),
                    held((ranks, targets, step_rows, seg), bf16),
                    held((ranks, targets, step_rows, seg), bf16),
                    held((ranks, targets * step_rows, seg), f32),
                    dma((PARTS,)),
                    dma((PARTS,)),
                    dma((PARTS,)),
                    dma((PARTS,)),
                    dma((ranks,)),
                    dma((ranks,)),
                    dma((ranks,)),
                    dma((ranks,)),
                    dma((ranks,)),
                    dma((ranks,)),
                    dma((late, nsrc)),
                    dma((late, ranks)),
                    dma((PARTS, ranks)),
                    dma((PARTS, ranks)),
                    dma((owners,)),
                    dma((owners,)),
                    dma((late,)),
                    dma((late,)),
                    dma((late, ranks)),
                    dma((late, nsrc)),
                    dma((ranks,)),
                    dma((ranks,)),
                    dma,
                    pltpu.SemaphoreType.REGULAR,
                    dma((8,)),
                ],
                compiler_params=pltpu.CompilerParams(collective_id=0, has_side_effects=True),
            )(*operands[:-1])
            return pl.pallas_call(
                steer_kernel,
                out_shape=jax.ShapeDtypeStruct((targets * points, seg), f32),
                in_specs=[vmem] * 2,
                out_specs=pl.BlockSpec(memory_space=pl.ANY),
                scratch_shapes=[held((targets * points, seg), f32), dma((targets,))],
                compiler_params=pltpu.CompilerParams(vmem_limit_bytes=16 << 20),
            )(steering, sums)
        return pl.pallas_call(
            functools.partial(kernel, (nchan, nsrc, ntm)),
            out_shape=jax.ShapeDtypeStruct((targets * points, seg), jnp.float32),
            in_specs=[smem] * 5 + [vmem] * 4,
            out_specs=vmem,
            scratch_shapes=[
                pltpu.VMEM((blocks, block_rows, ntaps), jnp.float32),
                pltpu.VMEM((blocks, block_rows, seg), jnp.float32),
                pltpu.VMEM((2 * ntaps, ntab * ntaps), jnp.bfloat16),
                pltpu.VMEM((2 * ntaps, ntab * ntaps), jnp.bfloat16),
                pltpu.VMEM((blocks, block_rows, block_rows), jnp.int32),
                pltpu.VMEM((blocks, step_rows, 2 * seg), jnp.float32),
                pltpu.VMEM((pairs, step_rows, seg), jnp.bfloat16),
                pltpu.VMEM((owners, cap, block_rows, seg), jnp.bfloat16),
                pltpu.VMEM((owners, cap, block_rows, seg), jnp.bfloat16),
                pltpu.VMEM((owners, 8, 128), jnp.float32),
                pltpu.VMEM((owners, 8, 128), jnp.float32),
                pltpu.VMEM((targets, block_rows, seg), jnp.float32),
                pltpu.SMEM((owners * cap,), jnp.int32),
                dma((GROUPS,)),
                dma((GROUPS,)),
                dma((GROUPS,)),
                dma((GROUPS,)),
                dma((GROUPS, owners)),
                dma((GROUPS, owners)),
                dma((owners,)),
                dma((owners,)),
            ],
            compiler_params=pltpu.CompilerParams(collective_id=0, has_side_effects=True),
        )(*operands)

    in_specs = (
        P(("groups", "chan", "src"), "tm"),
        P(),
        P(("chan", "src")),
        P(("chan", "src"), None, None),
        P(("chan", "src")),
        P(("chan", "src"), None),
        P(("chan", "src")),
        P(("chan", "src")),
        P(("chan", "src")),
    )
    out_specs = P(("groups", "chan", "src"), "tm")
    return jax.shard_map(local, mesh=mesh, in_specs=in_specs, out_specs=out_specs, check_vma=False)
```

```python
import functools

import jax
import jax.numpy as jnp
from jax import lax
from jax.experimental import pallas as pl
from jax.experimental.pallas import tpu as pltpu
from jax.sharding import PartitionSpec as P

NFRAC = 16
GROUPS = 4
PARTS = 8
LAG = 1
MESH = pl.DeviceIdType.MESH


def split(value):
    high = value.astype(jnp.bfloat16)
    return high, (value - high.astype(jnp.float32)).astype(jnp.bfloat16)


def mm(a, b):
    return jnp.dot(a, b, preferred_element_type=jnp.float32)


def kernel(
    dims,
    block_ref,
    owner_ref,
    sub_ref,
    delay_ref,
    frac_ref,
    record,
    taps_ref,
    table_ref,
    steer_ref,
    beam_ref,
    prev,
    after,
    band_hi,
    band_lo,
    tab,
    filt,
    shifted,
    out_slots,
    in_slots,
    out_label,
    in_label,
    sums,
    slot_pair,
    prev_send,
    prev_recv,
    after_send,
    after_recv,
    slot_send,
    slot_recv,
    label_send,
    label_recv,
):
    nchan, nsrc, ntm = dims
    owners = nchan * nsrc
    blocks, block_rows, seg = record.shape
    ntab, ntaps = taps_ref.shape
    pairs = block_ref.shape[0]
    cap = out_slots.shape[1]
    targets = steer_ref.shape[0]
    points = steer_ref.shape[1]
    step_rows = block_rows // GROUPS
    rows = blocks * step_rows
    me = lax.axis_index("chan") * nsrc + lax.axis_index("src")
    tm = lax.axis_index("tm")

    def place(owner):
        return {"chan": owner // nsrc, "src": owner % nsrc}

    barrier = pltpu.get_barrier_semaphore()

    @pl.when(tm > 0)
    def _():
        pl.semaphore_signal(barrier, inc=1, device_id={"tm": tm - 1}, device_id_type=MESH)

    @pl.when(tm < ntm - 1)
    def _():
        pl.semaphore_signal(barrier, inc=1, device_id={"tm": tm + 1}, device_id_type=MESH)

    def greet(i, carry):
        pl.semaphore_signal(
            barrier, inc=1, device_id=place((me + i) % owners), device_id_type=MESH
        )
        return carry

    lax.fori_loop(1, owners, greet, 0)

    build_band(taps_ref, band_hi, band_lo)

    @pl.when(tm == 0)
    def _():
        prev[...] = jnp.zeros_like(prev)

    @pl.when(tm == ntm - 1)
    def _():
        after[...] = jnp.zeros_like(after)

    pl.semaphore_wait(
        barrier,
        owners - 1 + jnp.where(tm > 0, 1, 0) + jnp.where(tm < ntm - 1, 1, 0),
    )

    def part(r):
        return pl.ds(pl.multiple_of(r * step_rows, step_rows), step_rows)

    def to_prev(r):
        return pltpu.make_async_remote_copy(
            src_ref=record.at[:, part(r), pl.ds(seg - ntaps, ntaps)],
            dst_ref=prev.at[:, part(r), :],
            send_sem=prev_send.at[r],
            recv_sem=prev_recv.at[r],
            device_id={"tm": tm + 1},
            device_id_type=MESH,
        )

    def to_after(r):
        return pltpu.make_async_remote_copy(
            src_ref=record.at[:, part(r), :],
            dst_ref=after.at[:, part(r), :],
            send_sem=after_send.at[r],
            recv_sem=after_recv.at[r],
            device_id={"tm": tm - 1},
            device_id_type=MESH,
        )

    def slots_to(r, other, landing):
        return pltpu.make_async_remote_copy(
            src_ref=out_slots.at[other, :, part(r), :],
            dst_ref=in_slots.at[landing, :, part(r), :],
            send_sem=slot_send.at[r, other],
            recv_sem=slot_recv.at[r, landing],
            device_id=place(other),
            device_id_type=MESH,
        )

    def label_to(other, landing):
        return pltpu.make_async_remote_copy(
            src_ref=out_label.at[other],
            dst_ref=in_label.at[landing],
            send_sem=label_send.at[other],
            recv_sem=label_recv.at[landing],
            device_id=place(other),
            device_id_type=MESH,
        )

    for r in range(GROUPS):

        @pl.when(tm > 0)
        def _():
            to_after(r).start()

        @pl.when(tm < ntm - 1)
        def _():
            to_prev(r).start()

    for g in range(blocks):
        tab[g] = jnp.broadcast_to(table_ref[g : g + 1, :], (block_rows, block_rows)).T

    def slots_of(owner, carry):
        def look(p, found):
            hit = owner_ref[p] == owner
            count = found[0]
            named = [
                jnp.where(jnp.logical_and(hit, count == k), p, found[1 + k]) for k in range(cap)
            ]
            return (count + jnp.where(hit, 1, 0), *named)

        found = lax.fori_loop(0, pairs, look, (0,) + (-1,) * cap, unroll=min(pairs, 8))
        line = lax.broadcasted_iota(jnp.int32, out_label.shape[1:], 0)
        labels = jnp.full(out_label.shape[1:], -1.0, jnp.float32)
        for k in range(cap):
            pair = jnp.maximum(found[1 + k], 0)
            slot_pair[owner * cap + k] = pair
            name = jnp.where(found[1 + k] >= 0, sub_ref[pair], -1).astype(jnp.float32)
            labels = jnp.where(line == k, name, labels)
        out_label[owner] = labels
        return carry

    lax.fori_loop(0, owners, slots_of, 0)

    def send_label(i, carry):
        label_to((me + i) % owners, me).start()
        return carry

    lax.fori_loop(1, owners, send_label, 0)

    def produce(r, carry):
        @pl.when(tm > 0)
        def _():
            to_prev(r).wait_recv()

        @pl.when(tm < ntm - 1)
        def _():
            to_after(r).wait_recv()

        window = jnp.concatenate(
            [
                prev[:, part(r), :].reshape(rows, ntaps),
                record[:, part(r), :].reshape(rows, seg),
                after[:, part(r), :].reshape(rows, seg),
            ],
            axis=1,
        )
        inside = jnp.where(tm < ntm - 1, 1.0, 0.0)
        which = tab[:, part(r), :].reshape(rows, block_rows)
        band_filter(window, band_hi, band_lo, which, inside, seg, ntab, filt)

        def one_pair(p, c):
            shifted[p] = shift_pair(filt[block_ref[p]], delay_ref[p], frac_ref[p], seg)
            return c

        lax.fori_loop(0, pairs, one_pair, 0, unroll=pairs)

        def ship(i, c):
            other = (me + owners // 2 + i) % owners
            for k in range(cap):
                out_slots[other, k, part(r), :] = shifted[slot_pair[other * cap + k]]

            @pl.when(other != me)
            def _():
                slots_to(r, other, me).start()

            return c

        lax.fori_loop(0, owners, ship, 0)
        return carry

    lax.fori_loop(0, GROUPS, produce, 0)

    def wait_label(i, carry):
        source = (me + i) % owners
        label_to(source, source).wait_recv()
        return carry

    lax.fori_loop(1, owners, wait_label, 0)

    def add(total, values, labels):
        for k in range(cap):
            name = jnp.concatenate([labels[k : k + 1, :]] * (seg // labels.shape[1]), axis=1)
            value = values[k].astype(jnp.float32)
            total = [
                total[b] + value * jnp.where(name == float(b), 1.0, 0.0) for b in range(targets)
            ]
        return total

    def gather(r, carry):
        total = [jnp.zeros((step_rows, seg), jnp.float32)] * targets
        total = add(total, out_slots[me, :, part(r), :], out_label[me])

        def one_source(i, running):
            source = (me + i) % owners
            slots_to(r, source, source).wait_recv()
            return tuple(add(list(running), in_slots[source, :, part(r), :], in_label[source]))

        total = lax.fori_loop(1, owners, one_source, tuple(total))
        for b in range(targets):
            sums[b, part(r), :] = total[b]
        return carry

    lax.fori_loop(0, GROUPS, gather, 0)

    for b in range(targets):
        high, low = split(sums[b])
        beam_ref[b * points : (b + 1) * points, :] = mm(steer_ref[b], high) + mm(steer_ref[b], low)

    def finish(i, carry):
        other = (me + i) % owners
        label_to(other, me).wait_send()
        for r in range(GROUPS):
            slots_to(r, other, me).wait_send()
        return carry

    lax.fori_loop(1, owners, finish, 0)
    for r in range(GROUPS):

        @pl.when(tm > 0)
        def _():
            to_after(r).wait_send()

        @pl.when(tm < ntm - 1)
        def _():
            to_prev(r).wait_send()


def copy_to(source, target, send, receive, place):
    return pltpu.make_async_remote_copy(
        src_ref=source,
        dst_ref=target,
        send_sem=send,
        recv_sem=receive,
        device_id=place,
        device_id_type=MESH,
    )


def line_kernel(
    dims,
    block_hbm,
    owner_hbm,
    sub_hbm,
    delay_hbm,
    frac_hbm,
    record_hbm,
    taps_hbm,
    table_hbm,
    sums,
    block_ref,
    owner_ref,
    sub_ref,
    delay_ref,
    frac_ref,
    record,
    taps_ref,
    table_ref,
    raw,
    prev_in,
    after_in,
    far_raw,
    far_prev,
    far_after,
    band,
    tab,
    far_tab,
    weight,
    filt,
    shifted,
    far_pairs,
    out_pairs,
    in_pairs,
    out_slots,
    in_slots,
    out_meta,
    in_meta,
    numbers,
    pick,
    pick_slots,
    pick_far,
    out_local,
    in_local,
    out_dense,
    in_dense,
    out_near,
    in_near,
    near_sum,
    prev_send,
    prev_recv,
    after_send,
    after_recv,
    raw_send,
    raw_recv,
    far_prev_send,
    far_prev_recv,
    far_after_send,
    far_after_recv,
    pair_send,
    pair_recv,
    slot_send,
    slot_recv,
    meta_send,
    meta_recv,
    local_send,
    local_recv,
    dense_send,
    dense_recv,
    near_send,
    near_recv,
    number_sem,
    ready,
    load_sem,
):
    nchan, nsrc, ntm = dims
    loads = [
        pltpu.make_async_copy(source, target, load_sem.at[i])
        for i, (source, target) in enumerate(
            (
                (record_hbm, record),
                (block_hbm, block_ref),
                (owner_hbm, owner_ref),
                (sub_hbm, sub_ref),
                (delay_hbm, delay_ref),
                (frac_hbm, frac_ref),
                (taps_hbm, taps_ref),
                (table_hbm, table_ref),
            )
        )
    ]
    owners = nchan * nsrc
    ranks = owners // 2
    blocks, block_rows, seg = record.shape
    ntab, ntaps = taps_ref.shape
    pairs = block_ref.shape[0]
    cap = out_slots.shape[2]
    targets = sums.shape[0]
    half = seg // nsrc
    late = PARTS - ranks
    step_rows = block_rows // PARTS
    rows = blocks * step_rows
    unit = pairs * step_rows
    lanes = 128
    chip = lax.axis_index("chan")
    core = lax.axis_index("src")
    mate = 1 - core
    tm = lax.axis_index("tm")
    me = chip * nsrc + core
    middle = jnp.logical_and(chip > 0, chip < nchan - 1)
    ending = jnp.logical_or(chip == 0, chip == nchan - 1)
    low_half = chip < nchan // 2
    outer = jnp.where(low_half, 0, nchan - 1)
    inner = jnp.where(low_half, 1, nchan - 2)
    other = nchan - 1 - inner
    far = nchan - 1 - outer
    rank = jnp.where(ending, 0, nsrc) + core

    def near_place(k):
        return {"chan": outer if k < nsrc else inner, "src": k % nsrc}

    def far_place(k):
        return {"chan": far if k < nsrc else other, "src": k % nsrc}

    at_mate = {"src": mate}

    barrier = pltpu.get_barrier_semaphore()

    def greet(place):
        pl.semaphore_signal(barrier, inc=1, device_id=place, device_id_type=MESH)

    for f in range(ranks):
        greet(far_place(f))

    @pl.when(tm > 0)
    def _():
        greet({"tm": tm - 1})

    @pl.when(tm < ntm - 1)
    def _():
        greet({"tm": tm + 1})

    def others(do):
        for k in range(ranks):

            @pl.when(rank != k)
            def _():
                do(k)

    others(lambda k: greet(near_place(k)))

    for load in loads:
        load.start()


    def part(r):
        return pl.ds(pl.multiple_of(r * step_rows, step_rows), step_rows)

    @pl.when(tm == 0)
    def _():
        prev_in[...] = jnp.zeros_like(prev_in)
        far_prev[...] = jnp.zeros_like(far_prev)

    @pl.when(tm == ntm - 1)
    def _():
        after_in[...] = jnp.zeros_like(after_in)
        far_after[...] = jnp.zeros_like(far_after)

    loads[0].wait()
    def narrow(r):
        raw[r] = record[:, part(r), :].astype(jnp.bfloat16)

    narrow(ranks)
    narrow(0)

    for load in loads[1:]:
        load.wait()
    lane = lax.broadcasted_iota(jnp.int32, (8, lanes), 1)
    own_numbers = jnp.zeros((8, lanes), jnp.int32)
    own_names = jnp.zeros((8, lanes), jnp.int32)
    for p in range(pairs):
        name = owner_ref[p] * targets + sub_ref[p]
        own_names = jnp.where(lane // step_rows == p, name, own_names)
        for k, ref in enumerate((block_ref, delay_ref, frac_ref)):
            own_numbers = jnp.where(lane == k * pairs + p, ref[p], own_numbers)
    slot_pair = []
    for k in range(ranks):
        owner = (outer if k < nsrc else inner) * nsrc + k % nsrc
        count = 0
        found = [-1] * cap
        for p in range(pairs):
            hit = owner_ref[p] == owner
            found = [jnp.where(jnp.logical_and(hit, count == j), p, found[j]) for j in range(cap)]
            count = count + jnp.where(hit, 1, 0)
        labels = jnp.full((8, lanes), -1, jnp.int32)
        for j in range(cap):
            pair = jnp.maximum(found[j], 0)
            slot_pair.append(pair)
            name = jnp.where(found[j] >= 0, sub_ref[pair], -1)
            labels = jnp.where(lane // step_rows % cap == j, name, labels)
        out_meta[k, 3:4, :] = labels[0:1]
    for f in range(ranks):
        tables = jnp.zeros((8, lanes), jnp.int32)
        for g in range(blocks):
            row = jnp.broadcast_to(table_ref[g : g + 1, :], (8, lanes))
            row = pltpu.roll(row, (g - f) * step_rows % lanes, 1)
            tables = jnp.where(lane // step_rows == g, row, tables)
        out_meta[ranks + f, 1:2, :] = tables[0:1]
        out_meta[f, 1:2, :] = own_names[0:1]
        out_meta[ranks + f, 3:4, :] = own_names[0:1]
    for k in range(owners):
        out_meta[k, 0:1, :] = own_numbers[0:1]
        out_meta[k, 2:3, :] = own_names[0:1]
    in_meta[rank] = out_meta[rank]

    pl.semaphore_wait(
        barrier,
        owners - 1
        + jnp.where(tm > 0, 1, 0)
        + jnp.where(tm < ntm - 1, 1, 0),
    )

    def tail(ref, r):
        return ref.at[r, :, :, pl.ds(seg - ntaps, ntaps)]

    def to_prev(r):
        return copy_to(
            tail(raw, r), prev_in.at[r], prev_send.at[r], prev_recv.at[r], {"tm": tm + 1}
        )

    def to_after(r):
        return copy_to(
            raw.at[r], after_in.at[r], after_send.at[r], after_recv.at[r], {"tm": tm - 1}
        )

    def far_to_prev(s):
        return copy_to(
            tail(far_raw, s),
            far_prev.at[s],
            far_prev_send.at[s],
            far_prev_recv.at[s],
            {"tm": tm + 1},
        )

    def far_to_after(s):
        return copy_to(
            far_raw.at[s],
            far_after.at[s],
            far_after_send.at[s],
            far_after_recv.at[s],
            {"tm": tm - 1},
        )

    def raw_to(f, landing):
        return copy_to(
            raw.at[f], far_raw.at[landing], raw_send.at[f], raw_recv.at[landing], far_place(f)
        )

    def meta_to(k, landing):
        place = near_place(k) if k < ranks else far_place(k - ranks)
        return copy_to(
            out_meta.at[k], in_meta.at[landing], meta_send.at[k], meta_recv.at[landing], place
        )

    def pairs_to(k, h, landing, place):
        return copy_to(
            out_pairs.at[h, k],
            in_pairs.at[h, landing],
            pair_send.at[h, k],
            pair_recv.at[h, landing],
            place,
        )

    def slots_to(k, r, landing, place):
        return copy_to(
            out_slots.at[r, k],
            in_slots.at[r, landing],
            slot_send.at[r, k],
            slot_recv.at[r, landing],
            place,
        )

    def local_to(h):
        return copy_to(
            out_local.at[h, mate], in_local.at[h], local_send.at[h], local_recv.at[h], at_mate
        )

    def dense_to(k, h, landing):
        return copy_to(
            out_dense.at[h, k],
            in_dense.at[h, landing],
            dense_send.at[h, k],
            dense_recv.at[h, landing],
            far_place(k),
        )

    def near_to(k, landing):
        return copy_to(
            out_near.at[k], in_near.at[landing], near_send.at[k], near_recv.at[landing], near_place(k)
        )

    def halo(r):
        @pl.when(tm > 0)
        def _():
            to_after(r).start()

        @pl.when(tm < ntm - 1)
        def _():
            to_prev(r).start()

    def cross():
        for f in range(ranks):
            raw_to(f, rank).start()
            meta_to(ranks + f, ranks + rank).start()

    halo(ranks)
    others(lambda k: meta_to(k, rank).start())

    for f in range(ranks):
        meta_to(ranks + f, ranks + rank).start()

    for i in range(ranks):
        if i > 0:
            narrow(ranks + i)
            narrow(i)
        if i > 0:
            halo(ranks + i)

        @pl.when(ending)
        def _():
            raw_to(i, rank).start()


    for i in range(ranks):
        halo(i)


    @pl.when(middle)
    def _():
        for f in range(ranks):
            raw_to(f, rank).start()

    depth = 2 * ntaps
    build_band(taps_ref, band.at[depth : 2 * depth, :], band.at[:depth, :])
    band[2 * depth :, :] = band[depth : 2 * depth, :]
    for g in range(blocks):
        tab[g] = jnp.broadcast_to(table_ref[g : g + 1, :], (block_rows, block_rows)).T
    step = lax.broadcasted_iota(jnp.int32, weight.shape, 0)
    value = jnp.zeros(weight.shape, jnp.float32)
    for k, rule in enumerate(lagrange((step // 4).astype(jnp.float32) / NFRAC)):
        value = jnp.where(step % 4 == k, rule, value)
    weight[...] = value

    def filter_part(before, high, low, behind, which):
        @pl.when(tm < ntm - 1)
        def _():
            filter_steps(before, high, low, behind, which, 2 * seg // ntaps)

        @pl.when(tm == ntm - 1)
        def _():
            filter_steps(before, high, low, behind, which, seg // ntaps)

    def filter_steps(before, high, low, behind, which, steps):

        def stack(window):
            return jnp.concatenate(
                [window[:, j * ntaps : (j + 2) * ntaps] for j in range(steps)], axis=0
            )

        lhs_hi = stack(jnp.concatenate([before, high, behind], axis=1))
        lhs = [lhs_hi, lhs_hi]
        if low is not None:
            none = jnp.zeros_like(before)
            lhs.append(stack(jnp.concatenate([none, low, none, none], axis=1)))
        every = mm(jnp.concatenate(lhs, axis=1), band[: len(lhs) * 2 * ntaps, :])
        pieces = []
        for j in range(steps):
            own = every[j * rows : (j + 1) * rows]
            value = own[:, :ntaps]
            for m in range(1, ntab):
                value = jnp.where(which == m, own[:, m * ntaps : (m + 1) * ntaps], value)
            pieces.append(value)
        if steps * ntaps < 2 * seg:
            pieces.append(jnp.zeros((rows, 2 * seg - steps * ntaps), jnp.float32))
        whole = jnp.concatenate(pieces, axis=1)
        for k in range(4):
            moved = whole if k == 0 else pltpu.roll(whole, 2 * seg - k, 1)
            filt[k] = moved.reshape(blocks, step_rows, 2 * seg)

    def shift_one(source, delay, frac):
        line = frac * 4
        mixed = []
        for j in range(2 * seg // lanes):
            cols = slice(j * lanes, (j + 1) * lanes)
            total = weight[pl.ds(line, 1), :] * filt[0, source, :, cols]
            for k in range(1, 4):
                total = total + weight[pl.ds(line + k, 1), :] * filt[k, source, :, cols]
            mixed.append(total)
        moved = pltpu.roll(jnp.concatenate(mixed, axis=1), 2 * seg - (delay - 1), 1)
        return moved[:, :seg].astype(jnp.bfloat16)

    def filter_own(r):
        @pl.when(tm > 0)
        def _():
            to_prev(r).wait_recv()

        @pl.when(tm < ntm - 1)
        def _():
            to_after(r).wait_recv()

        high, low = split(record[:, part(r), :].reshape(rows, seg))
        which = tab[:, part(r), :].reshape(rows, block_rows)
        filter_part(
            prev_in[r].reshape(rows, ntaps), high, low, after_in[r].reshape(rows, seg), which
        )

    def fill_slots(r, k):
        for j in range(cap):
            out_slots[r, k, j] = shifted[slot_pair[k * cap + j]]

    def keep_slots(r):
        for k in range(ranks):

            @pl.when(rank == k)
            def _():
                for j in range(cap):
                    in_slots[r, k, j] = shifted[slot_pair[k * cap + j]]

    def produce_late(h, carry):
        r = ranks + h

        filter_own(r)

        def one_pair(p, c):
            moved = shift_one(block_ref[p], delay_ref[p], frac_ref[p])
            shifted[p] = moved
            for k in range(nsrc):
                out_pairs[h, k, p] = moved[:, k * half : (k + 1) * half]
            in_pairs[h, rank, p] = jnp.where(core == 0, moved[:, :half], moved[:, half:])
            return c

        lax.fori_loop(0, pairs, one_pair, 0, unroll=pairs)

        @pl.when(ending)
        def _():
            for k in range(nsrc):
                pairs_to(k, h, rank, near_place(nsrc + k)).start()

        @pl.when(middle)
        def _():
            pairs_to(mate, h, rank, at_mate).start()

        for k in range(nsrc):
            fill_slots(r, k)

        @pl.when(ending)
        def _():
            slots_to(mate, r, rank, at_mate).start()
            keep_slots(r)

        @pl.when(middle)
        def _():
            for k in range(nsrc):
                slots_to(k, r, rank, near_place(k)).start()

        return carry

    def produce_early(r):
        filter_own(r)

        def one_pair(p, c):
            shifted[p] = shift_one(block_ref[p], delay_ref[p], frac_ref[p])
            return c

        lax.fori_loop(0, pairs, one_pair, 0, unroll=pairs)
        for k in range(ranks):
            fill_slots(r, k)
        others(lambda k: slots_to(k, r, rank, near_place(k)).start())
        keep_slots(r)

    def forward(s):
        raw_to(0, s).wait_recv()

        @pl.when(tm > 0)
        def _():
            far_to_after(s).start()

        @pl.when(tm < ntm - 1)
        def _():
            far_to_prev(s).start()

    def produce_far(s):
        @pl.when(tm > 0)
        def _():
            far_to_prev(s).wait_recv()

        @pl.when(tm < ntm - 1)
        def _():
            far_to_after(s).wait_recv()

        filter_part(
            far_prev[s].reshape(rows, ntaps),
            far_raw[s].reshape(rows, seg),
            None,
            far_after[s].reshape(rows, seg),
            far_tab[s],
        )

        def one_pair(p, c):
            source, delay, frac = (numbers[s, 0, k * pairs + p] for k in range(3))
            far_pairs[s, p] = shift_one(source, delay, frac)
            return c

        lax.fori_loop(0, pairs, one_pair, 0, unroll=pairs)

    def dense(h):
        others(lambda s: pairs_to(0, h, s, at_mate).wait_recv())
        total = mm(pick[...], in_pairs[h].reshape(ranks * unit, half))
        total = total.reshape(3 * nsrc, targets, step_rows, half)
        for k in range(2 * nsrc):
            out_dense[h, k] = total[k].astype(jnp.bfloat16)
            dense_to(k, h, core).start()
        for k in range(nsrc):
            out_local[h, k] = total[2 * nsrc + k]
        local_to(h).start()

    lax.fori_loop(0, late, produce_late, 0)

    spot = lax.broadcasted_iota(jnp.int32, (unit, unit), 0)
    line = lax.broadcasted_iota(jnp.int32, (unit, unit), 1)
    diagonal = spot % step_rows == line % step_rows

    def fill(ref, i, kind, chan, names):
        hit = jnp.logical_and(chan * nsrc * targets + spot // step_rows == names, diagonal)
        ref[i * unit : (i + 1) * unit, kind * unit : (kind + 1) * unit] = jnp.where(
            hit, 1.0, 0.0
        ).astype(jnp.bfloat16)

    for s in range(ranks):
        meta_to(ranks, ranks + s).wait_recv()
    move = pltpu.make_async_copy(in_meta.at[pl.ds(ranks, ranks)], numbers, number_sem)
    move.start()
    others(lambda k: meta_to(0, k).wait_recv())

    @pl.when(middle)
    def _():
        for i, chan in enumerate((far, other, chip)):
            for kind in range(ranks):
                fill(pick, i, kind, chan, in_meta[kind, 2:3, :])

    labels = in_meta[0, 3:4, :]
    for kind in range(1, ranks):
        labels = jnp.where(
            lane[0:1] // (cap * step_rows) == kind, in_meta[kind, 3:4, :], labels
        )
    hit = jnp.logical_and(spot // step_rows == labels, diagonal)
    pick_slots[...] = jnp.where(hit, 1.0, 0.0).astype(jnp.bfloat16)[: targets * step_rows]

    def early_step(i, carry):
        forward(i)
        produce_early(i)

        @pl.when(jnp.logical_and(middle, i % 2 == 1))
        def _():
            dense(i // 2)

        return carry

    lax.fori_loop(0, ranks, early_step, 0)

    for s in range(ranks):
        far_tab[s] = jnp.broadcast_to(in_meta[ranks + s, 1:2, :], (lanes, lanes)).T[:rows]
        for i, chan in enumerate((outer, inner)):
            fill(pick_far, i, s, chan, in_meta[ranks + s, 2:3, :])
    move.wait()

    def far_step(i, carry):
        produce_far(i)

        @pl.when(jnp.logical_and(middle, i % 2 == 0))
        def _():
            dense(late - 2 + i // 2)

        return carry

    lax.fori_loop(0, ranks, far_step, 0)
    everyone = far_pairs[...].reshape(ranks * unit, seg)
    for k in range(ranks):
        own_rows = targets * step_rows
        total = mm(pick_far[k * own_rows : (k + 1) * own_rows, :], everyone)
        out_near[k] = total.reshape(targets, step_rows, seg).astype(jnp.bfloat16)

        @pl.when(rank != k)
        def _():
            near_to(k, rank).start()

    in_near[rank] = out_near[rank]

    others(lambda k: meta_to(k, rank).wait_send())
    for f in range(ranks):
        meta_to(ranks + f, ranks + rank).wait_send()
        raw_to(f, rank).wait_send()

    def leave(r, carry):
        @pl.when(tm > 0)
        def _():
            to_after(r).wait_send()

        @pl.when(tm < ntm - 1)
        def _():
            to_prev(r).wait_send()

        return carry

    lax.fori_loop(0, PARTS, leave, 0)

    def leave_early(r, carry):
        others(lambda k: slots_to(k, r, rank, near_place(k)).wait_send())

        @pl.when(tm > 0)
        def _():
            far_to_after(r).wait_send()

        @pl.when(tm < ntm - 1)
        def _():
            far_to_prev(r).wait_send()

        return carry

    lax.fori_loop(0, ranks, leave_early, 0)

    def leave_late(h, carry):
        @pl.when(ending)
        def _():
            for k in range(nsrc):
                pairs_to(k, h, rank, near_place(nsrc + k)).wait_send()
            slots_to(mate, ranks + h, rank, at_mate).wait_send()

        @pl.when(middle)
        def _():
            pairs_to(mate, h, rank, at_mate).wait_send()
            for k in range(nsrc):
                slots_to(k, ranks + h, rank, near_place(k)).wait_send()

        return carry

    lax.fori_loop(0, late, leave_late, 0)

    def store(r, b, value):
        high, low = split(value)
        sums[b, part(r), :] = high
        sums[b, pl.ds(pl.multiple_of(block_rows + r * step_rows, step_rows), step_rows), :] = low

    def from_slots(r):
        others(lambda s: slots_to(0, r, s, at_mate).wait_recv())
        return mm(pick_slots[...], in_slots[r].reshape(ranks * cap * step_rows, seg))

    def slots_first(r, carry):
        near_sum[r] = from_slots(r)
        return carry

    lax.fori_loop(0, ranks, slots_first, 0)

    def finish_late(h, carry):
        r = ranks + h

        @pl.when(ending)
        def _():
            total = from_slots(r)
            for k in range(nsrc):
                dense_to(0, h, k).wait_recv()
            for b in range(targets):
                added = jnp.concatenate([in_dense[h, k, b] for k in range(nsrc)], axis=1)
                store(
                    r, b, total[b * step_rows : (b + 1) * step_rows] + added.astype(jnp.float32)
                )

        @pl.when(middle)
        def _():
            local_to(h).wait_recv()
            for k in range(nsrc):
                dense_to(0, h, k).wait_recv()
            for b in range(targets):
                mine, theirs = out_local[h, core, b], in_local[h, b]
                total = jnp.concatenate(
                    [jnp.where(core == k, mine, theirs) for k in range(nsrc)], axis=1
                )
                added = jnp.concatenate([in_dense[h, k, b] for k in range(nsrc)], axis=1)
                store(r, b, total + added.astype(jnp.float32))

        return carry

    lax.fori_loop(0, late, finish_late, 0)

    def finish_early(r, carry):
        @pl.when(rank != r)
        def _():
            near_to(0, r).wait_recv()

        for b in range(targets):
            store(
                r,
                b,
                near_sum[r, b * step_rows : (b + 1) * step_rows, :]
                + in_near[r, b].astype(jnp.float32),
            )
        return carry

    lax.fori_loop(0, ranks, finish_early, 0)

    others(lambda k: near_to(k, rank).wait_send())

    @pl.when(middle)
    def _():
        for h in range(late):
            for k in range(2 * nsrc):
                dense_to(k, h, core).wait_send()
            local_to(h).wait_send()

def lagrange(mu):
    return (
        -mu * (mu - 1.0) * (mu - 2.0) / 6.0,
        (mu + 1.0) * (mu - 1.0) * (mu - 2.0) / 2.0,
        -(mu + 1.0) * mu * (mu - 2.0) / 2.0,
        (mu + 1.0) * mu * (mu - 1.0) / 6.0,
    )


def steer_kernel(steer_ref, sums, beam_ref, held, done):
    points = steer_ref.shape[1]
    sends = []
    for b in range(sums.shape[0]):
        rows = pl.ds(b * points, points)
        twice = jnp.concatenate([steer_ref[b], steer_ref[b]], axis=1)
        held[rows, :] = mm(twice, sums[b])
        send = pltpu.make_async_copy(held.at[rows, :], beam_ref.at[rows, :], done.at[b])
        send.start()
        sends.append(send)
    for send in sends:
        send.wait()


def build_band(taps_ref, band_hi, band_lo):
    ntab, ntaps = taps_ref.shape
    for m in range(ntab):
        row = jnp.concatenate([taps_ref[m : m + 1, :], jnp.zeros((1, ntaps), jnp.float32)], axis=1)
        full = jnp.broadcast_to(row, (2 * ntaps, 2 * ntaps))
        rolled = pltpu.roll(full, ntaps, 1, stride=1, stride_axis=0)[:, :ntaps]
        high, low = split(rolled)
        band_hi[:, m * ntaps : (m + 1) * ntaps] = high
        band_lo[:, m * ntaps : (m + 1) * ntaps] = low


def band_filter(window, band_hi, band_lo, which, inside, seg, ntab, filt):
    blocks, step_rows, _ = filt.shape
    rows = blocks * step_rows
    ntaps = band_hi.shape[0] // 2
    high, low = split(window)
    steps = 2 * seg // ntaps
    lhs_hi = jnp.concatenate([high[:, j * ntaps : (j + 2) * ntaps] for j in range(steps)], axis=0)
    lhs_lo = jnp.concatenate([low[:, j * ntaps : (j + 2) * ntaps] for j in range(steps)], axis=0)
    every = mm(lhs_lo, band_hi[...]) + mm(lhs_hi, band_lo[...]) + mm(lhs_hi, band_hi[...])
    for j in range(steps):
        own = every[j * rows : (j + 1) * rows]
        value = own[:, :ntaps]
        for m in range(1, ntab):
            value = jnp.where(which == m, own[:, m * ntaps : (m + 1) * ntaps], value)
        if j >= seg // ntaps:
            value = value * inside
        filt[:, :, j * ntaps : (j + 1) * ntaps] = value.reshape(blocks, step_rows, ntaps)


def shift_pair(source, delay, frac, seg):
    mu = jnp.full((1, seg), frac.astype(jnp.float32)) / NFRAC
    first = -mu * (mu - 1.0) * (mu - 2.0) / 6.0
    second = (mu + 1.0) * (mu - 1.0) * (mu - 2.0) / 2.0
    third = -(mu + 1.0) * mu * (mu - 2.0) / 2.0
    fourth = (mu + 1.0) * mu * (mu - 1.0) / 6.0
    base = pltpu.roll(source, 2 * seg - (delay - 1), 1)
    mixed = first * base[:, :seg]
    mixed = mixed + second * pltpu.roll(base, 2 * seg - 1, 1)[:, :seg]
    mixed = mixed + third * pltpu.roll(base, 2 * seg - 2, 1)[:, :seg]
    mixed = mixed + fourth * pltpu.roll(base, 2 * seg - 3, 1)[:, :seg]
    return mixed.astype(jnp.bfloat16)


def solution(mesh):
    nchan, nsrc, ntm = mesh.shape["chan"], mesh.shape["src"], mesh.shape["tm"]
    owners = nchan * nsrc

    def local(
        record, fir_taps, chan_table, steering, pair_block, pair_owner, pair_sub, pair_delay, pair_frac
    ):
        channels, seg = record.shape
        ntab, ntaps = fir_taps.shape
        targets, points, block_rows = steering.shape
        blocks = channels // block_rows
        pairs = pair_block.shape[0]
        cap = 2 * pairs // owners
        step_rows = block_rows // GROUPS
        smem = pl.BlockSpec(memory_space=pltpu.SMEM)
        vmem = pl.BlockSpec(memory_space=pltpu.VMEM)
        dma = pltpu.SemaphoreType.DMA
        operands = (
            pair_block,
            pair_owner.reshape(pairs),
            pair_sub,
            pair_delay,
            pair_frac,
            record.reshape(blocks, block_rows, seg),
            fir_taps,
            chan_table.reshape(blocks, block_rows),
            steering,
        )
        unit = pairs * block_rows // PARTS
        square = unit == 128 and pairs == nsrc * targets and cap * (2 * nsrc) == pairs
        if nchan == 4 and nsrc == 2 and square:
            step_rows = block_rows // PARTS
            half = seg // nsrc
            ranks = owners // 2
            late = PARTS - ranks
            whole = (blocks, step_rows, seg)
            edge = (blocks, step_rows, ntaps)
            bf16, f32, i32 = jnp.bfloat16, jnp.float32, jnp.int32
            held = pltpu.VMEM
            sums = pl.pallas_call(
                functools.partial(line_kernel, (nchan, nsrc, ntm)),
                out_shape=pltpu.VMEM((targets, 2 * block_rows, seg), bf16),
                in_specs=[pl.BlockSpec(memory_space=pltpu.HBM)] * 8,
                out_specs=vmem,
                scratch_shapes=[
                    *[pltpu.SMEM((pairs,), i32)] * 5,
                    held((blocks, block_rows, seg), f32),
                    held((ntab, ntaps), f32),
                    held((blocks, block_rows), i32),
                    held((PARTS, *whole), bf16),
                    held((PARTS, *edge), bf16),
                    held((PARTS, *whole), bf16),
                    held((ranks, *whole), bf16),
                    held((ranks, *edge), bf16),
                    held((ranks, *whole), bf16),
                    held((6 * ntaps, ntab * ntaps), bf16),
                    held((blocks, block_rows, block_rows), i32),
                    held((ranks, blocks * step_rows, 128), i32),
                    held((NFRAC * 4, 128), f32),
                    held((4, blocks, step_rows, 2 * seg), f32),
                    held((pairs, step_rows, seg), bf16),
                    held((ranks, pairs, step_rows, seg), bf16),
                    held((late, nsrc, pairs, step_rows, half), bf16),
                    held((late, ranks, pairs, step_rows, half), bf16),
                    held((PARTS, ranks, cap, step_rows, seg), bf16),
                    held((PARTS, ranks, cap, step_rows, seg), bf16),
                    held((owners, 4, 128), i32),
                    held((owners, 4, 128), i32),
                    pltpu.SMEM((ranks, 4, 128), i32),
                    held((3 * unit, ranks * unit), bf16),
                    held((targets * step_rows, unit), bf16),
                    held((nsrc * unit, ranks * unit), bf16),
                    held((late, nsrc, targets, step_rows, half), f32),
                    held((late, targets, step_rows, half), f32),
                    held((late, ranks, targets, step_rows, half), bf16),
                    held((late, nsrc, targets, step_rows, half), bf16),
                    held((ranks, targets, step_rows, seg), bf16),
                    held((ranks, targets, step_rows, seg), bf16),
                    held((ranks, targets * step_rows, seg), f32),
                    dma((PARTS,)),
                    dma((PARTS,)),
                    dma((PARTS,)),
                    dma((PARTS,)),
                    dma((ranks,)),
                    dma((ranks,)),
                    dma((ranks,)),
                    dma((ranks,)),
                    dma((ranks,)),
                    dma((ranks,)),
                    dma((late, nsrc)),
                    dma((late, ranks)),
                    dma((PARTS, ranks)),
                    dma((PARTS, ranks)),
                    dma((owners,)),
                    dma((owners,)),
                    dma((late,)),
                    dma((late,)),
                    dma((late, ranks)),
                    dma((late, nsrc)),
                    dma((ranks,)),
                    dma((ranks,)),
                    dma,
                    pltpu.SemaphoreType.REGULAR,
                    dma((8,)),
                ],
                compiler_params=pltpu.CompilerParams(collective_id=0, has_side_effects=True),
            )(*operands[:-1])
            return pl.pallas_call(
                steer_kernel,
                out_shape=jax.ShapeDtypeStruct((targets * points, seg), f32),
                in_specs=[vmem] * 2,
                out_specs=pl.BlockSpec(memory_space=pl.ANY),
                scratch_shapes=[held((targets * points, seg), f32), dma((targets,))],
                compiler_params=pltpu.CompilerParams(vmem_limit_bytes=16 << 20),
            )(steering, sums)
        return pl.pallas_call(
            functools.partial(kernel, (nchan, nsrc, ntm)),
            out_shape=jax.ShapeDtypeStruct((targets * points, seg), jnp.float32),
            in_specs=[smem] * 5 + [vmem] * 4,
            out_specs=vmem,
            scratch_shapes=[
                pltpu.VMEM((blocks, block_rows, ntaps), jnp.float32),
                pltpu.VMEM((blocks, block_rows, seg), jnp.float32),
                pltpu.VMEM((2 * ntaps, ntab * ntaps), jnp.bfloat16),
                pltpu.VMEM((2 * ntaps, ntab * ntaps), jnp.bfloat16),
                pltpu.VMEM((blocks, block_rows, block_rows), jnp.int32),
                pltpu.VMEM((blocks, step_rows, 2 * seg), jnp.float32),
                pltpu.VMEM((pairs, step_rows, seg), jnp.bfloat16),
                pltpu.VMEM((owners, cap, block_rows, seg), jnp.bfloat16),
                pltpu.VMEM((owners, cap, block_rows, seg), jnp.bfloat16),
                pltpu.VMEM((owners, 8, 128), jnp.float32),
                pltpu.VMEM((owners, 8, 128), jnp.float32),
                pltpu.VMEM((targets, block_rows, seg), jnp.float32),
                pltpu.SMEM((owners * cap,), jnp.int32),
                dma((GROUPS,)),
                dma((GROUPS,)),
                dma((GROUPS,)),
                dma((GROUPS,)),
                dma((GROUPS, owners)),
                dma((GROUPS, owners)),
                dma((owners,)),
                dma((owners,)),
            ],
            compiler_params=pltpu.CompilerParams(collective_id=0, has_side_effects=True),
        )(*operands)

    in_specs = (
        P(("groups", "chan", "src"), "tm"),
        P(),
        P(("chan", "src")),
        P(("chan", "src"), None, None),
        P(("chan", "src")),
        P(("chan", "src"), None),
        P(("chan", "src")),
        P(("chan", "src")),
        P(("chan", "src")),
    )
    out_specs = P(("groups", "chan", "src"), "tm")
    return jax.shard_map(local, mesh=mesh, in_specs=in_specs, out_specs=out_specs, check_vma=False)
```
